512 devices in a mesh: patch: 2 (over core), lat: 8 (over y), lon: 32 (over z, x).
Axes of the slice: x: 4, y: 8, z: 8, core: 2. Of those that a mesh axis runs over, the one named last changes fastest.
Arguments:
- velocity: float32 [2, 3, 128, 256, 128], P('patch', None, 'lat', 'lon'), may hold values from -6 to 6
- forcing: float32 [2, 3, 128, 256, 128], P('patch', None, 'lat', 'lon'), may hold values from -3 to 3
- viscosity: float32 [2, 128, 256, 128], P('patch', 'lat', 'lon'), may hold values from 1 to 10
- ghost_slots: int32 [2, 768], P('patch'), may hold values from 0 to 767, each once within a row
- corner_rows: int32 [2, 8, 96], P('patch', 'lat', 'lon'), may hold values from 0 to 15
- corner_cols: int32 [2, 8, 96], P('patch', 'lat', 'lon'), may hold values from 0 to 7
- corner_weights: float32 [2, 8, 4, 96], P('patch', 'lat', None, 'lon'), may hold values from 0 to 1, as said below
Outputs:
- new_velocity: float32 [2, 3, 128, 256, 128], P('patch', None, 'lat', 'lon')
- residual: float32 [2, 3, 128, 256, 128], P('patch', None, 'lat', 'lon')
The draws below stay inside these ranges and needn't reach their ends.
Inputs may be any that keep to these rules, and one draw needn't show every extreme that they name: `ghost_slots`: each row names every slot of the other patch exactly once. `corner_rows`: the row below the corner is read too, from the next device or as zero beyond the patch. `corner_cols`: the column after the corner is read too, from the next device or as zero beyond the patch. `corner_weights`: the four weights of a slot are (1 - s)(1 - t), s(1 - t), (1 - s)t and st for some s and t in [0, 1).
All inputs are finite; a program needn't handle non-finite values.
Results may differ from the reference program's by a relative error of at most 0.0001.
Values sent between devices are 32-bit elements; how exact they have to be, the bound alone decides.
No kernel may reach another device: no remote copies, remote signals or barrier semaphores. Data moves between devices by JAX's collectives and lax.ppermute only.
A program may use at most 64 MiB of HBM per device.

```python
import math
import jax
import jax.numpy as jnp

CLAT = 16
CLON = 8
R = 128
SWEEPS = 2
COARSE = 8
NLAT = 128
NLON = 256
G = 768
Q = 3
N_PATCH = 2
N_LAT = 8
N_LON = 32


def draw_forcing(key, part):
    array_shape = (N_PATCH, 3, NLAT, NLON, R)
    return jax.random.uniform(key, array_shape, jnp.float32, -3.0, 3.0)


def draw_corner_weights(key, part):
    array_shape = (N_PATCH, N_LAT, 1, N_LON * Q)
    along_lat = jax.random.uniform(jax.random.fold_in(key, 11), array_shape, jnp.float32)
    along_lon = jax.random.uniform(jax.random.fold_in(key, 12), array_shape, jnp.float32)
    return jnp.concatenate([(1.0 - along_lat) * (1.0 - along_lon), along_lat * (1.0 - along_lon), (1.0 - along_lat) * along_lon, along_lat * along_lon], axis=2)


def with_ends(result, rng, low, largest):
    index_at = [jax.random.randint(jax.random.fold_in(rng, axis), (), 0, length) for axis, length in enumerate(result.shape)]
    main_axis = result.shape.index(max(result.shape))
    next_to = index_at[:main_axis] + [(index_at[main_axis] + 1) % result.shape[main_axis]] + index_at[main_axis + 1:]
    return result.at[tuple(index_at)].set(low).at[tuple(next_to)].set(largest)


def block_levels(own_key, shape, split, smallest, top_value):
    gain = 1.0
    for position, parts in split:
        heights = jax.random.uniform(jax.random.fold_in(jax.random.fold_in(own_key, 6), position), (parts,), jnp.float32, smallest / len(split), top_value / len(split))
        gain = gain * jnp.repeat(jnp.exp(heights), shape[position] // parts).reshape((-1,) + (1,) * (len(shape) - 1 - position))
    return gain


def gaussian(own_key, dims, deviation, most, cuts=(), kind=jnp.bfloat16):
    array = deviation * jax.random.normal(own_key, dims, jnp.float32)
    if cuts:
        array = array * block_levels(own_key, dims, cuts, -0.22, 0.18)
    return jnp.clip(array, -most, most).astype(kind)


def setup_inputs(seed: int = 0) -> dict:
    key_list = jax.random.split(jax.random.key(seed), 8)
    velocity = gaussian(key_list[0], (N_PATCH, 3, NLAT, NLON, R), 1.0, 6.0, ((0, 2), (2, 8), (3, 32)), jnp.float32)
    forcing = draw_forcing(jax.random.fold_in(key_list[7], 71), 0)
    viscosity = jnp.clip(jnp.exp(math.log(10.0) - 2.3025851 * jax.random.uniform(key_list[2], (N_PATCH, NLAT, NLON, R), jnp.float32) ** block_levels(key_list[2], (N_PATCH, NLAT, NLON, R), ((0, 2), (1, 8), (2, 32)), -0.2, 0.2)), 1.0, 10.0)
    ghost_slots = jax.vmap(lambda own: jax.random.permutation(own, G))(jax.random.split(key_list[3], N_PATCH)).reshape((N_PATCH, G)).astype(jnp.int32)
    corner_rows = with_ends(jax.random.randint(key_list[4], (N_PATCH, N_LAT, N_LON * Q), 0, CLAT), jax.random.fold_in(key_list[4], 1), 0, CLAT - 1).astype(jnp.int32)
    corner_cols = with_ends(jax.random.randint(key_list[5], (N_PATCH, N_LAT, N_LON * Q), 0, CLON), jax.random.fold_in(key_list[5], 1), 0, CLON - 1).astype(jnp.int32)
    corner_weights = draw_corner_weights(jax.random.fold_in(key_list[7], 71), 0)
    return {"velocity": velocity, "forcing": forcing, "viscosity": viscosity, "ghost_slots": ghost_slots, "corner_rows": corner_rows, "corner_cols": corner_cols, "corner_weights": corner_weights}


RELAX = 0.8


def face_terms(padded_visc, weight_scale):
    centre = padded_visc[1:-1, 1:-1, 1:-1]
    return (weight_scale * (centre + padded_visc[:-2, 1:-1, 1:-1]),
            weight_scale * (centre + padded_visc[2:, 1:-1, 1:-1]),
            weight_scale * (centre + padded_visc[1:-1, :-2, 1:-1]),
            weight_scale * (centre + padded_visc[1:-1, 2:, 1:-1]),
            weight_scale * (centre + padded_visc[1:-1, 1:-1, :-2]),
            weight_scale * (centre + padded_visc[1:-1, 1:-1, 2:]))


def diagonal_of(face_coefs):
    return face_coefs[0] + face_coefs[1] + face_coefs[2] + face_coefs[3] + face_coefs[4] + face_coefs[5]


def neighbour_sum(padded, face_coefs):
    summed = face_coefs[0] * padded[:, :-2, 1:-1, 1:-1]
    summed = summed + face_coefs[1] * padded[:, 2:, 1:-1, 1:-1]
    summed = summed + face_coefs[2] * padded[:, 1:-1, :-2, 1:-1]
    summed = summed + face_coefs[3] * padded[:, 1:-1, 2:, 1:-1]
    summed = summed + face_coefs[4] * padded[:, 1:-1, 1:-1, :-2]
    summed = summed + face_coefs[5] * padded[:, 1:-1, 1:-1, 2:]
    return summed


def bilinear(weight_rows, corner_list):
    summed = weight_rows[0][None, :, None] * corner_list[0]
    summed = summed + weight_rows[1][None, :, None] * corner_list[1]
    summed = summed + weight_rows[2][None, :, None] * corner_list[2]
    summed = summed + weight_rows[3][None, :, None] * corner_list[3]
    return summed


def interpolants(velocity_patch, rows_given, cols_given, weights_given):
    padded = jnp.pad(velocity_patch, ((0, 0), (0, 1), (0, 1), (0, 0)))
    slot_count = N_LAT * N_LON * Q
    slot_ids = jnp.arange(slot_count, dtype=jnp.int32)
    lat_block = slot_ids // (N_LON * Q)
    lon_block = (slot_ids // Q) % N_LON
    row_index = lat_block * CLAT + rows_given.reshape(-1).astype(jnp.int32)
    col_index = lon_block * CLON + cols_given.reshape(-1).astype(jnp.int32)
    weight_rows = jnp.transpose(weights_given, (1, 0, 2)).reshape(4, slot_count)
    corner_list = (padded[:, row_index, col_index], padded[:, row_index + 1, col_index],
                   padded[:, row_index, col_index + 1], padded[:, row_index + 1, col_index + 1])
    return bilinear(weight_rows, corner_list)


def with_loop(velocity_patch, ghost_loop):
    lat_cells = velocity_patch.shape[1]
    lon_cells = velocity_patch.shape[2]
    padded = jnp.pad(velocity_patch, ((0, 0), (1, 1), (1, 1), (1, 1)))
    padded = padded.at[:, 0, 1:-1, 1:-1].set(ghost_loop[:, :lon_cells])
    padded = padded.at[:, -1, 1:-1, 1:-1].set(ghost_loop[:, lon_cells:2 * lon_cells])
    padded = padded.at[:, 1:-1, 0, 1:-1].set(ghost_loop[:, 2 * lon_cells:2 * lon_cells + lat_cells])
    padded = padded.at[:, 1:-1, -1, 1:-1].set(ghost_loop[:, 2 * lon_cells + lat_cells:])
    return padded


def reference(velocity, forcing, viscosity, ghost_slots, corner_rows, corner_cols, corner_weights):
    lat_cells = CLAT * N_LAT
    lon_cells = CLON * N_LON
    slot_values = [interpolants(velocity[patch_index], corner_rows[patch_index], corner_cols[patch_index],
                                corner_weights[patch_index]) for patch_index in range(N_PATCH)]
    parity = (jnp.arange(lat_cells)[:, None, None] + jnp.arange(lon_cells)[None, :, None]
              + jnp.arange(R)[None, None, :]) % 2
    new_fields = []
    residuals = []
    for patch_index in range(N_PATCH):
        ghost_loop = slot_values[N_PATCH - 1 - patch_index][:, ghost_slots[patch_index], :]
        force_patch = forcing[patch_index]
        viscous_patch = viscosity[patch_index]
        face_coefs = face_terms(jnp.pad(viscous_patch, 1, mode="edge"), 0.5)
        diagonal = diagonal_of(face_coefs)
        current = velocity[patch_index]
        for sweep_index in range(SWEEPS):
            for colour in range(2):
                relaxed = (force_patch + neighbour_sum(with_loop(current, ghost_loop), face_coefs)) / diagonal
                current = jnp.where((parity == colour)[None], relaxed, current)
        residual_field = force_patch - (diagonal * current - neighbour_sum(with_loop(current, ghost_loop), face_coefs))
        coarse_rhs = residual_field.reshape(3, lat_cells // 2, 2, lon_cells // 2, 2, R // 2, 2).mean(axis=(2, 4, 6))
        coarse_visc = jnp.pad(viscous_patch, 2, mode="edge").reshape(
            lat_cells // 2 + 2, 2, lon_cells // 2 + 2, 2, R // 2 + 2, 2).mean(axis=(1, 3, 5))
        coarse_coefs = face_terms(coarse_visc, 0.125)
        coarse_diag = diagonal_of(coarse_coefs)
        coarse_error = RELAX * coarse_rhs / coarse_diag
        for turn_index in range(COARSE - 1):
            padded = jnp.pad(coarse_error, ((0, 0), (1, 1), (1, 1), (1, 1)))
            coarse_error = coarse_error + RELAX * (coarse_rhs - (coarse_diag * coarse_error
                                                                - neighbour_sum(padded, coarse_coefs))) / coarse_diag
        correction = jnp.repeat(jnp.repeat(jnp.repeat(coarse_error, 2, axis=1), 2, axis=2), 2, axis=3)
        new_fields.append(current + correction)
        residuals.append(residual_field)
    return jnp.stack(new_fields), jnp.stack(residuals)
```

```python
import jax
import jax.numpy as jnp
from jax import lax
from jax.experimental import pallas as pl
from jax.experimental.pallas import tpu as pltpu
from jax.sharding import PartitionSpec as P

AXES = ("patch", "lat", "lon")
RELAX = 0.8
COARSE = 8
PAD = 6
VMEM = pl.BlockSpec(memory_space=pltpu.VMEM)
SMEM = pl.BlockSpec(memory_space=pltpu.SMEM)


def shifted(value, by_lat, by_lon):
    patches, lats, lons = (lax.axis_size(axis) for axis in AXES)
    pairs = []
    for p in range(patches):
        for a in range(lats):
            for b in range(lons):
                a2, b2 = a + by_lat, b + by_lon
                if 0 <= a2 < lats and 0 <= b2 < lons:
                    pairs.append(((p * lats + a) * lons + b, (p * lats + a2) * lons + b2))
    return lax.ppermute(value, AXES, pairs)


def lanes_of(shape):
    return lax.broadcasted_iota(jnp.int32, shape, len(shape) - 1)


def rows_of(shape):
    return lax.broadcasted_iota(jnp.int32, shape, len(shape) - 2)


def roll(value, by, axis):
    return pltpu.roll(value, by % value.shape[axis], axis)


def lane_partner(value, odd_lane):
    return jnp.where(odd_lane, roll(value, 1, 1), roll(value, -1, 1))


def row_partner(value, odd_row):
    return jnp.where(odd_row, roll(value, 1, 0), roll(value, -1, 0))


def interp_kernel(rows_ref, cols_ref, weights_ref, v_ref, right_ref, below_ref, out_ref, pad_ref):
    rows = v_ref.shape[1]
    pad_ref[:, :rows, 0:8] = v_ref[...]
    pad_ref[:, :rows, 8:16] = right_ref[...]
    pad_ref[:, rows] = below_ref[:, 0, 8:24]
    for slot in range(3):
        row, col = rows_ref[slot], cols_ref[slot]
        for comp in range(3):
            total = weights_ref[0, slot] * pad_ref[comp, row, pl.ds(col, 1), :]
            total = total + weights_ref[1, slot] * pad_ref[comp, row + 1, pl.ds(col, 1), :]
            total = total + weights_ref[2, slot] * pad_ref[comp, row, pl.ds(col + 1, 1), :]
            total = total + weights_ref[3, slot] * pad_ref[comp, row + 1, pl.ds(col + 1, 1), :]
            out_ref[pl.ds(slot * 3 + comp, 1), :] = total


def smooth_kernel(
    place_ref, ghost_ref, v_ref, f_ref, mu_ref, left_ref, right_ref, above_ref, below_ref, slot_ref,
    res_ref, smooth_ref, message_ref,
    V, F, MU, CN, CW, CE, CD, CU, DG, INV,
):
    lat, lon = place_ref[0], place_ref[1]
    last_lat, last_lon = place_ref[2], place_ref[3]
    wide = (24, 128)
    lane, row = lanes_of(wide), rows_of(wide)
    odd_lane, odd_row = (lane & 1) == 1, (row & 1) == 1
    own = slice(PAD, PAD + 16)

    for comp in range(3):
        V[comp, own, 0:8] = left_ref[comp]
        V[comp, own, 8:16] = v_ref[comp]
        V[comp, own, 16:24] = right_ref[comp]
        V[comp, 1:6] = above_ref[comp]
        V[comp, 22:27] = below_ref[comp]
        F[comp, own, 0:8] = left_ref[3 + comp]
        F[comp, own, 8:16] = f_ref[comp]
        F[comp, own, 16:24] = right_ref[3 + comp]
        F[comp, 1:6] = above_ref[3 + comp]
        F[comp, 22:27] = below_ref[3 + comp]
    MU[own, 0:8] = left_ref[6]
    MU[own, 8:16] = mu_ref[...]
    MU[own, 16:24] = right_ref[6]
    MU[1:6] = above_ref[6]
    MU[22:27] = below_ref[6]

    @pl.when(lat == 0)
    def _():
        MU[4] = MU[6]
        MU[5] = MU[6]
        for col in range(-4, 12):
            base = ghost_ref[jnp.clip(lon * 8 + col, 0, (last_lon + 1) * 8 - 1)]
            for comp in range(3):
                V[comp, 5, 8 + col : 9 + col] = slot_ref[base + comp]

    @pl.when(lat == last_lat)
    def _():
        MU[22] = MU[21]
        MU[23] = MU[21]
        for col in range(-4, 12):
            base = ghost_ref[(last_lon + 1) * 8 + jnp.clip(lon * 8 + col, 0, (last_lon + 1) * 8 - 1)]
            for comp in range(3):
                V[comp, 22, 8 + col : 9 + col] = slot_ref[base + comp]

    side_start = 2 * (last_lon + 1) * 8
    side_rows = (last_lat + 1) * 16

    @pl.when(lon == 0)
    def _():
        for i in range(1, 27):
            MU[i, 0:8] = jnp.broadcast_to(MU[i, 8:9], (8, 128))
        for r in range(-4, 20):
            base = ghost_ref[side_start + jnp.clip(lat * 16 + r, 0, side_rows - 1)]
            for comp in range(3):
                V[comp, r + PAD, 7:8] = slot_ref[base + comp]

    @pl.when(lon == last_lon)
    def _():
        for i in range(1, 27):
            MU[i, 16:24] = jnp.broadcast_to(MU[i, 15:16], (8, 128))
        for r in range(-4, 20):
            base = ghost_ref[side_start + side_rows + jnp.clip(lat * 16 + r, 0, side_rows - 1)]
            for comp in range(3):
                V[comp, r + PAD, 16:17] = slot_ref[base + comp]

    def coefficients(i, carry):
        mid = MU[i]
        north = 0.5 * (mid + MU[i - 1])
        south = 0.5 * (mid + MU[i + 1])
        west = 0.5 * (mid + roll(mid, 1, 0))
        east = 0.5 * (mid + roll(mid, -1, 0))
        down = 0.5 * (mid + jnp.where(lane == 0, mid, roll(mid, 1, 1)))
        up = 0.5 * (mid + jnp.where(lane == 127, mid, roll(mid, -1, 1)))
        total = north + south + west + east + down + up
        CN[i] = north
        CN[i + 1] = south
        CW[i] = west
        CE[i] = east
        CD[i] = jnp.where(lane == 0, 0.0, down)
        CU[i] = jnp.where(lane == 127, 0.0, up)
        DG[i] = total
        INV[i] = 1.0 / total
        return carry

    lax.fori_loop(2, 26, coefficients, 0)

    inside = ((row >= 8) | (lon > 0)) & ((row < 16) | (lon < last_lon))
    parity = (row + lane) & 1
    masks = ((parity == 0) & inside, (parity == 1) & inside)

    def weighted(comp, i, here):
        total = F[comp, i] + CN[i] * V[comp, i - 1]
        total = total + CN[i + 1] * V[comp, i + 1]
        total = total + CW[i] * roll(here, 1, 0)
        total = total + CE[i] * roll(here, -1, 0)
        total = total + CD[i] * roll(here, 1, 1)
        return total + CU[i] * roll(here, -1, 1)

    def relax(colour, pairs):
        def step(pair, carry):
            for k in range(2):
                i = 2 * pair + PAD + k
                for comp in range(3):
                    here = V[comp, i]
                    fresh = weighted(comp, i, here) * INV[i]
                    V[comp, i] = jnp.where(masks[(colour + k) % 2], fresh, here)
            return carry

        first = jnp.where(lat == 0, 0, -pairs)
        last = jnp.where(lat == last_lat, 8, 8 + pairs)
        lax.fori_loop(first, last, step, 0)

    relax(0, 2)
    relax(1, 2)
    relax(0, 1)
    relax(1, 1)

    def coarse_visc(i):
        both = MU[i] + MU[i + 1]
        flat = 0.25 * (both + row_partner(both, odd_row))
        return flat, 0.5 * (flat + lane_partner(flat, odd_lane))

    tile = (8, 128)
    lane8, row8 = lanes_of(tile), rows_of(tile)
    odd_lane8, odd_row8 = (lane8 & 1) == 1, (row8 & 1) == 1

    def packed(parts):
        low = jnp.where(odd_lane8, parts[1], parts[0])
        high = jnp.where(odd_lane8, parts[3], parts[2])
        return jnp.where(odd_row8, high, low)

    layers = [coarse_visc(PAD + 2 * k) for k in (-1, 0)]
    inverse = []
    for k in range(8):
        layers.append(coarse_visc(PAD + 2 * k + 2))
        before, (flat, visc), after = layers[k][1], layers[k + 1], layers[k + 2][1]
        edge_down = jnp.where(lane == 0, flat, roll(flat, 1, 1))
        edge_up = jnp.where(lane == 127, flat, roll(flat, -1, 1))
        total = 6.0 * visc + before + after + roll(visc, 2, 0) + roll(visc, -2, 0)
        total = total + jnp.where(lane < 2, edge_down, roll(visc, 2, 1))
        total = total + jnp.where(lane >= 126, edge_up, roll(visc, -2, 1))
        over = RELAX / (0.125 * total[8:16])
        inverse.append(over)
        parts = []
        for comp in range(3):
            rhs = jnp.zeros(tile, jnp.float32)
            for r in (2 * k, 2 * k + 1):
                i = r + PAD
                here = V[comp, i]
                left = (weighted(comp, i, here) - DG[i] * here)[8:16]
                res_ref[comp, r] = left
                rhs = rhs + left
            rhs = rhs + lane_partner(rhs, odd_lane8)
            rhs = rhs + row_partner(rhs, odd_row8)
            parts.append(0.125 * rhs * over)
        message_ref[k] = packed(parts + [visc[8:16]])
        if k % 4 == 3:
            message_ref[8 + k // 4] = packed(inverse[k - 3 : k + 1])
    for comp in range(3):
        smooth_ref[comp] = V[comp, own, 8:16]


def coarse_kernel(
    mid_ref, above_ref, below_ref, smooth_ref, out_ref, Q, CV, DV, E, AN, AS, AW, AE, AD, AU
):
    wide = (40, 128)
    lane, row = lanes_of(wide), rows_of(wide)
    odd_lane, odd_row = (lane & 1) == 1, (row & 1) == 1

    def spread(value, part, odd_l, odd_r):
        keep = odd_l if part % 2 else ~odd_l
        value = jnp.where(keep, value, roll(value, -1 if part % 2 else 1, 1))
        keep = odd_r if part // 2 else ~odd_r
        return jnp.where(keep, value, roll(value, -1 if part // 2 else 1, 0))

    for n in range(22):
        ref, t = (above_ref, n + 1) if n < 7 else (mid_ref, n - 7) if n < 15 else (below_ref, n - 15)
        value = ref[t]
        Q[n] = value
        CV[n] = spread(value, 3, odd_lane, odd_row)
        if 1 <= n <= 20:
            DV[n] = 0.125 * spread(ref[8 + t // 4], t % 4, odd_lane, odd_row)

    def coefficients(n, carry):
        visc, over = CV[n], DV[n]
        AN[n] = over * (visc + CV[n - 1])
        AS[n] = over * (visc + CV[n + 1])
        AW[n] = over * (visc + roll(visc, 2, 0))
        AE[n] = over * (visc + roll(visc, -2, 0))
        AD[n] = jnp.where(lane < 2, 0.0, over * (visc + roll(visc, 2, 1)))
        AU[n] = jnp.where(lane >= 126, 0.0, over * (visc + roll(visc, -2, 1)))
        return carry

    lax.fori_loop(1, 21, coefficients, 0)

    for turn in range(1, COARSE):
        old = Q if turn == 1 else E.at[turn % 2]
        new = E.at[(turn + 1) % 2]

        def step(n, carry, old=old, new=new):
            here = old[n]
            total = Q[n] + (1.0 - RELAX) * here
            total = total + AN[n] * old[n - 1]
            total = total + AS[n] * old[n + 1]
            total = total + AW[n] * roll(here, 2, 0)
            total = total + AE[n] * roll(here, -2, 0)
            total = total + AD[n] * roll(here, 2, 1)
            new[n] = total + AU[n] * roll(here, -2, 1)
            return carry

        lax.fori_loop(turn, 22 - turn, step, 0)

    final = E.at[COARSE % 2]
    tile = (8, 128)
    lane8, row8 = lanes_of(tile), rows_of(tile)
    odd_lane8, odd_row8 = (lane8 & 1) == 1, (row8 & 1) == 1
    for k in range(8):
        value = final[7 + k, 16:24]
        for comp in range(3):
            error = spread(value, comp, odd_lane8, odd_row8)
            for r in (2 * k, 2 * k + 1):
                out_ref[comp, r] = smooth_ref[comp, r] + error


def whole(shape):
    return pl.BlockSpec(shape, lambda step: (0,) * len(shape))


def per_device(velocity, forcing, viscosity, ghost_slots, corner_rows, corner_cols, corner_weights):
    v, f, mu = velocity[0], forcing[0], viscosity[0]
    lats, lons = lax.axis_size("lat"), lax.axis_size("lon")
    params = pltpu.CompilerParams(vmem_limit_bytes=32 * 2**20)
    f32 = jnp.float32
    place = jnp.stack(
        [lax.axis_index("lat"), lax.axis_index("lon"), jnp.int32(lats - 1), jnp.int32(lons - 1)]
    ).astype(jnp.int32)
    slots = ghost_slots[0]
    ghost_base = ((slots // 3) % lons) * (9 * lats) + ((slots // (3 * lons)) * 3 + slots % 3) * 3

    own = jnp.concatenate([v, f, mu[None]], axis=0)
    left = shifted(own, 0, 1)
    right = shifted(own, 0, -1)
    ext_top = jnp.concatenate([left[:, :5], own[:, :5], right[:, :5]], axis=2)
    ext_low = jnp.concatenate([left[:, 11:], own[:, 11:], right[:, 11:]], axis=2)
    below = shifted(ext_top, -1, 0)
    above = shifted(ext_low, 1, 0)

    values = pl.pallas_call(
        interp_kernel,
        grid=(1,),
        out_shape=jax.ShapeDtypeStruct((9, 128), f32),
        in_specs=[SMEM, SMEM, SMEM, VMEM, whole((3, 16, 8, 128)), whole((3, 1, 24, 128))],
        out_specs=VMEM,
        scratch_shapes=[pltpu.VMEM((3, 17, 16, 128), f32)],
        compiler_params=params,
        name="interp",
    )(corner_rows[0, 0], corner_cols[0, 0], corner_weights[0, 0], v, right, below)

    spread = jnp.broadcast_to(values[None], (2 * lats, 9, 128))
    column = lax.all_to_all(spread, ("patch", "lat"), 0, 0, tiled=True)
    column = column.reshape(2, lats * 9, 128)
    column = jnp.where(lax.axis_index("patch") == 0, column[1], column[0])
    everything = lax.all_to_all(
        jnp.broadcast_to(column[None], (lons, lats * 9, 128)), "lon", 0, 0, tiled=True
    )
    everything = everything.reshape(lons * lats * 9, 1, 128)

    block = jax.ShapeDtypeStruct((3, 16, 8, 128), f32)
    field = pltpu.VMEM((3, 28, 24, 128), f32)
    plane = pltpu.VMEM((28, 24, 128), f32)
    residual, smoothed, message = pl.pallas_call(
        smooth_kernel,
        out_shape=(block, block, jax.ShapeDtypeStruct((10, 8, 128), f32)),
        in_specs=[SMEM, SMEM] + [VMEM] * 8,
        out_specs=(VMEM, VMEM, VMEM),
        scratch_shapes=[field, field] + [plane] * 8,
        compiler_params=params,
        name="smooth",
    )(place, ghost_base, v, f, mu, left, right, above, below, everything)

    tiles = [
        shifted(message, 0, 2),
        shifted(message, 0, 1),
        message,
        shifted(message, 0, -1),
        shifted(message, 0, -2),
    ]
    band = jnp.concatenate(tiles, axis=1)
    band_below = shifted(band, -1, 0)
    band_above = shifted(band, 1, 0)
    coarse = pltpu.VMEM((22, 40, 128), f32)
    new = pl.pallas_call(
        coarse_kernel,
        out_shape=block,
        in_specs=[VMEM] * 4,
        out_specs=VMEM,
        scratch_shapes=[coarse, coarse, coarse, pltpu.VMEM((2, 22, 40, 128), f32)] + [coarse] * 6,
        compiler_params=params,
        name="coarse",
    )(band, band_above, band_below, smoothed)
    return new[None], residual[None]


def solution(mesh):
    placed = (
        P("patch", None, "lat", "lon", None),
        P("patch", None, "lat", "lon", None),
        P("patch", "lat", "lon", None),
        P("patch", None),
        P("patch", "lat", "lon"),
        P("patch", "lat", "lon"),
        P("patch", "lat", None, "lon"),
    )
    return jax.shard_map(
        per_device,
        mesh=mesh,
        in_specs=placed,
        out_specs=(P("patch", None, "lat", "lon", None), P("patch", None, "lat", "lon", None)),
        check_vma=False,
    )
```

```python
import jax
import jax.numpy as jnp
from jax import lax
from jax.experimental import pallas as pl
from jax.experimental.pallas import tpu as pltpu
from jax.sharding import PartitionSpec as P

AXES = ("patch", "lat", "lon")
RELAX = 0.8
COARSE = 8
PAD = 6
CELLS = 32
VMEM = pl.BlockSpec(memory_space=pltpu.VMEM)
SMEM = pl.BlockSpec(memory_space=pltpu.SMEM)


def shifted(value, by_lat, by_lon):
    patches, lats, lons = (lax.axis_size(axis) for axis in AXES)
    pairs = []
    for p in range(patches):
        for a in range(lats):
            for b in range(lons):
                a2, b2 = a + by_lat, b + by_lon
                if 0 <= a2 < lats and 0 <= b2 < lons:
                    pairs.append(((p * lats + a) * lons + b, (p * lats + a2) * lons + b2))
    return lax.ppermute(value, AXES, pairs)


def lanes_of(shape):
    return lax.broadcasted_iota(jnp.int32, shape, len(shape) - 1)


def rows_of(shape):
    return lax.broadcasted_iota(jnp.int32, shape, len(shape) - 2)


def roll(value, by, axis):
    return pltpu.roll(value, by % value.shape[axis], axis)


def lane_partner(value, odd_lane):
    return jnp.where(odd_lane, roll(value, 1, 1), roll(value, -1, 1))


def row_partner(value, odd_row):
    return jnp.where(odd_row, roll(value, 1, 0), roll(value, -1, 0))


def interp_kernel(
    rows_ref, cols_ref, weights_ref, v_ref, right_ref, below_ref, corner_ref, out_ref, pad_ref
):
    rows = v_ref.shape[1]
    for comp in range(3):
        pad_ref[comp, :rows, 0:8] = v_ref[comp]
        pad_ref[comp, rows, 0:8] = below_ref[comp]
        for row in range(rows):
            pad_ref[comp, row, 8:9] = right_ref[comp, row : row + 1]
        pad_ref[comp, rows, 8:9] = corner_ref[comp : comp + 1]
    for slot in range(3):
        row, col = rows_ref[slot], cols_ref[slot]
        for comp in range(3):
            total = weights_ref[0, slot] * pad_ref[comp, row, pl.ds(col, 1), :]
            total = total + weights_ref[1, slot] * pad_ref[comp, row + 1, pl.ds(col, 1), :]
            total = total + weights_ref[2, slot] * pad_ref[comp, row, pl.ds(col + 1, 1), :]
            total = total + weights_ref[3, slot] * pad_ref[comp, row + 1, pl.ds(col + 1, 1), :]
            out_ref[slot * 3 + comp : slot * 3 + comp + 1] = total


def pick_kernel(place_ref, cells_ref, source_ref, row_ref, out_ref):
    lon, last_lat, last_lon = place_ref[1], place_ref[2], place_ref[3]
    edge = (lon == 0) | (lon == last_lon)

    def copy(dest, position):
        base = source_ref[cells_ref[dest * CELLS + position]]
        for comp in range(3):
            out_ref[dest * 3 * CELLS + position * 3 + comp] = row_ref[base + comp]

    @pl.when(edge)
    def _():
        def step(dest, carry):
            for position in range(CELLS):
                copy(dest, position)
            return carry

        lax.fori_loop(0, last_lat + 1, step, 0)

    @pl.when(~edge)
    def _():
        for position in range(16):
            copy(0, position)
            copy(last_lat, position)


def prepare_kernel(
    place_ref, f_ref, mu_ref, left_ref, right_ref, above_ref, below_ref,
    F, CN, CS, CW, CE, CD, CU, DG, over_ref, visc_ref, MU,
):
    lat, lon = place_ref[0], place_ref[1]
    last_lat, last_lon = place_ref[2], place_ref[3]
    wide = (24, 128)
    lane, row = lanes_of(wide), rows_of(wide)
    odd_lane, odd_row = (lane & 1) == 1, (row & 1) == 1
    own = slice(PAD, PAD + 16)
    MU[own, 0:8] = left_ref[6]
    MU[own, 8:16] = mu_ref[...]
    MU[own, 16:24] = right_ref[6]
    MU[1:6] = above_ref[6]
    MU[22:27] = below_ref[6]

    @pl.when(lat == 0)
    def _():
        MU[4] = MU[6]
        MU[5] = MU[6]

    @pl.when(lat == last_lat)
    def _():
        MU[22] = MU[21]
        MU[23] = MU[21]

    @pl.when(lon == 0)
    def _():
        for i in range(1, 27):
            MU[i, 0:8] = jnp.broadcast_to(MU[i, 8:9], (8, 128))

    @pl.when(lon == last_lon)
    def _():
        for i in range(1, 27):
            MU[i, 16:24] = jnp.broadcast_to(MU[i, 15:16], (8, 128))

    for i in range(2, 26):
        mid = MU[i]
        north = 0.5 * (mid + MU[i - 1])
        south = 0.5 * (mid + MU[i + 1])
        west = 0.5 * (mid + roll(mid, 1, 0))
        east = 0.5 * (mid + roll(mid, -1, 0))
        down = 0.5 * (mid + jnp.where(lane == 0, mid, roll(mid, 1, 1)))
        up = 0.5 * (mid + jnp.where(lane == 127, mid, roll(mid, -1, 1)))
        total = north + south + west + east + down + up
        inverse = 1.0 / total
        CN[i] = north * inverse
        CS[i] = south * inverse
        CW[i] = west * inverse
        CE[i] = east * inverse
        CD[i] = jnp.where(lane == 0, 0.0, down * inverse)
        CU[i] = jnp.where(lane == 127, 0.0, up * inverse)
        if PAD <= i < PAD + 16:
            DG[i - PAD] = total[8:16]
        for comp in range(3):
            if i < PAD:
                force = above_ref[3 + comp, i - 1]
                F[comp, i] = force * inverse
            elif i >= PAD + 16:
                force = below_ref[3 + comp, i - PAD - 16]
                F[comp, i] = force * inverse
            else:
                F[comp, i, 0:8] = left_ref[3 + comp, i - PAD] * inverse[0:8]
                F[comp, i, 8:16] = f_ref[comp, i - PAD] * inverse[8:16]
                F[comp, i, 16:24] = right_ref[3 + comp, i - PAD] * inverse[16:24]

    def coarse_visc(i):
        both = MU[i] + MU[i + 1]
        flat = 0.25 * (both + row_partner(both, odd_row))
        return flat, 0.5 * (flat + lane_partner(flat, odd_lane))

    layers = [coarse_visc(PAD + 2 * k) for k in (-1, 0)]
    for k in range(8):
        layers.append(coarse_visc(PAD + 2 * k + 2))
        before, (flat, visc), after = layers[k][1], layers[k + 1], layers[k + 2][1]
        edge_down = jnp.where(lane == 0, flat, roll(flat, 1, 1))
        edge_up = jnp.where(lane == 127, flat, roll(flat, -1, 1))
        total = 6.0 * visc + before + after + roll(visc, 2, 0) + roll(visc, -2, 0)
        total = total + jnp.where(lane < 2, edge_down, roll(visc, 2, 1))
        total = total + jnp.where(lane >= 126, edge_up, roll(visc, -2, 1))
        over_ref[k] = RELAX / (0.125 * total[8:16])
        visc_ref[k] = visc[8:16]


def smooth_kernel(
    place_ref, ghost_ref, v_ref, left_ref, right_ref, above_ref, below_ref, slot_ref,
    F, CN, CS, CW, CE, CD, CU, DG, over_ref, visc_ref,
    res_ref, smooth_ref, message_ref, A, B,
):
    lat, lon = place_ref[0], place_ref[1]
    last_lat, last_lon = place_ref[2], place_ref[3]
    wide = (24, 128)
    lane, row = lanes_of(wide), rows_of(wide)
    own = slice(PAD, PAD + 16)

    for comp in range(3):
        A[comp, own, 0:8] = left_ref[comp]
        A[comp, own, 8:16] = v_ref[comp]
        A[comp, own, 16:24] = right_ref[comp]
        A[comp, 1:6] = above_ref[comp]
        A[comp, 22:27] = below_ref[comp]

    edge = (lon == 0) | (lon == last_lon)
    all_cols, all_rows = (last_lon + 1) * 8, (last_lat + 1) * 16

    def fill_row(i, start):
        for col in range(-4, 12):
            along = jnp.where(lon == 0, col, col + 4)
            packed_at = jnp.where((lat == 0) & (along < 4), along, along + 20)
            position = jnp.clip(jnp.where(edge, packed_at, col + 4), 0, CELLS - 1)
            cell = start + jnp.clip(lon * 8 + col, 0, all_cols - 1)
            base = ghost_ref[cell] + 3 * position
            for comp in range(3):
                A[comp, i, 8 + col : 9 + col] = slot_ref[base + comp]

    def fill_side(col, start):
        for r in range(-4, 20):
            base = ghost_ref[start + jnp.clip(lat * 16 + r, 0, all_rows - 1)] + 3 * (r + 4)
            for comp in range(3):
                A[comp, r + PAD, 8 + col : 9 + col] = slot_ref[base + comp]

    pl.when(lat == 0)(lambda: fill_row(5, 0))
    pl.when(lat == last_lat)(lambda: fill_row(22, all_cols))
    pl.when(lon == 0)(lambda: fill_side(-1, 2 * all_cols))
    pl.when(lon == last_lon)(lambda: fill_side(8, 2 * all_cols + all_rows))

    inside = ((row >= 8) | (lon > 0)) & ((row < 16) | (lon < last_lon))
    parity = jnp.where(inside, (row + lane) & 1, 2)

    def weighted(source, comp, i, here):
        total = F[comp, i] + CN[i] * source[comp, i - 1]
        total = total + CS[i] * source[comp, i + 1]
        total = total + CW[i] * roll(here, 1, 0)
        total = total + CE[i] * roll(here, -1, 0)
        total = total + CD[i] * roll(here, 1, 1)
        return total + CU[i] * roll(here, -1, 1)

    wanted = {}
    for colour in range(2):
        wanted[colour, "mid"] = jnp.int32(colour)
        wanted[colour, "top"] = jnp.where(lat == 0, 3, colour)
        wanted[colour, "low"] = jnp.where(lat == last_lat, 3, colour)

    def relax(colour, reach, source, target):
        for r in range(-reach, 16 + reach):
            i = r + PAD
            zone = "top" if r < 0 else "low" if r > 15 else "mid"
            mask = parity == wanted[(colour + r) % 2, zone]
            for comp in range(3):
                here = source[comp, i]
                target[comp, i] = jnp.where(mask, weighted(source, comp, i, here), here)

    relax(0, 4, A, B)
    relax(1, 3, B, A)
    relax(0, 2, A, B)
    relax(1, 1, B, A)

    tile = (8, 128)
    lane8, row8 = lanes_of(tile), rows_of(tile)
    odd_lane8, odd_row8 = (lane8 & 1) == 1, (row8 & 1) == 1

    def packed(parts):
        low = jnp.where(odd_lane8, parts[1], parts[0])
        high = jnp.where(odd_lane8, parts[3], parts[2])
        return jnp.where(odd_row8, high, low)

    for k in range(8):
        parts = []
        for comp in range(3):
            rhs = jnp.zeros(tile, jnp.float32)
            for r in (2 * k, 2 * k + 1):
                here = A[comp, r + PAD]
                smooth_ref[comp, r] = here[8:16]
                left = DG[r] * (weighted(A, comp, r + PAD, here) - here)[8:16]
                res_ref[comp, r] = left
                rhs = rhs + left
            rhs = rhs + lane_partner(rhs, odd_lane8)
            rhs = rhs + row_partner(rhs, odd_row8)
            parts.append(0.125 * rhs * over_ref[k])
        message_ref[k] = packed(parts + [visc_ref[k]])
        if k % 4 == 3:
            message_ref[8 + k // 4] = packed([over_ref[j] for j in range(k - 3, k + 1)])


def coarse_kernel(
    mid_ref, above_ref, below_ref, smooth_ref, out_ref, Q, CV, DV, E, AN, AS, AW, AE, AD, AU
):
    wide = (40, 128)
    lane, row = lanes_of(wide), rows_of(wide)
    odd_lane, odd_row = (lane & 1) == 1, (row & 1) == 1

    def spread(value, part, odd_l, odd_r):
        keep = odd_l if part % 2 else ~odd_l
        value = jnp.where(keep, value, roll(value, -1 if part % 2 else 1, 1))
        keep = odd_r if part // 2 else ~odd_r
        return jnp.where(keep, value, roll(value, -1 if part // 2 else 1, 0))

    for n in range(22):
        ref, t = (above_ref, n + 1) if n < 7 else (mid_ref, n - 7) if n < 15 else (below_ref, n - 15)
        value = ref[t]
        Q[n] = value
        CV[n] = spread(value, 3, odd_lane, odd_row)
        if 1 <= n <= 20:
            DV[n] = 0.125 * spread(ref[8 + t // 4], t % 4, odd_lane, odd_row)

    def far(n):
        return max(0, 7 - n, n - 14)

    def span(reach):
        return slice(0, 40) if reach > 3 else slice(8, 32)

    for n in range(1, 21):
        cols = span(6 - far(n))
        edge = lane[cols]
        visc, over = CV[n, cols], DV[n, cols]
        AN[n, cols] = over * (visc + CV[n - 1, cols])
        AS[n, cols] = over * (visc + CV[n + 1, cols])
        AW[n, cols] = over * (visc + roll(visc, 2, 0))
        AE[n, cols] = over * (visc + roll(visc, -2, 0))
        AD[n, cols] = jnp.where(edge < 2, 0.0, over * (visc + roll(visc, 2, 1)))
        AU[n, cols] = jnp.where(edge >= 126, 0.0, over * (visc + roll(visc, -2, 1)))

    for turn in range(1, COARSE):
        old = Q if turn == 1 else E.at[turn % 2]
        new = E.at[(turn + 1) % 2]
        for n in range(turn, 22 - turn):
            cols = span(7 - turn - far(n))
            here = old[n, cols]
            total = Q[n, cols] + (1.0 - RELAX) * here
            total = total + AN[n, cols] * old[n - 1, cols]
            total = total + AS[n, cols] * old[n + 1, cols]
            total = total + AW[n, cols] * roll(here, 2, 0)
            total = total + AE[n, cols] * roll(here, -2, 0)
            total = total + AD[n, cols] * roll(here, 2, 1)
            new[n, cols] = total + AU[n, cols] * roll(here, -2, 1)

    final = E.at[COARSE % 2]
    tile = (8, 128)
    lane8, row8 = lanes_of(tile), rows_of(tile)
    odd_lane8, odd_row8 = (lane8 & 1) == 1, (row8 & 1) == 1
    for k in range(8):
        value = final[7 + k, 16:24]
        for comp in range(3):
            error = spread(value, comp, odd_lane8, odd_row8)
            for r in (2 * k, 2 * k + 1):
                out_ref[comp, r] = smooth_ref[comp, r] + error


def wanted_cells(lats, lons, lon):
    dest = jnp.arange(lats, dtype=jnp.int32)[:, None]
    position = jnp.arange(CELLS, dtype=jnp.int32)[None, :]
    rows, cols = lats * 16, lons * 8
    edge = (lon == 0) | (lon == lons - 1)
    side_row = dest * 16 + position - 4
    on_side = edge & (position < 24) & (side_row >= 0) & (side_row < rows)
    side = 2 * cols + jnp.where(lon == 0, 0, rows) + jnp.clip(side_row, 0, rows - 1)
    along = jnp.where((dest == 0) & (position < 4), position, position - 20)
    corner_col = jnp.where(lon == 0, along, lon * 8 + along - 4)
    col = jnp.where(edge, corner_col, lon * 8 + position - 4)
    row_cell = jnp.where(dest == 0, 0, cols) + jnp.clip(col, 0, cols - 1)
    return jnp.where(on_side, side, row_cell)


def per_device(velocity, forcing, viscosity, ghost_slots, corner_rows, corner_cols, corner_weights):
    v, f, mu = velocity[0], forcing[0], viscosity[0]
    lats, lons = lax.axis_size("lat"), lax.axis_size("lon")
    params = pltpu.CompilerParams(vmem_limit_bytes=32 * 2**20)
    f32 = jnp.float32
    place = jnp.stack(
        [lax.axis_index("lat"), lax.axis_index("lon"), jnp.int32(lats - 1), jnp.int32(lons - 1)]
    ).astype(jnp.int32)
    slots = ghost_slots[0]
    source_rows = ((slots // 3) % lons) * 9 + (slots % 3) * 3
    ghost_rows = (slots // (3 * lons)) * (3 * CELLS)
    cells = wanted_cells(lats, lons, lax.axis_index("lon")).reshape(-1)

    corner_right = shifted(v[:, :, 0], 0, -1)
    corner_below = shifted(v[:, 0], -1, 0)
    corner_both = shifted(v[:, 0, 0], -1, -1)
    values = pl.pallas_call(
        interp_kernel,
        out_shape=jax.ShapeDtypeStruct((9, 128), f32),
        in_specs=[SMEM] * 3 + [VMEM] * 4,
        out_specs=VMEM,
        scratch_shapes=[pltpu.VMEM((3, 17, 16, 128), f32)],
        compiler_params=params,
        name="interp",
    )(
        corner_rows[0, 0], corner_cols[0, 0], corner_weights[0, 0],
        v, corner_right, corner_below, corner_both,
    )
    values = lax.ppermute(values, "patch", [(0, 1), (1, 0)])

    own = jnp.concatenate([v, f, mu[None]], axis=0)
    left = shifted(own, 0, 1)
    right = shifted(own, 0, -1)
    ext_top = jnp.concatenate([left[:, :5], own[:, :5], right[:, :5]], axis=2)
    ext_low = jnp.concatenate([left[:, 11:], own[:, 11:], right[:, 11:]], axis=2)
    below = shifted(ext_top, -1, 0)
    above = shifted(ext_low, 1, 0)

    around = lax.all_to_all(
        jnp.broadcast_to(values[None], (lons, 9, 128)), "lon", 0, 0, tiled=True
    )
    chosen = pl.pallas_call(
        pick_kernel,
        out_shape=jax.ShapeDtypeStruct((lats * 3 * CELLS, 1, 128), f32),
        in_specs=[SMEM, SMEM, SMEM, VMEM],
        out_specs=VMEM,
        compiler_params=params,
        name="pick",
    )(place, cells, source_rows, around.reshape(lons * 9, 1, 128))
    everything = lax.all_to_all(chosen.reshape(lats, 3 * CELLS, 128), "lat", 0, 0, tiled=True)
    everything = everything.reshape(lats * 3 * CELLS, 1, 128)

    block = jax.ShapeDtypeStruct((3, 16, 8, 128), f32)
    field = (3, 28, 24, 128)
    plane = jax.ShapeDtypeStruct((28, 24, 128), f32)
    half = jax.ShapeDtypeStruct((8, 8, 128), f32)
    prepared = pl.pallas_call(
        prepare_kernel,
        out_shape=[jax.ShapeDtypeStruct(field, f32)] + [plane] * 6
        + [jax.ShapeDtypeStruct((16, 8, 128), f32), half, half],
        in_specs=[SMEM] + [VMEM] * 6,
        out_specs=[VMEM] * 10,
        scratch_shapes=[pltpu.VMEM((28, 24, 128), f32)],
        compiler_params=params,
        name="prepare",
    )(place, f, mu, left, right, above, below)
    residual, smoothed, message = pl.pallas_call(
        smooth_kernel,
        out_shape=(block, block, jax.ShapeDtypeStruct((10, 8, 128), f32)),
        in_specs=[SMEM, SMEM] + [VMEM] * 16,
        out_specs=(VMEM, VMEM, VMEM),
        scratch_shapes=[pltpu.VMEM(field, f32)] * 2,
        compiler_params=params,
        name="smooth",
    )(place, ghost_rows, v, left, right, above, below, everything, *prepared)

    tiles = [
        shifted(message, 0, 2),
        shifted(message, 0, 1),
        message,
        shifted(message, 0, -1),
        shifted(message, 0, -2),
    ]
    band = jnp.concatenate(tiles, axis=1)
    band_below = shifted(band, -1, 0)
    band_above = shifted(band, 1, 0)
    coarse = pltpu.VMEM((22, 40, 128), f32)
    new = pl.pallas_call(
        coarse_kernel,
        out_shape=block,
        in_specs=[VMEM] * 4,
        out_specs=VMEM,
        scratch_shapes=[coarse, coarse, coarse, pltpu.VMEM((2, 22, 40, 128), f32)] + [coarse] * 6,
        compiler_params=params,
        name="coarse",
    )(band, band_above, band_below, smoothed)
    return new[None], residual[None]


def solution(mesh):
    placed = (
        P("patch", None, "lat", "lon", None),
        P("patch", None, "lat", "lon", None),
        P("patch", "lat", "lon", None),
        P("patch", None),
        P("patch", "lat", "lon"),
        P("patch", "lat", "lon"),
        P("patch", "lat", None, "lon"),
    )
    return jax.shard_map(
        per_device,
        mesh=mesh,
        in_specs=placed,
        out_specs=(P("patch", None, "lat", "lon", None), P("patch", None, "lat", "lon", None)),
        check_vma=False,
    )
```

```python
import jax
import jax.numpy as jnp
from jax import lax
from jax.experimental import pallas as pl
from jax.experimental.pallas import tpu as pltpu
from jax.sharding import PartitionSpec as P


AXES = ("patch", "lat", "lon")
RELAX = 0.8
COARSE = 8
PAD = 6
CELLS = 32
VMEM = pl.BlockSpec(memory_space=pltpu.VMEM)
SMEM = pl.BlockSpec(memory_space=pltpu.SMEM)


def shifted(value, by_lat, by_lon):
    patches, lats, lons = (lax.axis_size(axis) for axis in AXES)
    pairs = []
    for p in range(patches):
        for a in range(lats):
            for b in range(lons):
                a2, b2 = a + by_lat, b + by_lon
                if 0 <= a2 < lats and 0 <= b2 < lons:
                    pairs.append(((p * lats + a) * lons + b, (p * lats + a2) * lons + b2))
    return lax.ppermute(value, AXES, pairs)


def lanes_of(shape):
    return lax.broadcasted_iota(jnp.int32, shape, len(shape) - 1)


def rows_of(shape):
    return lax.broadcasted_iota(jnp.int32, shape, len(shape) - 2)


def roll(value, by, axis):
    return pltpu.roll(value, by % value.shape[axis], axis)


def lane_partner(value, odd_lane):
    return jnp.where(odd_lane, roll(value, 1, 1), roll(value, -1, 1))


def row_partner(value, odd_row):
    return jnp.where(odd_row, roll(value, 1, 0), roll(value, -1, 0))


def interp_kernel(
    rows_ref, cols_ref, weights_ref, v_ref, right_ref, below_ref, corner_ref, out_ref, pad_ref
):
    rows = v_ref.shape[1]
    for comp in range(3):
        pad_ref[comp, :rows, 0:8] = v_ref[comp]
        pad_ref[comp, rows, 0:8] = below_ref[comp, 0]
        for row in range(rows):
            pad_ref[comp, row, 8:9] = right_ref[comp, row : row + 1]
        pad_ref[comp, rows, 8:9] = corner_ref[comp : comp + 1]
    for slot in range(3):
        row, col = rows_ref[slot], cols_ref[slot]
        for comp in range(3):
            total = weights_ref[0, slot] * pad_ref[comp, row, pl.ds(col, 1), :]
            total = total + weights_ref[1, slot] * pad_ref[comp, row + 1, pl.ds(col, 1), :]
            total = total + weights_ref[2, slot] * pad_ref[comp, row, pl.ds(col + 1, 1), :]
            total = total + weights_ref[3, slot] * pad_ref[comp, row + 1, pl.ds(col + 1, 1), :]
            out_ref[slot * 3 + comp : slot * 3 + comp + 1] = total


def pick_kernel(place_ref, cells_ref, source_ref, row_ref, out_ref):
    lon, last_lat, last_lon = place_ref[1], place_ref[2], place_ref[3]
    edge = (lon == 0) | (lon == last_lon)

    def copy(dest, position):
        base = source_ref[cells_ref[dest * CELLS + position]]
        for comp in range(3):
            out_ref[dest * 3 * CELLS + position * 3 + comp] = row_ref[base + comp]

    @pl.when(edge)
    def _():
        def step(dest, carry):
            for position in range(CELLS):
                copy(dest, position)
            return carry

        lax.fori_loop(0, last_lat + 1, step, 0)

    @pl.when(~edge)
    def _():
        for position in range(16):
            copy(0, position)
            copy(last_lat, position)


def pack_kernel(v_ref, f_ref, mu_ref, above_ref, below_ref, right_ref, left_ref):
    sub = rows_of((8, 128))

    def row(field, r):
        if r < 0:
            return above_ref[field, r + 5]
        if r > 15:
            return below_ref[field, r - 16]
        if field == 6:
            return mu_ref[r]
        return v_ref[field, r] if field < 3 else f_ref[field - 3, r]

    for field in range(7):
        for t in range(12):
            even, odd = row(field, 2 * t - 4), roll(row(field, 2 * t - 3), 4, 0)
            right_ref[12 * field + t] = jnp.where(sub < 4, odd, even)
            left_ref[12 * field + t] = jnp.where(sub < 4, even, odd)
    for n, field in enumerate((0, 1, 2, 6)):
        for j in range(2):
            third = fourth = row(field, 8 * j)
            for s in range(8):
                value = row(field, 8 * j + s)
                third = jnp.where(sub == s, roll(value, s - 3, 0), third)
                fourth = jnp.where(sub == s, roll(value, s - 4, 0), fourth)
            right_ref[84 + 2 * n + j] = third
            left_ref[84 + 2 * n + j] = fourth


def side_tile(ref, field, r, col, sub):
    value = ref[12 * field + (r + 4) // 2]
    if r % 2:
        value = roll(value, 4, 0)
    extra = {0: 0, 1: 1, 2: 2, 6: 3}.get(field)
    if extra is None or not 0 <= r < 16:
        return value
    fifth = roll(ref[84 + 2 * extra + r // 8], col - r % 8, 0)
    return jnp.where(sub == col, fifth, value)


def prepare(
    place_ref, f_ref, mu_ref, left_ref, right_ref, above_ref, below_ref,
    F, C, DG, over_ref, visc_ref, MU,
):
    lat, lon = place_ref[0], place_ref[1]
    last_lat, last_lon = place_ref[2], place_ref[3]
    wide = (24, 128)
    lane, row = lanes_of(wide), rows_of(wide)
    odd_lane, odd_row = (lane & 1) == 1, (row & 1) == 1
    own = slice(PAD, PAD + 16)
    sub = rows_of((8, 128))
    MU[own, 8:16] = mu_ref[...]
    MU[1:6, 8:16] = above_ref[6]
    MU[22:27, 8:16] = below_ref[6]
    for r in range(-4, 20):
        MU[r + PAD, 0:8] = side_tile(left_ref, 6, r, 3, sub)
        MU[r + PAD, 16:24] = side_tile(right_ref, 6, r, 4, sub)
    for i in (1, 26):
        MU[i, 0:8] = MU[i, 8:16]
        MU[i, 16:24] = MU[i, 8:16]

    @pl.when(lat == 0)
    def _():
        MU[4] = MU[6]
        MU[5] = MU[6]

    @pl.when(lat == last_lat)
    def _():
        MU[22] = MU[21]
        MU[23] = MU[21]

    @pl.when(lon == 0)
    def _():
        for i in range(1, 27):
            MU[i, 0:8] = jnp.broadcast_to(MU[i, 8:9], (8, 128))

    @pl.when(lon == last_lon)
    def _():
        for i in range(1, 27):
            MU[i, 16:24] = jnp.broadcast_to(MU[i, 15:16], (8, 128))

    for i in range(2, 26):
        mid = MU[i]
        north = 0.5 * (mid + MU[i - 1])
        south = 0.5 * (mid + MU[i + 1])
        west = 0.5 * (mid + roll(mid, 1, 0))
        east = 0.5 * (mid + roll(mid, -1, 0))
        down = 0.5 * (mid + jnp.where(lane == 0, mid, roll(mid, 1, 1)))
        up = 0.5 * (mid + jnp.where(lane == 127, mid, roll(mid, -1, 1)))
        total = north + south + west + east + down + up
        inverse = 1.0 / total
        C[0, i] = north * inverse
        C[1, i] = south * inverse
        C[2, i] = west * inverse
        C[3, i] = east * inverse
        C[4, i] = jnp.where(lane == 0, 0.0, down * inverse)
        C[5, i] = jnp.where(lane == 127, 0.0, up * inverse)
        r = i - PAD
        if 0 <= r < 16:
            DG[r] = total[8:16]
        for comp in range(3):
            if r < 0:
                force = above_ref[3 + comp, r + 5]
            else:
                force = f_ref[comp, r] if r < 16 else below_ref[3 + comp, r - 16]
            F[comp, i, 8:16] = force * inverse[8:16]
            F[comp, i, 0:8] = side_tile(left_ref, 3 + comp, r, 3, sub) * inverse[0:8]
            F[comp, i, 16:24] = side_tile(right_ref, 3 + comp, r, 4, sub) * inverse[16:24]

    def coarse_visc(i):
        both = MU[i] + MU[i + 1]
        flat = 0.25 * (both + row_partner(both, odd_row))
        return flat, 0.5 * (flat + lane_partner(flat, odd_lane))

    layers = [coarse_visc(PAD + 2 * k) for k in (-1, 0)]
    for k in range(8):
        layers.append(coarse_visc(PAD + 2 * k + 2))
        before, (flat, visc), after = layers[k][1], layers[k + 1], layers[k + 2][1]
        edge_down = jnp.where(lane == 0, flat, roll(flat, 1, 1))
        edge_up = jnp.where(lane == 127, flat, roll(flat, -1, 1))
        total = 6.0 * visc + before + after + roll(visc, 2, 0) + roll(visc, -2, 0)
        total = total + jnp.where(lane < 2, edge_down, roll(visc, 2, 1))
        total = total + jnp.where(lane >= 126, edge_up, roll(visc, -2, 1))
        over_ref[k] = RELAX / (0.125 * total[8:16])
        visc_ref[k] = visc[8:16]


def smooth_kernel(
    place_ref, ghost_ref, v_ref, f_ref, mu_ref, left_ref, right_ref, above_ref, below_ref, slot_ref,
    res_ref, smooth_ref, message_ref, A, B, F, C, DG, over_ref, visc_ref, MU,
):
    lat, lon = place_ref[0], place_ref[1]
    last_lat, last_lon = place_ref[2], place_ref[3]
    wide = (24, 128)
    lane, row = lanes_of(wide), rows_of(wide)
    sub = rows_of((8, 128))
    own = slice(PAD, PAD + 16)

    for comp in range(3):
        A[comp, own, 8:16] = v_ref[comp]
        A[comp, 1:6, 8:16] = above_ref[comp]
        A[comp, 22:27, 8:16] = below_ref[comp]
        for r in range(-4, 20):
            A[comp, r + PAD, 0:8] = side_tile(left_ref, comp, r, 3, sub)
            A[comp, r + PAD, 16:24] = side_tile(right_ref, comp, r, 4, sub)
        for i in (1, 26):
            A[comp, i, 0:8] = A[comp, i, 8:16]
            A[comp, i, 16:24] = A[comp, i, 8:16]

    edge = (lon == 0) | (lon == last_lon)
    all_cols, all_rows = (last_lon + 1) * 8, (last_lat + 1) * 16

    def fill_row(i, start):
        for col in range(-4, 12):
            along = jnp.where(lon == 0, col, col + 4)
            packed_at = jnp.where((lat == 0) & (along < 4), along, along + 20)
            position = jnp.clip(jnp.where(edge, packed_at, col + 4), 0, CELLS - 1)
            cell = start + jnp.clip(lon * 8 + col, 0, all_cols - 1)
            base = ghost_ref[cell] + 3 * position
            for comp in range(3):
                A[comp, i, 8 + col : 9 + col] = slot_ref[base + comp]

    def fill_side(col, start):
        for r in range(-4, 20):
            base = ghost_ref[start + jnp.clip(lat * 16 + r, 0, all_rows - 1)] + 3 * (r + 4)
            for comp in range(3):
                A[comp, r + PAD, 8 + col : 9 + col] = slot_ref[base + comp]

    prepare(
        place_ref, f_ref, mu_ref, left_ref, right_ref, above_ref, below_ref,
        F, C, DG, over_ref, visc_ref, MU,
    )
    pl.when(lat == 0)(lambda: fill_row(5, 0))
    pl.when(lat == last_lat)(lambda: fill_row(22, all_cols))
    pl.when(lon == 0)(lambda: fill_side(-1, 2 * all_cols))
    pl.when(lon == last_lon)(lambda: fill_side(8, 2 * all_cols + all_rows))

    inside = ((row >= 8) | (lon > 0)) & ((row < 16) | (lon < last_lon))
    parity = jnp.where(inside, (row + lane) & 1, 2)

    def weighted(source, comp, i, here):
        total = F[comp, i] + C[0, i] * source[comp, i - 1]
        total = total + C[1, i] * source[comp, i + 1]
        total = total + C[2, i] * roll(here, 1, 0)
        total = total + C[3, i] * roll(here, -1, 0)
        total = total + C[4, i] * roll(here, 1, 1)
        return total + C[5, i] * roll(here, -1, 1)

    wanted = {}
    for colour in range(2):
        wanted[colour, "mid"] = jnp.int32(colour)
        wanted[colour, "top"] = jnp.where(lat == 0, 3, colour)
        wanted[colour, "low"] = jnp.where(lat == last_lat, 3, colour)

    def relax(colour, reach, source, target):
        for r in range(-reach, 16 + reach):
            i = r + PAD
            zone = "top" if r < 0 else "low" if r > 15 else "mid"
            mask = parity == wanted[(colour + r) % 2, zone]
            for comp in range(3):
                here = source[comp, i]
                target[comp, i] = jnp.where(mask, weighted(source, comp, i, here), here)

    relax(0, 4, A, B)
    relax(1, 3, B, A)
    relax(0, 2, A, B)
    relax(1, 1, B, A)

    tile = (8, 128)
    lane8, row8 = lanes_of(tile), rows_of(tile)
    odd_lane8, odd_row8 = (lane8 & 1) == 1, (row8 & 1) == 1

    def packed(parts):
        low = jnp.where(odd_lane8, parts[1], parts[0])
        high = jnp.where(odd_lane8, parts[3], parts[2])
        return jnp.where(odd_row8, high, low)

    for k in range(8):
        parts = []
        for comp in range(3):
            rhs = jnp.zeros(tile, jnp.float32)
            for r in (2 * k, 2 * k + 1):
                here = A[comp, r + PAD]
                smooth_ref[comp, r] = here[8:16]
                left = DG[r] * (weighted(A, comp, r + PAD, here) - here)[8:16]
                res_ref[comp, r] = left
                rhs = rhs + left
            rhs = rhs + lane_partner(rhs, odd_lane8)
            rhs = rhs + row_partner(rhs, odd_row8)
            parts.append(0.125 * rhs * over_ref[k])
        message_ref[k] = packed(parts + [visc_ref[k]])
        if k % 4 == 3:
            message_ref[8 + k // 4] = packed([over_ref[j] for j in range(k - 3, k + 1)])


def coarse_kernel(
    mid_ref, above_ref, below_ref, smooth_ref, out_ref, Q, CV, DV, E, AN, AS, AW, AE, AD, AU
):
    wide = (40, 128)
    lane, row = lanes_of(wide), rows_of(wide)
    odd_lane, odd_row = (lane & 1) == 1, (row & 1) == 1

    def spread(value, part, odd_l, odd_r):
        keep = odd_l if part % 2 else ~odd_l
        value = jnp.where(keep, value, roll(value, -1 if part % 2 else 1, 1))
        keep = odd_r if part // 2 else ~odd_r
        return jnp.where(keep, value, roll(value, -1 if part // 2 else 1, 0))

    def far(n):
        return max(0, 7 - n, n - 14)

    for n in range(22):
        away = far(n)
        if away == 0:
            t = n - 7
            Q[n] = mid_ref[t]
            cols, over = slice(0, 40), mid_ref[8 + t // 4]
        else:
            ref, t = (above_ref, n + 1) if n < 7 else (below_ref, n - 15)
            tiles = range(5) if away < 3 else range(1, 4)
            first = 5 * (away - 1) if away < 3 else 10 + 3 * (away - 3) - 1
            for j in tiles:
                Q[n, 8 * j : 8 * j + 8] = ref[first + j]
            cols = slice(8 * tiles[0], 8 * tiles[-1] + 8)
            over = [ref[25 + 5 * (t // 4) + j] for j in tiles]
            over = jnp.concatenate(over, axis=0)
        CV[n, cols] = spread(Q[n, cols], 3, odd_lane[cols], odd_row[cols])
        DV[n, cols] = 0.125 * spread(over, t % 4, odd_lane[cols], odd_row[cols])

    def span(reach):
        return slice(0, 40) if reach > 3 else slice(8, 32)

    for n in range(1, 21):
        cols = span(6 - far(n))
        edge = lane[cols]
        visc, over = CV[n, cols], DV[n, cols]
        AN[n, cols] = over * (visc + CV[n - 1, cols])
        AS[n, cols] = over * (visc + CV[n + 1, cols])
        AW[n, cols] = over * (visc + roll(visc, 2, 0))
        AE[n, cols] = over * (visc + roll(visc, -2, 0))
        AD[n, cols] = jnp.where(edge < 2, 0.0, over * (visc + roll(visc, 2, 1)))
        AU[n, cols] = jnp.where(edge >= 126, 0.0, over * (visc + roll(visc, -2, 1)))

    for turn in range(1, COARSE):
        old = Q if turn == 1 else E.at[turn % 2]
        new = E.at[(turn + 1) % 2]
        for n in range(turn, 22 - turn):
            cols = span(7 - turn - far(n))
            here = old[n, cols]
            total = Q[n, cols] + (1.0 - RELAX) * here
            total = total + AN[n, cols] * old[n - 1, cols]
            total = total + AS[n, cols] * old[n + 1, cols]
            total = total + AW[n, cols] * roll(here, 2, 0)
            total = total + AE[n, cols] * roll(here, -2, 0)
            total = total + AD[n, cols] * roll(here, 2, 1)
            new[n, cols] = total + AU[n, cols] * roll(here, -2, 1)

    final = E.at[COARSE % 2]
    tile = (8, 128)
    lane8, row8 = lanes_of(tile), rows_of(tile)
    odd_lane8, odd_row8 = (lane8 & 1) == 1, (row8 & 1) == 1
    for k in range(8):
        value = final[7 + k, 16:24]
        for comp in range(3):
            error = spread(value, comp, odd_lane8, odd_row8)
            for r in (2 * k, 2 * k + 1):
                out_ref[comp, r] = smooth_ref[comp, r] + error


def wanted_cells(lats, lons, lon):
    dest = jnp.arange(lats, dtype=jnp.int32)[:, None]
    position = jnp.arange(CELLS, dtype=jnp.int32)[None, :]
    rows, cols = lats * 16, lons * 8
    edge = (lon == 0) | (lon == lons - 1)
    side_row = dest * 16 + position - 4
    on_side = edge & (position < 24) & (side_row >= 0) & (side_row < rows)
    side = 2 * cols + jnp.where(lon == 0, 0, rows) + jnp.clip(side_row, 0, rows - 1)
    along = jnp.where((dest == 0) & (position < 4), position, position - 20)
    corner_col = jnp.where(lon == 0, along, lon * 8 + along - 4)
    col = jnp.where(edge, corner_col, lon * 8 + position - 4)
    row_cell = jnp.where(dest == 0, 0, cols) + jnp.clip(col, 0, cols - 1)
    return jnp.where(on_side, side, row_cell)


def per_device(velocity, forcing, viscosity, ghost_slots, corner_rows, corner_cols, corner_weights):
    v, f, mu = velocity[0], forcing[0], viscosity[0]
    lats, lons = lax.axis_size("lat"), lax.axis_size("lon")
    params = pltpu.CompilerParams(vmem_limit_bytes=32 * 2**20)
    f32 = jnp.float32
    place = jnp.stack(
        [lax.axis_index("lat"), lax.axis_index("lon"), jnp.int32(lats - 1), jnp.int32(lons - 1)]
    ).astype(jnp.int32)
    slots = ghost_slots[0]
    source_rows = ((slots // 3) % lons) * 9 + (slots % 3) * 3
    ghost_rows = (slots // (3 * lons)) * (3 * CELLS)
    cells = wanted_cells(lats, lons, lax.axis_index("lon")).reshape(-1)

    corner_right = shifted(v[:, :, 0], 0, -1)
    corner_both = shifted(v[:, 0, 0], -1, -1)
    top = jnp.concatenate([v[:, :5], f[:, :5], mu[None, :5]], axis=0)
    low = jnp.concatenate([v[:, 11:], f[:, 11:], mu[None, 11:]], axis=0)
    below = shifted(top, -1, 0)
    above = shifted(low, 1, 0)
    values = pl.pallas_call(
        interp_kernel,
        out_shape=jax.ShapeDtypeStruct((9, 128), f32),
        in_specs=[SMEM] * 3 + [VMEM] * 4,
        out_specs=VMEM,
        scratch_shapes=[pltpu.VMEM((3, 17, 16, 128), f32)],
        compiler_params=params,
        name="interp",
    )(
        corner_rows[0, 0], corner_cols[0, 0], corner_weights[0, 0],
        v, corner_right, below, corner_both,
    )
    values = lax.ppermute(values, "patch", [(0, 1), (1, 0)])
    spread = jnp.broadcast_to(values.reshape(1, 1, 1152), (lons, 1, 1152))
    around = lax.all_to_all(spread, "lon", 0, 0, tiled=True)

    message_tiles = jax.ShapeDtypeStruct((92, 8, 128), f32)
    to_right, to_left = pl.pallas_call(
        pack_kernel,
        out_shape=(message_tiles, message_tiles),
        in_specs=[VMEM] * 5,
        out_specs=(VMEM, VMEM),
        compiler_params=params,
        name="pack",
    )(v, f, mu, above, below)
    left = shifted(to_right, 0, 1)
    right = shifted(to_left, 0, -1)

    chosen = pl.pallas_call(
        pick_kernel,
        out_shape=jax.ShapeDtypeStruct((lats * 3 * CELLS, 1, 128), f32),
        in_specs=[SMEM, SMEM, SMEM, VMEM],
        out_specs=VMEM,
        compiler_params=params,
        name="pick",
    )(place, cells, source_rows, around.reshape(lons * 9, 1, 128))
    everything = lax.all_to_all(chosen.reshape(lats, 3 * CELLS, 128), "lat", 0, 0, tiled=True)
    everything = everything.reshape(lats * 3 * CELLS, 1, 128)

    block = jax.ShapeDtypeStruct((3, 16, 8, 128), f32)
    field = (3, 28, 24, 128)
    residual, smoothed, message = pl.pallas_call(
        smooth_kernel,
        out_shape=(block, block, jax.ShapeDtypeStruct((10, 8, 128), f32)),
        in_specs=[SMEM, SMEM] + [VMEM] * 8,
        out_specs=(VMEM, VMEM, VMEM),
        scratch_shapes=[pltpu.VMEM(field, f32)] * 3
        + [
            pltpu.VMEM(shape, f32)
            for shape in ((6, 28, 24, 128), (16, 8, 128), (8, 8, 128), (8, 8, 128), (28, 24, 128))
        ],
        compiler_params=params,
        name="smooth",
    )(place, ghost_rows, v, f, mu, left, right, above, below, everything)

    tiles = [
        shifted(message, 0, 2),
        shifted(message, 0, 1),
        message,
        shifted(message, 0, -1),
        shifted(message, 0, -2),
    ]
    band = jnp.concatenate(tiles, axis=1)
    tile_list = (-1, 8, 128)
    inverse = band[8:10].reshape(tile_list)
    to_above = [band[0:2].reshape(tile_list), band[2:7, 8:32].reshape(tile_list), inverse]
    to_below = [band[7:8], band[6:7]] + [band[r : r + 1, 8:32] for r in (5, 4, 3, 2, 1)]
    to_below = [part.reshape(tile_list) for part in to_below] + [inverse]
    band_below = shifted(jnp.concatenate(to_above, axis=0), -1, 0)
    band_above = shifted(jnp.concatenate(to_below, axis=0), 1, 0)
    coarse = pltpu.VMEM((22, 40, 128), f32)
    new = pl.pallas_call(
        coarse_kernel,
        out_shape=block,
        in_specs=[VMEM] * 4,
        out_specs=VMEM,
        scratch_shapes=[coarse, coarse, coarse, pltpu.VMEM((2, 22, 40, 128), f32)] + [coarse] * 6,
        compiler_params=params,
        name="coarse",
    )(band, band_above, band_below, smoothed)
    return new[None], residual[None]


def solution(mesh):
    placed = (
        P("patch", None, "lat", "lon", None),
        P("patch", None, "lat", "lon", None),
        P("patch", "lat", "lon", None),
        P("patch", None),
        P("patch", "lat", "lon"),
        P("patch", "lat", "lon"),
        P("patch", "lat", None, "lon"),
    )
    return jax.shard_map(
        per_device,
        mesh=mesh,
        in_specs=placed,
        out_specs=(P("patch", None, "lat", "lon", None), P("patch", None, "lat", "lon", None)),
        check_vma=False,
    )
```

```python
import jax
import jax.numpy as jnp
from jax import lax
from jax.experimental import pallas as pl
from jax.experimental.pallas import tpu as pltpu
from jax.sharding import PartitionSpec as P


AXES = ("patch", "lat", "lon")
RELAX = 0.8
COARSE = 8
PAD = 6
CELLS = 32
VMEM = pl.BlockSpec(memory_space=pltpu.VMEM)
SMEM = pl.BlockSpec(memory_space=pltpu.SMEM)


def shifted(value, by_lat, by_lon):
    patches, lats, lons = (lax.axis_size(axis) for axis in AXES)
    pairs = []
    for p in range(patches):
        for a in range(lats):
            for b in range(lons):
                a2, b2 = a + by_lat, b + by_lon
                if 0 <= a2 < lats and 0 <= b2 < lons:
                    pairs.append(((p * lats + a) * lons + b, (p * lats + a2) * lons + b2))
    return lax.ppermute(value, AXES, pairs)


def lanes_of(shape):
    return lax.broadcasted_iota(jnp.int32, shape, len(shape) - 1)


def rows_of(shape):
    return lax.broadcasted_iota(jnp.int32, shape, len(shape) - 2)


def roll(value, by, axis):
    return pltpu.roll(value, by % value.shape[axis], axis)


def lane_partner(value, odd_lane):
    return jnp.where(odd_lane, roll(value, 1, 1), roll(value, -1, 1))


def row_partner(value, odd_row):
    return jnp.where(odd_row, roll(value, 1, 0), roll(value, -1, 0))


def first_kernel(v_ref, edge_ref, below_ref, corner_ref):
    sub = rows_of((8, 128))
    for comp in range(3):
        corner_ref[comp : comp + 1] = v_ref[comp, 0, 0:1]
        below_ref[comp] = v_ref[comp, 0]
        for j in range(2):
            first = v_ref[comp, 8 * j]
            for r in range(1, 8):
                first = jnp.where(sub == r, roll(v_ref[comp, 8 * j + r], r, 0), first)
            edge_ref[comp, 8 * j : 8 * j + 8] = first


def cut_kernel(v_ref, f_ref, mu_ref, right_ref, left_ref):
    sub = rows_of((8, 128))

    def row(field, r):
        if field == 6:
            return mu_ref[r]
        return v_ref[field, r] if field < 3 else f_ref[field - 3, r]

    for field in range(7):
        for t in range(8):
            even, odd = row(field, 2 * t), roll(row(field, 2 * t + 1), 4, 0)
            right_ref[8 * field + t] = jnp.where(sub < 4, odd, even)
            left_ref[8 * field + t] = jnp.where(sub < 4, even, odd)
    for n, field in enumerate((0, 1, 2, 6)):
        for j in range(2):
            third = fourth = row(field, 8 * j)
            for r in range(8):
                value = row(field, 8 * j + r)
                third = jnp.where(sub == r, roll(value, r - 3, 0), third)
                fourth = jnp.where(sub == r, roll(value, r - 4, 0), fourth)
            right_ref[56 + 2 * n + j] = third
            left_ref[56 + 2 * n + j] = fourth


def blend_kernel(rows_ref, cols_ref, weights_ref, v_ref, own_ref, edge_ref, below_ref, corner_ref):
    tall, flat = rows_of((16, 128)), rows_of((8, 128))
    for slot in range(3):
        row, col = rows_ref[slot], cols_ref[slot]
        w0, w1, w2, w3 = (weights_ref[k, slot] for k in range(4))
        here, next_one = flat == col, flat == col + 1
        upper = jnp.where(here, w0, jnp.where(next_one, w2, 0.0))
        lower = jnp.where(here, w1, jnp.where(next_one, w3, 0.0))
        within = row < 15
        next_row = jnp.where(within, row + 1, row)
        inner = jnp.where(within, lower, 0.0)
        for comp in range(3):
            total = upper * v_ref[comp, row] + inner * v_ref[comp, next_row]
            own_ref[3 * slot + comp] = jnp.sum(total, axis=0, keepdims=True)
        beside = jnp.where(tall == row, w2, jnp.where(tall == row + 1, w3, 0.0))
        edge_ref[slot] = jnp.where(col == 7, beside, 0.0)
        below_ref[slot] = jnp.where(within, 0.0, lower)
        both = jnp.where((row == 15) & (col == 7), w3, 0.0)
        corner_ref[slot] = jnp.full((1, 128), both, jnp.float32)


def interp_kernel(
    own_ref, edge_w, below_w, corner_w, edge_ref, below_ref, corner_ref, out_ref
):
    for slot in range(3):
        for comp in range(3):
            beside = edge_w[slot] * edge_ref[comp]
            total = beside[0:8] + beside[8:16] + below_w[slot] * below_ref[comp]
            total = jnp.sum(total, axis=0, keepdims=True) + own_ref[3 * slot + comp]
            total = total + corner_w[slot] * corner_ref[comp : comp + 1]
            for dest in range(out_ref.shape[0] // 9):
                out_ref[9 * dest + 3 * slot + comp] = total


def pick_kernel(place_ref, cells_ref, source_ref, row_ref, out_ref):
    lon, last_lat, last_lon = place_ref[1], place_ref[2], place_ref[3]
    edge = (lon == 0) | (lon == last_lon)

    def copy(dest, position):
        base = source_ref[cells_ref[dest * CELLS + position]]
        for comp in range(3):
            out_ref[dest * 3 * CELLS + position * 3 + comp] = row_ref[base + comp]

    @pl.when(edge)
    def _():
        def step(dest, carry):
            for position in range(CELLS):
                copy(dest, position)
            return carry

        lax.fori_loop(0, last_lat + 1, step, 0)

    @pl.when(~edge)
    def _():
        for position in range(16):
            copy(0, position)
            copy(last_lat, position)


def lat_tile(field, away, side):
    if field in (0, 1, 2, 6):
        return 9 * (field if field < 6 else 3) + (5 if side else 0) + away - 1
    return 36 + 7 * (field - 3) + (4 if side else 0) + away - 1


def side_tile(ref, field, r, col, sub):
    value = ref[8 * field + r // 2]
    if r % 2:
        value = roll(value, 4, 0)
    extra = {0: 0, 1: 1, 2: 2, 6: 3}.get(field)
    if extra is None:
        return value
    fifth = roll(ref[56 + 2 * extra + r // 8], col - r % 8, 0)
    return jnp.where(sub == col, fifth, value)


def pack_kernel(v_ref, f_ref, mu_ref, left_ref, right_ref, up_ref, down_ref):
    sub = rows_of((8, 128))
    for field in range(7):
        force = 3 <= field < 6
        for away in range(1, 5 if force else 6):
            for ref, r in ((up_ref, away - 1), (down_ref, 16 - away)):
                if field == 6:
                    value = mu_ref[r]
                else:
                    value = f_ref[field - 3, r] if force else v_ref[field, r]
                ref[lat_tile(field, away, False)] = value
                if away < (4 if force else 5):
                    ref[lat_tile(field, away, True)] = jnp.where(
                        sub < 4,
                        side_tile(right_ref, field, r, 4, sub),
                        side_tile(left_ref, field, r, 3, sub),
                    )


def prepare(
    place_ref, f_ref, mu_ref, left_ref, right_ref, above_ref, below_ref,
    F, C, DG, over_ref, visc_ref, MU,
):
    lat, lon = place_ref[0], place_ref[1]
    last_lat, last_lon = place_ref[2], place_ref[3]
    wide = (24, 128)
    lane, row = lanes_of(wide), rows_of(wide)
    odd_lane, odd_row = (lane & 1) == 1, (row & 1) == 1
    own = slice(PAD, PAD + 16)
    sub = rows_of((8, 128))

    def outer(ref, field, away, side):
        return ref[lat_tile(field, away, side)]

    MU[own, 8:16] = mu_ref[...]
    for r in range(16):
        MU[r + PAD, 0:8] = side_tile(left_ref, 6, r, 3, sub)
        MU[r + PAD, 16:24] = side_tile(right_ref, 6, r, 4, sub)
    for away in range(1, 6):
        for i, ref in ((PAD - away, above_ref), (PAD + 15 + away, below_ref)):
            value = outer(ref, 6, away, False)
            beside = outer(ref, 6, away, True) if away < 5 else value
            MU[i, 0:8], MU[i, 8:16], MU[i, 16:24] = beside, value, beside

    @pl.when(lat == 0)
    def _():
        MU[4] = MU[6]
        MU[5] = MU[6]

    @pl.when(lat == last_lat)
    def _():
        MU[22] = MU[21]
        MU[23] = MU[21]

    @pl.when(lon == 0)
    def _():
        for i in range(1, 27):
            MU[i, 0:8] = jnp.broadcast_to(MU[i, 8:9], (8, 128))

    @pl.when(lon == last_lon)
    def _():
        for i in range(1, 27):
            MU[i, 16:24] = jnp.broadcast_to(MU[i, 15:16], (8, 128))

    for i in range(2, 26):
        mid = MU[i]
        north = 0.5 * (mid + MU[i - 1])
        south = 0.5 * (mid + MU[i + 1])
        west = 0.5 * (mid + roll(mid, 1, 0))
        east = 0.5 * (mid + roll(mid, -1, 0))
        down = 0.5 * (mid + jnp.where(lane == 0, mid, roll(mid, 1, 1)))
        up = 0.5 * (mid + jnp.where(lane == 127, mid, roll(mid, -1, 1)))
        total = north + south + west + east + down + up
        inverse = 1.0 / total
        C[0, i] = north * inverse
        C[1, i] = south * inverse
        C[2, i] = west * inverse
        C[3, i] = east * inverse
        C[4, i] = jnp.where(lane == 0, 0.0, down * inverse)
        C[5, i] = jnp.where(lane == 127, 0.0, up * inverse)
        r = i - PAD
        if 0 <= r < 16:
            DG[r] = total[8:16]
        for comp in range(3):
            if 0 <= r < 16:
                force = f_ref[comp, r]
                west_force = side_tile(left_ref, 3 + comp, r, 3, sub)
                east_force = side_tile(right_ref, 3 + comp, r, 4, sub)
            else:
                ref, away = (above_ref, -r) if r < 0 else (below_ref, r - 15)
                force = outer(ref, 3 + comp, away, False)
                beside = outer(ref, 3 + comp, away, True) if away < 4 else force
                west_force = east_force = beside
            F[comp, i, 0:8] = west_force * inverse[0:8]
            F[comp, i, 8:16] = force * inverse[8:16]
            F[comp, i, 16:24] = east_force * inverse[16:24]

    def coarse_visc(i):
        both = MU[i] + MU[i + 1]
        flat = 0.25 * (both + row_partner(both, odd_row))
        return flat, 0.5 * (flat + lane_partner(flat, odd_lane))

    layers = [coarse_visc(PAD + 2 * k) for k in (-1, 0)]
    for k in range(8):
        layers.append(coarse_visc(PAD + 2 * k + 2))
        before, (flat, visc), after = layers[k][1], layers[k + 1], layers[k + 2][1]
        edge_down = jnp.where(lane == 0, flat, roll(flat, 1, 1))
        edge_up = jnp.where(lane == 127, flat, roll(flat, -1, 1))
        total = 6.0 * visc + before + after + roll(visc, 2, 0) + roll(visc, -2, 0)
        total = total + jnp.where(lane < 2, edge_down, roll(visc, 2, 1))
        total = total + jnp.where(lane >= 126, edge_up, roll(visc, -2, 1))
        over_ref[k] = RELAX / (0.125 * total[8:16])
        visc_ref[k] = visc[8:16]


def smooth_kernel(
    place_ref, ghost_ref, v_ref, f_ref, mu_ref, left_ref, right_ref, above_ref, below_ref, slot_ref,
    res_ref, smooth_ref, message_ref, A, B, F, C, DG, over_ref, visc_ref, MU,
):
    lat, lon = place_ref[0], place_ref[1]
    last_lat, last_lon = place_ref[2], place_ref[3]
    wide = (24, 128)
    lane, row = lanes_of(wide), rows_of(wide)
    sub = rows_of((8, 128))
    own = slice(PAD, PAD + 16)

    for comp in range(3):
        A[comp, own, 8:16] = v_ref[comp]
        for r in range(16):
            A[comp, r + PAD, 0:8] = side_tile(left_ref, comp, r, 3, sub)
            A[comp, r + PAD, 16:24] = side_tile(right_ref, comp, r, 4, sub)
        for away in range(1, 6):
            for i, ref in ((PAD - away, above_ref), (PAD + 15 + away, below_ref)):
                value = ref[lat_tile(comp, away, False)]
                beside = ref[lat_tile(comp, away, True)] if away < 5 else value
                A[comp, i, 0:8], A[comp, i, 8:16], A[comp, i, 16:24] = beside, value, beside

    edge = (lon == 0) | (lon == last_lon)
    all_cols, all_rows = (last_lon + 1) * 8, (last_lat + 1) * 16

    def fill_row(i, start):
        for col in range(-4, 12):
            along = jnp.where(lon == 0, col, col + 4)
            packed_at = jnp.where((lat == 0) & (along < 4), along, along + 20)
            position = jnp.clip(jnp.where(edge, packed_at, col + 4), 0, CELLS - 1)
            cell = start + jnp.clip(lon * 8 + col, 0, all_cols - 1)
            base = ghost_ref[cell] + 3 * position
            for comp in range(3):
                A[comp, i, 8 + col : 9 + col] = slot_ref[base + comp]

    def fill_side(col, start):
        for r in range(-4, 20):
            base = ghost_ref[start + jnp.clip(lat * 16 + r, 0, all_rows - 1)] + 3 * (r + 4)
            for comp in range(3):
                A[comp, r + PAD, 8 + col : 9 + col] = slot_ref[base + comp]

    prepare(
        place_ref, f_ref, mu_ref, left_ref, right_ref, above_ref, below_ref,
        F, C, DG, over_ref, visc_ref, MU,
    )
    pl.when(lat == 0)(lambda: fill_row(5, 0))
    pl.when(lat == last_lat)(lambda: fill_row(22, all_cols))
    pl.when(lon == 0)(lambda: fill_side(-1, 2 * all_cols))
    pl.when(lon == last_lon)(lambda: fill_side(8, 2 * all_cols + all_rows))

    inside = ((row >= 8) | (lon > 0)) & ((row < 16) | (lon < last_lon))
    parity = jnp.where(inside, (row + lane) & 1, 2)

    def weighted(source, comp, i, here):
        total = F[comp, i] + C[0, i] * source[comp, i - 1]
        total = total + C[1, i] * source[comp, i + 1]
        total = total + C[2, i] * roll(here, 1, 0)
        total = total + C[3, i] * roll(here, -1, 0)
        total = total + C[4, i] * roll(here, 1, 1)
        return total + C[5, i] * roll(here, -1, 1)

    wanted = {}
    for colour in range(2):
        wanted[colour, "mid"] = jnp.int32(colour)
        wanted[colour, "top"] = jnp.where(lat == 0, 3, colour)
        wanted[colour, "low"] = jnp.where(lat == last_lat, 3, colour)

    def relax(colour, reach, source, target):
        for r in range(-reach, 16 + reach):
            i = r + PAD
            zone = "top" if r < 0 else "low" if r > 15 else "mid"
            mask = parity == wanted[(colour + r) % 2, zone]
            for comp in range(3):
                here = source[comp, i]
                target[comp, i] = jnp.where(mask, weighted(source, comp, i, here), here)

    relax(0, 4, A, B)
    relax(1, 3, B, A)
    relax(0, 2, A, B)
    relax(1, 1, B, A)

    tile = (8, 128)
    lane8, row8 = lanes_of(tile), rows_of(tile)
    odd_lane8, odd_row8 = (lane8 & 1) == 1, (row8 & 1) == 1

    def packed(parts):
        low = jnp.where(odd_lane8, parts[1], parts[0])
        high = jnp.where(odd_lane8, parts[3], parts[2])
        return jnp.where(odd_row8, high, low)

    for k in range(8):
        parts = []
        for comp in range(3):
            rhs = jnp.zeros(tile, jnp.float32)
            for r in (2 * k, 2 * k + 1):
                here = A[comp, r + PAD]
                smooth_ref[comp, r] = here[8:16]
                left = DG[r] * (weighted(A, comp, r + PAD, here) - here)[8:16]
                res_ref[comp, r] = left
                rhs = rhs + left
            rhs = rhs + lane_partner(rhs, odd_lane8)
            rhs = rhs + row_partner(rhs, odd_row8)
            parts.append(0.125 * rhs * over_ref[k])
        message_ref[k] = packed(parts + [visc_ref[k]])
        if k % 4 == 3:
            message_ref[8 + k // 4] = packed([over_ref[j] for j in range(k - 3, k + 1)])


def coarse_kernel(
    mid_ref, above_ref, below_ref, smooth_ref, out_ref, Q, CV, DV, E, AN, AS, AW, AE, AD, AU
):
    wide = (40, 128)
    lane, row = lanes_of(wide), rows_of(wide)
    odd_lane, odd_row = (lane & 1) == 1, (row & 1) == 1

    def spread(value, part, odd_l, odd_r):
        keep = odd_l if part % 2 else ~odd_l
        value = jnp.where(keep, value, roll(value, -1 if part % 2 else 1, 1))
        keep = odd_r if part // 2 else ~odd_r
        return jnp.where(keep, value, roll(value, -1 if part // 2 else 1, 0))

    def far(n):
        return max(0, 7 - n, n - 14)

    for n in range(22):
        away = far(n)
        if away == 0:
            t = n - 7
            Q[n] = mid_ref[t]
            cols, over = slice(0, 40), mid_ref[8 + t // 4]
        else:
            ref, t = (above_ref, n + 1) if n < 7 else (below_ref, n - 15)
            tiles = range(5) if away < 3 else range(1, 4)
            first = 5 * (away - 1) if away < 3 else 10 + 3 * (away - 3) - 1
            for j in tiles:
                Q[n, 8 * j : 8 * j + 8] = ref[first + j]
            cols = slice(8 * tiles[0], 8 * tiles[-1] + 8)
            over = [ref[25 + 5 * (t // 4) + j] for j in tiles]
            over = jnp.concatenate(over, axis=0)
        CV[n, cols] = spread(Q[n, cols], 3, odd_lane[cols], odd_row[cols])
        DV[n, cols] = 0.125 * spread(over, t % 4, odd_lane[cols], odd_row[cols])

    def span(reach):
        return slice(0, 40) if reach > 3 else slice(8, 32)

    for n in range(1, 21):
        cols = span(6 - far(n))
        edge = lane[cols]
        visc, over = CV[n, cols], DV[n, cols]
        AN[n, cols] = over * (visc + CV[n - 1, cols])
        AS[n, cols] = over * (visc + CV[n + 1, cols])
        AW[n, cols] = over * (visc + roll(visc, 2, 0))
        AE[n, cols] = over * (visc + roll(visc, -2, 0))
        AD[n, cols] = jnp.where(edge < 2, 0.0, over * (visc + roll(visc, 2, 1)))
        AU[n, cols] = jnp.where(edge >= 126, 0.0, over * (visc + roll(visc, -2, 1)))

    for turn in range(1, COARSE):
        old = Q if turn == 1 else E.at[turn % 2]
        new = E.at[(turn + 1) % 2]
        for n in range(turn, 22 - turn):
            cols = span(7 - turn - far(n))
            here = old[n, cols]
            total = Q[n, cols] + (1.0 - RELAX) * here
            total = total + AN[n, cols] * old[n - 1, cols]
            total = total + AS[n, cols] * old[n + 1, cols]
            total = total + AW[n, cols] * roll(here, 2, 0)
            total = total + AE[n, cols] * roll(here, -2, 0)
            total = total + AD[n, cols] * roll(here, 2, 1)
            new[n, cols] = total + AU[n, cols] * roll(here, -2, 1)

    final = E.at[COARSE % 2]
    tile = (8, 128)
    lane8, row8 = lanes_of(tile), rows_of(tile)
    odd_lane8, odd_row8 = (lane8 & 1) == 1, (row8 & 1) == 1
    for k in range(8):
        value = final[7 + k, 16:24]
        for comp in range(3):
            error = spread(value, comp, odd_lane8, odd_row8)
            for r in (2 * k, 2 * k + 1):
                out_ref[comp, r] = smooth_ref[comp, r] + error


def wanted_cells(lats, lons, lon):
    dest = jnp.arange(lats, dtype=jnp.int32)[:, None]
    position = jnp.arange(CELLS, dtype=jnp.int32)[None, :]
    rows, cols = lats * 16, lons * 8
    edge = (lon == 0) | (lon == lons - 1)
    side_row = dest * 16 + position - 4
    on_side = edge & (position < 24) & (side_row >= 0) & (side_row < rows)
    side = 2 * cols + jnp.where(lon == 0, 0, rows) + jnp.clip(side_row, 0, rows - 1)
    along = jnp.where((dest == 0) & (position < 4), position, position - 20)
    corner_col = jnp.where(lon == 0, along, lon * 8 + along - 4)
    col = jnp.where(edge, corner_col, lon * 8 + position - 4)
    row_cell = jnp.where(dest == 0, 0, cols) + jnp.clip(col, 0, cols - 1)
    return jnp.where(on_side, side, row_cell)


def per_device(velocity, forcing, viscosity, ghost_slots, corner_rows, corner_cols, corner_weights):
    v, f, mu = velocity[0], forcing[0], viscosity[0]
    lats, lons = lax.axis_size("lat"), lax.axis_size("lon")
    params = pltpu.CompilerParams(vmem_limit_bytes=32 * 2**20)
    f32 = jnp.float32
    place = jnp.stack(
        [lax.axis_index("lat"), lax.axis_index("lon"), jnp.int32(lats - 1), jnp.int32(lons - 1)]
    ).astype(jnp.int32)
    slots = ghost_slots[0]
    source_rows = ((slots // 3) % lons) * 9 + (slots % 3) * 3
    ghost_rows = (slots // (3 * lons)) * (3 * CELLS)
    cells = wanted_cells(lats, lons, lax.axis_index("lon")).reshape(-1)

    def kernel(body, shapes, specs):
        return pl.pallas_call(
            body,
            out_shape=[jax.ShapeDtypeStruct(shape, f32) for shape in shapes],
            in_specs=specs,
            out_specs=[VMEM] * len(shapes),
            compiler_params=params,
        )

    edge, first_row, first_cell = kernel(
        first_kernel, ((3, 16, 128), (3, 8, 128), (3, 128)), [VMEM]
    )(v)
    edge = shifted(edge, 0, -1)
    first_cell = shifted(first_cell, -1, -1)
    first_row = shifted(first_row, -1, 0)
    to_right, to_left = kernel(cut_kernel, ((64, 8, 128),) * 2, [VMEM] * 3)(v, f, mu)
    left = shifted(to_right, 0, 1)
    right = shifted(to_left, 0, -1)
    blended = kernel(
        blend_kernel, ((9, 1, 128), (3, 16, 128), (3, 8, 128), (3, 1, 128)), [SMEM] * 3 + [VMEM]
    )(corner_rows[0, 0], corner_cols[0, 0], corner_weights[0, 0], v)
    (values,) = kernel(interp_kernel, ((9 * lons, 1, 128),), [VMEM] * 7)(
        *blended, edge, first_row, first_cell
    )
    values = lax.ppermute(values.reshape(lons, 1, 1152), "patch", [(0, 1), (1, 0)])
    around = lax.all_to_all(values, "lon", 0, 0, tiled=True)
    to_above, to_below = kernel(pack_kernel, ((57, 8, 128),) * 2, [VMEM] * 5)(v, f, mu, left, right)
    below = shifted(to_above, -1, 0)
    above = shifted(to_below, 1, 0)

    chosen = pl.pallas_call(
        pick_kernel,
        out_shape=jax.ShapeDtypeStruct((lats * 3 * CELLS, 1, 128), f32),
        in_specs=[SMEM, SMEM, SMEM, VMEM],
        out_specs=VMEM,
        compiler_params=params,
        name="pick",
    )(place, cells, source_rows, around.reshape(lons * 9, 1, 128))
    everything = lax.all_to_all(chosen.reshape(lats, 3 * CELLS, 128), "lat", 0, 0, tiled=True)
    everything = everything.reshape(lats * 3 * CELLS, 1, 128)

    block = jax.ShapeDtypeStruct((3, 16, 8, 128), f32)
    field = (3, 28, 24, 128)
    residual, smoothed, message = pl.pallas_call(
        smooth_kernel,
        out_shape=(block, block, jax.ShapeDtypeStruct((10, 8, 128), f32)),
        in_specs=[SMEM, SMEM] + [VMEM] * 8,
        out_specs=(VMEM, VMEM, VMEM),
        scratch_shapes=[pltpu.VMEM(field, f32)] * 3
        + [
            pltpu.VMEM(shape, f32)
            for shape in ((6, 28, 24, 128), (16, 8, 128), (8, 8, 128), (8, 8, 128), (28, 24, 128))
        ],
        compiler_params=params,
        name="smooth",
    )(place, ghost_rows, v, f, mu, left, right, above, below, everything)

    tiles = [
        shifted(message, 0, 2),
        shifted(message, 0, 1),
        message,
        shifted(message, 0, -1),
        shifted(message, 0, -2),
    ]
    band = jnp.concatenate(tiles, axis=1)
    tile_list = (-1, 8, 128)
    inverse = band[8:10].reshape(tile_list)
    to_above = [band[0:2].reshape(tile_list), band[2:7, 8:32].reshape(tile_list), inverse]
    to_below = [band[7:8], band[6:7]] + [band[r : r + 1, 8:32] for r in (5, 4, 3, 2, 1)]
    to_below = [part.reshape(tile_list) for part in to_below] + [inverse]
    band_below = shifted(jnp.concatenate(to_above, axis=0), -1, 0)
    band_above = shifted(jnp.concatenate(to_below, axis=0), 1, 0)
    coarse = pltpu.VMEM((22, 40, 128), f32)
    new = pl.pallas_call(
        coarse_kernel,
        out_shape=block,
        in_specs=[VMEM] * 4,
        out_specs=VMEM,
        scratch_shapes=[coarse, coarse, coarse, pltpu.VMEM((2, 22, 40, 128), f32)] + [coarse] * 6,
        compiler_params=params,
        name="coarse",
    )(band, band_above, band_below, smoothed)
    return new[None], residual[None]


def solution(mesh):
    placed = (
        P("patch", None, "lat", "lon", None),
        P("patch", None, "lat", "lon", None),
        P("patch", "lat", "lon", None),
        P("patch", None),
        P("patch", "lat", "lon"),
        P("patch", "lat", "lon"),
        P("patch", "lat", None, "lon"),
    )
    return jax.shard_map(
        per_device,
        mesh=mesh,
        in_specs=placed,
        out_specs=(P("patch", None, "lat", "lon", None), P("patch", None, "lat", "lon", None)),
        check_vma=False,
    )
```

```python
import jax
import jax.numpy as jnp
from jax import lax
from jax.experimental import pallas as pl
from jax.experimental.pallas import tpu as pltpu
from jax.sharding import PartitionSpec as P


AXES = ("patch", "lat", "lon")
RELAX = 0.8
COARSE = 8
PAD = 6
CELLS = 32
VMEM = pl.BlockSpec(memory_space=pltpu.VMEM)
SMEM = pl.BlockSpec(memory_space=pltpu.SMEM)


def shifted(value, by_lat, by_lon):
    patches, lats, lons = (lax.axis_size(axis) for axis in AXES)
    pairs = []
    for p in range(patches):
        for a in range(lats):
            for b in range(lons):
                a2, b2 = a + by_lat, b + by_lon
                if 0 <= a2 < lats and 0 <= b2 < lons:
                    pairs.append(((p * lats + a) * lons + b, (p * lats + a2) * lons + b2))
    return lax.ppermute(value, AXES, pairs)


def lanes_of(shape):
    return lax.broadcasted_iota(jnp.int32, shape, len(shape) - 1)


def rows_of(shape):
    return lax.broadcasted_iota(jnp.int32, shape, len(shape) - 2)


def roll(value, by, axis):
    return pltpu.roll(value, by % value.shape[axis], axis)


def lane_partner(value, odd_lane):
    return jnp.where(odd_lane, roll(value, 1, 1), roll(value, -1, 1))


def row_partner(value, odd_row):
    return jnp.where(odd_row, roll(value, 1, 0), roll(value, -1, 0))


def first_kernel(v_ref, edge_ref, below_ref, corner_ref):
    sub = rows_of((8, 128))
    for comp in range(3):
        corner_ref[comp : comp + 1] = v_ref[comp, 0, 0:1]
        below_ref[comp] = v_ref[comp, 0]
        for j in range(2):
            first = v_ref[comp, 8 * j]
            for r in range(1, 8):
                first = jnp.where(sub == r, roll(v_ref[comp, 8 * j + r], r, 0), first)
            edge_ref[comp, 8 * j : 8 * j + 8] = first


def lat_tile(field, away):
    if 3 <= field < 6:
        return 20 + 4 * (field - 3) + away - 1
    return 5 * min(field, 3) + away - 1


def cut_kernel(v_ref, f_ref, mu_ref, up_ref, down_ref):
    for field in range(7):
        for away in range(1, 5 if 3 <= field < 6 else 6):
            for ref, r in ((up_ref, away - 1), (down_ref, 16 - away)):
                if field == 6:
                    value = mu_ref[r]
                else:
                    value = v_ref[field, r] if field < 3 else f_ref[field - 3, r]
                ref[lat_tile(field, away)] = value


def blend_kernel(rows_ref, cols_ref, weights_ref, v_ref, own_ref, edge_ref, below_ref, corner_ref):
    tall, flat = rows_of((16, 128)), rows_of((8, 128))
    for slot in range(3):
        row, col = rows_ref[slot], cols_ref[slot]
        w0, w1, w2, w3 = (weights_ref[k, slot] for k in range(4))
        here, next_one = flat == col, flat == col + 1
        upper = jnp.where(here, w0, jnp.where(next_one, w2, 0.0))
        lower = jnp.where(here, w1, jnp.where(next_one, w3, 0.0))
        within = row < 15
        next_row = jnp.where(within, row + 1, row)
        inner = jnp.where(within, lower, 0.0)
        for comp in range(3):
            total = upper * v_ref[comp, row] + inner * v_ref[comp, next_row]
            own_ref[3 * slot + comp] = jnp.sum(total, axis=0, keepdims=True)
        beside = jnp.where(tall == row, w2, jnp.where(tall == row + 1, w3, 0.0))
        edge_ref[slot] = jnp.where(col == 7, beside, 0.0)
        below_ref[slot] = jnp.where(within, 0.0, lower)
        both = jnp.where((row == 15) & (col == 7), w3, 0.0)
        corner_ref[slot] = jnp.full((1, 128), both, jnp.float32)


def interp_kernel(
    own_ref, edge_w, below_w, corner_w, edge_ref, below_ref, corner_ref, out_ref
):
    for slot in range(3):
        for comp in range(3):
            beside = edge_w[slot] * edge_ref[comp]
            total = beside[0:8] + beside[8:16] + below_w[slot] * below_ref[comp]
            total = jnp.sum(total, axis=0, keepdims=True) + own_ref[3 * slot + comp]
            total = total + corner_w[slot] * corner_ref[comp : comp + 1]
            for dest in range(out_ref.shape[0] // 9):
                out_ref[9 * dest + 3 * slot + comp] = total


def pick_kernel(place_ref, cells_ref, source_ref, row_ref, out_ref):
    lon, last_lat, last_lon = place_ref[1], place_ref[2], place_ref[3]
    edge = (lon == 0) | (lon == last_lon)

    def copy(dest, position):
        base = source_ref[cells_ref[dest * CELLS + position]]
        for comp in range(3):
            out_ref[dest * 3 * CELLS + position * 3 + comp] = row_ref[base + comp]

    @pl.when(edge)
    def _():
        def step(dest, carry):
            for position in range(CELLS):
                copy(dest, position)
            return carry

        lax.fori_loop(0, last_lat + 1, step, 0)

    @pl.when(~edge)
    def _():
        for position in range(16):
            copy(0, position)
            copy(last_lat, position)


def side_tile(ref, field, r, col, sub):
    value = ref[12 * field + (r + 4) // 2]
    if r % 2:
        value = roll(value, 4, 0)
    extra = {0: 0, 1: 1, 2: 2, 6: 3}.get(field)
    if extra is None or not 0 <= r < 16:
        return value
    fifth = roll(ref[84 + 2 * extra + r // 8], col - r % 8, 0)
    return jnp.where(sub == col, fifth, value)


def pack_kernel(v_ref, f_ref, mu_ref, above_ref, below_ref, right_ref, left_ref):
    sub = rows_of((8, 128))

    def row(field, r):
        if r < 0:
            return above_ref[lat_tile(field, -r)]
        if r > 15:
            return below_ref[lat_tile(field, r - 15)]
        if field == 6:
            return mu_ref[r]
        return v_ref[field, r] if field < 3 else f_ref[field - 3, r]

    for field in range(7):
        for t in range(12):
            even, odd = row(field, 2 * t - 4), roll(row(field, 2 * t - 3), 4, 0)
            right_ref[12 * field + t] = jnp.where(sub < 4, odd, even)
            left_ref[12 * field + t] = jnp.where(sub < 4, even, odd)
    for n, field in enumerate((0, 1, 2, 6)):
        for j in range(2):
            third = fourth = row(field, 8 * j)
            for r in range(8):
                value = row(field, 8 * j + r)
                third = jnp.where(sub == r, roll(value, r - 3, 0), third)
                fourth = jnp.where(sub == r, roll(value, r - 4, 0), fourth)
            right_ref[84 + 2 * n + j] = third
            left_ref[84 + 2 * n + j] = fourth


def prepare(
    place_ref, f_ref, mu_ref, left_ref, right_ref, above_ref, below_ref,
    F, C, DG, over_ref, visc_ref, MU,
):
    lat, lon = place_ref[0], place_ref[1]
    last_lat, last_lon = place_ref[2], place_ref[3]
    wide = (24, 128)
    lane, row = lanes_of(wide), rows_of(wide)
    odd_lane, odd_row = (lane & 1) == 1, (row & 1) == 1
    own = slice(PAD, PAD + 16)
    sub = rows_of((8, 128))
    MU[own, 8:16] = mu_ref[...]
    for r in range(-4, 20):
        MU[r + PAD, 0:8] = side_tile(left_ref, 6, r, 3, sub)
        MU[r + PAD, 16:24] = side_tile(right_ref, 6, r, 4, sub)
    for away in range(1, 6):
        for i, ref in ((PAD - away, above_ref), (PAD + 15 + away, below_ref)):
            value = ref[lat_tile(6, away)]
            MU[i, 8:16] = value
            if away == 5:
                MU[i, 0:8] = MU[i, 16:24] = value

    @pl.when(lat == 0)
    def _():
        MU[4] = MU[6]
        MU[5] = MU[6]

    @pl.when(lat == last_lat)
    def _():
        MU[22] = MU[21]
        MU[23] = MU[21]

    @pl.when(lon == 0)
    def _():
        for i in range(1, 27):
            MU[i, 0:8] = jnp.broadcast_to(MU[i, 8:9], (8, 128))

    @pl.when(lon == last_lon)
    def _():
        for i in range(1, 27):
            MU[i, 16:24] = jnp.broadcast_to(MU[i, 15:16], (8, 128))

    for i in range(2, 26):
        mid = MU[i]
        north = 0.5 * (mid + MU[i - 1])
        south = 0.5 * (mid + MU[i + 1])
        west = 0.5 * (mid + roll(mid, 1, 0))
        east = 0.5 * (mid + roll(mid, -1, 0))
        down = 0.5 * (mid + jnp.where(lane == 0, mid, roll(mid, 1, 1)))
        up = 0.5 * (mid + jnp.where(lane == 127, mid, roll(mid, -1, 1)))
        total = north + south + west + east + down + up
        inverse = 1.0 / total
        C[0, i] = north * inverse
        C[1, i] = south * inverse
        C[2, i] = west * inverse
        C[3, i] = east * inverse
        C[4, i] = jnp.where(lane == 0, 0.0, down * inverse)
        C[5, i] = jnp.where(lane == 127, 0.0, up * inverse)
        r = i - PAD
        if 0 <= r < 16:
            DG[r] = total[8:16]
        for comp in range(3):
            if 0 <= r < 16:
                force = f_ref[comp, r]
            else:
                ref, away = (above_ref, -r) if r < 0 else (below_ref, r - 15)
                force = ref[lat_tile(3 + comp, away)]
            F[comp, i, 0:8] = side_tile(left_ref, 3 + comp, r, 3, sub) * inverse[0:8]
            F[comp, i, 8:16] = force * inverse[8:16]
            F[comp, i, 16:24] = side_tile(right_ref, 3 + comp, r, 4, sub) * inverse[16:24]

    def coarse_visc(i):
        both = MU[i] + MU[i + 1]
        flat = 0.25 * (both + row_partner(both, odd_row))
        return flat, 0.5 * (flat + lane_partner(flat, odd_lane))

    layers = [coarse_visc(PAD + 2 * k) for k in (-1, 0)]
    for k in range(8):
        layers.append(coarse_visc(PAD + 2 * k + 2))
        before, (flat, visc), after = layers[k][1], layers[k + 1], layers[k + 2][1]
        edge_down = jnp.where(lane == 0, flat, roll(flat, 1, 1))
        edge_up = jnp.where(lane == 127, flat, roll(flat, -1, 1))
        total = 6.0 * visc + before + after + roll(visc, 2, 0) + roll(visc, -2, 0)
        total = total + jnp.where(lane < 2, edge_down, roll(visc, 2, 1))
        total = total + jnp.where(lane >= 126, edge_up, roll(visc, -2, 1))
        over_ref[k] = RELAX / (0.125 * total[8:16])
        visc_ref[k] = visc[8:16]


def smooth_kernel(
    place_ref, ghost_ref, v_ref, f_ref, mu_ref, left_ref, right_ref, above_ref, below_ref, slot_ref,
    res_ref, smooth_ref, message_ref, A, B, F, C, DG, over_ref, visc_ref, MU,
):
    lat, lon = place_ref[0], place_ref[1]
    last_lat, last_lon = place_ref[2], place_ref[3]
    wide = (24, 128)
    lane, row = lanes_of(wide), rows_of(wide)
    sub = rows_of((8, 128))
    own = slice(PAD, PAD + 16)

    for comp in range(3):
        A[comp, own, 8:16] = v_ref[comp]
        for r in range(-4, 20):
            A[comp, r + PAD, 0:8] = side_tile(left_ref, comp, r, 3, sub)
            A[comp, r + PAD, 16:24] = side_tile(right_ref, comp, r, 4, sub)
        for away in range(1, 6):
            for i, ref in ((PAD - away, above_ref), (PAD + 15 + away, below_ref)):
                value = ref[lat_tile(comp, away)]
                A[comp, i, 8:16] = value
                if away == 5:
                    A[comp, i, 0:8] = A[comp, i, 16:24] = value

    edge = (lon == 0) | (lon == last_lon)
    all_cols, all_rows = (last_lon + 1) * 8, (last_lat + 1) * 16

    def fill_row(i, start):
        for col in range(-4, 12):
            along = jnp.where(lon == 0, col, col + 4)
            packed_at = jnp.where((lat == 0) & (along < 4), along, along + 20)
            position = jnp.clip(jnp.where(edge, packed_at, col + 4), 0, CELLS - 1)
            cell = start + jnp.clip(lon * 8 + col, 0, all_cols - 1)
            base = ghost_ref[cell] + 3 * position
            for comp in range(3):
                A[comp, i, 8 + col : 9 + col] = slot_ref[base + comp]

    def fill_side(col, start):
        for r in range(-4, 20):
            base = ghost_ref[start + jnp.clip(lat * 16 + r, 0, all_rows - 1)] + 3 * (r + 4)
            for comp in range(3):
                A[comp, r + PAD, 8 + col : 9 + col] = slot_ref[base + comp]

    prepare(
        place_ref, f_ref, mu_ref, left_ref, right_ref, above_ref, below_ref,
        F, C, DG, over_ref, visc_ref, MU,
    )
    pl.when(lat == 0)(lambda: fill_row(5, 0))
    pl.when(lat == last_lat)(lambda: fill_row(22, all_cols))
    pl.when(lon == 0)(lambda: fill_side(-1, 2 * all_cols))
    pl.when(lon == last_lon)(lambda: fill_side(8, 2 * all_cols + all_rows))

    inside = ((row >= 8) | (lon > 0)) & ((row < 16) | (lon < last_lon))
    parity = jnp.where(inside, (row + lane) & 1, 2)

    def weighted(source, comp, i, here):
        total = F[comp, i] + C[0, i] * source[comp, i - 1]
        total = total + C[1, i] * source[comp, i + 1]
        total = total + C[2, i] * roll(here, 1, 0)
        total = total + C[3, i] * roll(here, -1, 0)
        total = total + C[4, i] * roll(here, 1, 1)
        return total + C[5, i] * roll(here, -1, 1)

    wanted = {}
    for colour in range(2):
        wanted[colour, "mid"] = jnp.int32(colour)
        wanted[colour, "top"] = jnp.where(lat == 0, 3, colour)
        wanted[colour, "low"] = jnp.where(lat == last_lat, 3, colour)

    def relax(colour, reach, source, target):
        for r in range(-reach, 16 + reach):
            i = r + PAD
            zone = "top" if r < 0 else "low" if r > 15 else "mid"
            mask = parity == wanted[(colour + r) % 2, zone]
            for comp in range(3):
                here = source[comp, i]
                target[comp, i] = jnp.where(mask, weighted(source, comp, i, here), here)

    relax(0, 4, A, B)
    relax(1, 3, B, A)
    relax(0, 2, A, B)
    relax(1, 1, B, A)

    tile = (8, 128)
    lane8, row8 = lanes_of(tile), rows_of(tile)
    odd_lane8, odd_row8 = (lane8 & 1) == 1, (row8 & 1) == 1

    def packed(parts):
        low = jnp.where(odd_lane8, parts[1], parts[0])
        high = jnp.where(odd_lane8, parts[3], parts[2])
        return jnp.where(odd_row8, high, low)

    for k in range(8):
        parts = []
        for comp in range(3):
            rhs = jnp.zeros(tile, jnp.float32)
            for r in (2 * k, 2 * k + 1):
                here = A[comp, r + PAD]
                smooth_ref[comp, r] = here[8:16]
                left = DG[r] * (weighted(A, comp, r + PAD, here) - here)[8:16]
                res_ref[comp, r] = left
                rhs = rhs + left
            rhs = rhs + lane_partner(rhs, odd_lane8)
            rhs = rhs + row_partner(rhs, odd_row8)
            parts.append(0.125 * rhs * over_ref[k])
        message_ref[k] = packed(parts + [visc_ref[k]])
        if k % 4 == 3:
            message_ref[8 + k // 4] = packed([over_ref[j] for j in range(k - 3, k + 1)])


def coarse_kernel(
    mid_ref, above_ref, below_ref, smooth_ref, out_ref, Q, CV, DV, E, AN, AS, AW, AE, AD, AU
):
    wide = (40, 128)
    lane, row = lanes_of(wide), rows_of(wide)
    odd_lane, odd_row = (lane & 1) == 1, (row & 1) == 1

    def spread(value, part, odd_l, odd_r):
        keep = odd_l if part % 2 else ~odd_l
        value = jnp.where(keep, value, roll(value, -1 if part % 2 else 1, 1))
        keep = odd_r if part // 2 else ~odd_r
        return jnp.where(keep, value, roll(value, -1 if part // 2 else 1, 0))

    def far(n):
        return max(0, 7 - n, n - 14)

    for n in range(22):
        away = far(n)
        if away == 0:
            t = n - 7
            Q[n] = mid_ref[t]
            cols, over = slice(0, 40), mid_ref[8 + t // 4]
        else:
            ref, t = (above_ref, n + 1) if n < 7 else (below_ref, n - 15)
            tiles = range(5) if away < 3 else range(1, 4)
            first = 5 * (away - 1) if away < 3 else 10 + 3 * (away - 3) - 1
            for j in tiles:
                Q[n, 8 * j : 8 * j + 8] = ref[first + j]
            cols = slice(8 * tiles[0], 8 * tiles[-1] + 8)
            over = [ref[25 + 5 * (t // 4) + j] for j in tiles]
            over = jnp.concatenate(over, axis=0)
        CV[n, cols] = spread(Q[n, cols], 3, odd_lane[cols], odd_row[cols])
        DV[n, cols] = 0.125 * spread(over, t % 4, odd_lane[cols], odd_row[cols])

    def span(reach):
        return slice(0, 40) if reach > 3 else slice(8, 32)

    for n in range(1, 21):
        cols = span(6 - far(n))
        edge = lane[cols]
        visc, over = CV[n, cols], DV[n, cols]
        AN[n, cols] = over * (visc + CV[n - 1, cols])
        AS[n, cols] = over * (visc + CV[n + 1, cols])
        AW[n, cols] = over * (visc + roll(visc, 2, 0))
        AE[n, cols] = over * (visc + roll(visc, -2, 0))
        AD[n, cols] = jnp.where(edge < 2, 0.0, over * (visc + roll(visc, 2, 1)))
        AU[n, cols] = jnp.where(edge >= 126, 0.0, over * (visc + roll(visc, -2, 1)))

    for turn in range(1, COARSE):
        old = Q if turn == 1 else E.at[turn % 2]
        new = E.at[(turn + 1) % 2]
        for n in range(turn, 22 - turn):
            cols = span(7 - turn - far(n))
            here = old[n, cols]
            total = Q[n, cols] + (1.0 - RELAX) * here
            total = total + AN[n, cols] * old[n - 1, cols]
            total = total + AS[n, cols] * old[n + 1, cols]
            total = total + AW[n, cols] * roll(here, 2, 0)
            total = total + AE[n, cols] * roll(here, -2, 0)
            total = total + AD[n, cols] * roll(here, 2, 1)
            new[n, cols] = total + AU[n, cols] * roll(here, -2, 1)

    final = E.at[COARSE % 2]
    tile = (8, 128)
    lane8, row8 = lanes_of(tile), rows_of(tile)
    odd_lane8, odd_row8 = (lane8 & 1) == 1, (row8 & 1) == 1
    for k in range(8):
        value = final[7 + k, 16:24]
        for comp in range(3):
            error = spread(value, comp, odd_lane8, odd_row8)
            for r in (2 * k, 2 * k + 1):
                out_ref[comp, r] = smooth_ref[comp, r] + error


def wanted_cells(lats, lons, lon):
    dest = jnp.arange(lats, dtype=jnp.int32)[:, None]
    position = jnp.arange(CELLS, dtype=jnp.int32)[None, :]
    rows, cols = lats * 16, lons * 8
    edge = (lon == 0) | (lon == lons - 1)
    side_row = dest * 16 + position - 4
    on_side = edge & (position < 24) & (side_row >= 0) & (side_row < rows)
    side = 2 * cols + jnp.where(lon == 0, 0, rows) + jnp.clip(side_row, 0, rows - 1)
    along = jnp.where((dest == 0) & (position < 4), position, position - 20)
    corner_col = jnp.where(lon == 0, along, lon * 8 + along - 4)
    col = jnp.where(edge, corner_col, lon * 8 + position - 4)
    row_cell = jnp.where(dest == 0, 0, cols) + jnp.clip(col, 0, cols - 1)
    return jnp.where(on_side, side, row_cell)


def per_device(velocity, forcing, viscosity, ghost_slots, corner_rows, corner_cols, corner_weights):
    v, f, mu = velocity[0], forcing[0], viscosity[0]
    lats, lons = lax.axis_size("lat"), lax.axis_size("lon")
    params = pltpu.CompilerParams(vmem_limit_bytes=32 * 2**20)
    f32 = jnp.float32
    place = jnp.stack(
        [lax.axis_index("lat"), lax.axis_index("lon"), jnp.int32(lats - 1), jnp.int32(lons - 1)]
    ).astype(jnp.int32)
    slots = ghost_slots[0]
    source_rows = ((slots // 3) % lons) * 9 + (slots % 3) * 3
    ghost_rows = (slots // (3 * lons)) * (3 * CELLS)
    cells = wanted_cells(lats, lons, lax.axis_index("lon")).reshape(-1)

    def kernel(body, shapes, specs):
        return pl.pallas_call(
            body,
            out_shape=[jax.ShapeDtypeStruct(shape, f32) for shape in shapes],
            in_specs=specs,
            out_specs=[VMEM] * len(shapes),
            compiler_params=params,
        )

    edge, first_row, first_cell = kernel(
        first_kernel, ((3, 16, 128), (3, 8, 128), (3, 128)), [VMEM]
    )(v)
    edge = shifted(edge, 0, -1)
    first_cell = shifted(first_cell, -1, -1)
    first_row = shifted(first_row, -1, 0)
    blended = kernel(
        blend_kernel, ((9, 1, 128), (3, 16, 128), (3, 8, 128), (3, 1, 128)), [SMEM] * 3 + [VMEM]
    )(corner_rows[0, 0], corner_cols[0, 0], corner_weights[0, 0], v)
    (values,) = kernel(interp_kernel, ((9 * lons, 1, 128),), [VMEM] * 7)(
        *blended, edge, first_row, first_cell
    )
    values = lax.ppermute(values.reshape(lons, 1, 1152), "patch", [(0, 1), (1, 0)])
    around = lax.all_to_all(values, "lon", 0, 0, tiled=True)
    to_above, to_below = kernel(cut_kernel, ((32, 8, 128),) * 2, [VMEM] * 3)(v, f, mu)
    below = shifted(to_above, -1, 0)
    above = shifted(to_below, 1, 0)

    chosen = pl.pallas_call(
        pick_kernel,
        out_shape=jax.ShapeDtypeStruct((lats * 3 * CELLS, 1, 128), f32),
        in_specs=[SMEM, SMEM, SMEM, VMEM],
        out_specs=VMEM,
        compiler_params=params,
        name="pick",
    )(place, cells, source_rows, around.reshape(lons * 9, 1, 128))
    everything = lax.all_to_all(chosen.reshape(lats, 3 * CELLS, 128), "lat", 0, 0, tiled=True)
    everything = everything.reshape(lats * 3 * CELLS, 1, 128)
    to_right, to_left = kernel(pack_kernel, ((92, 8, 128),) * 2, [VMEM] * 5)(v, f, mu, above, below)
    left = shifted(to_right, 0, 1)
    right = shifted(to_left, 0, -1)

    block = jax.ShapeDtypeStruct((3, 16, 8, 128), f32)
    field = (3, 28, 24, 128)
    residual, smoothed, message = pl.pallas_call(
        smooth_kernel,
        out_shape=(block, block, jax.ShapeDtypeStruct((10, 8, 128), f32)),
        in_specs=[SMEM, SMEM] + [VMEM] * 8,
        out_specs=(VMEM, VMEM, VMEM),
        scratch_shapes=[pltpu.VMEM(field, f32)] * 3
        + [
            pltpu.VMEM(shape, f32)
            for shape in ((6, 28, 24, 128), (16, 8, 128), (8, 8, 128), (8, 8, 128), (28, 24, 128))
        ],
        compiler_params=params,
        name="smooth",
    )(place, ghost_rows, v, f, mu, left, right, above, below, everything)

    tiles = [
        shifted(message, 0, 2),
        shifted(message, 0, 1),
        message,
        shifted(message, 0, -1),
        shifted(message, 0, -2),
    ]
    band = jnp.concatenate(tiles, axis=1)
    tile_list = (-1, 8, 128)
    inverse = band[8:10].reshape(tile_list)
    to_above = [band[0:2].reshape(tile_list), band[2:7, 8:32].reshape(tile_list), inverse]
    to_below = [band[7:8], band[6:7]] + [band[r : r + 1, 8:32] for r in (5, 4, 3, 2, 1)]
    to_below = [part.reshape(tile_list) for part in to_below] + [inverse]
    band_below = shifted(jnp.concatenate(to_above, axis=0), -1, 0)
    band_above = shifted(jnp.concatenate(to_below, axis=0), 1, 0)
    coarse = pltpu.VMEM((22, 40, 128), f32)
    new = pl.pallas_call(
        coarse_kernel,
        out_shape=block,
        in_specs=[VMEM] * 4,
        out_specs=VMEM,
        scratch_shapes=[coarse, coarse, coarse, pltpu.VMEM((2, 22, 40, 128), f32)] + [coarse] * 6,
        compiler_params=params,
        name="coarse",
    )(band, band_above, band_below, smoothed)
    return new[None], residual[None]


def solution(mesh):
    placed = (
        P("patch", None, "lat", "lon", None),
        P("patch", None, "lat", "lon", None),
        P("patch", "lat", "lon", None),
        P("patch", None),
        P("patch", "lat", "lon"),
        P("patch", "lat", "lon"),
        P("patch", "lat", None, "lon"),
    )
    return jax.shard_map(
        per_device,
        mesh=mesh,
        in_specs=placed,
        out_specs=(P("patch", None, "lat", "lon", None), P("patch", None, "lat", "lon", None)),
        check_vma=False,
    )
```

```python
import jax
import jax.numpy as jnp
from jax import lax
from jax.experimental import pallas as pl
from jax.experimental.pallas import tpu as pltpu
from jax.sharding import PartitionSpec as P


AXES = ("patch", "lat", "lon")
RELAX = 0.8
COARSE = 8
PAD = 6
CELLS = 32
VMEM = pl.BlockSpec(memory_space=pltpu.VMEM)
SMEM = pl.BlockSpec(memory_space=pltpu.SMEM)


def shifted(value, by_lat, by_lon):
    patches, lats, lons = (lax.axis_size(axis) for axis in AXES)
    pairs = []
    for p in range(patches):
        for a in range(lats):
            for b in range(lons):
                a2, b2 = a + by_lat, b + by_lon
                if 0 <= a2 < lats and 0 <= b2 < lons:
                    pairs.append(((p * lats + a) * lons + b, (p * lats + a2) * lons + b2))
    return lax.ppermute(value, AXES, pairs)


def swap_pairs(value, axis, first):
    size = lax.axis_size(axis)
    pairs = []
    for i in range(first, size - 1, 2):
        pairs += [(i, i + 1), (i + 1, i)]
    return lax.ppermute(value, axis, pairs)


def exchange(axis, to_low, to_high):
    odd = lax.axis_index(axis) % 2 == 1
    one = swap_pairs(jnp.where(odd, to_low, to_high), axis, 0)
    two = swap_pairs(jnp.where(odd, to_high, to_low), axis, 1)
    return jnp.where(odd, one, two), jnp.where(odd, two, one)


def two_neighbours(axis, value):
    odd = lax.axis_index(axis) % 2 == 1
    one = swap_pairs(value, axis, 0)
    two = swap_pairs(jnp.concatenate([value, one], axis=0), axis, 1)
    near, far = jnp.split(two, 2, axis=0)
    three = swap_pairs(near, axis, 0)
    left = (jnp.where(odd, three, far), jnp.where(odd, one, near))
    right = (jnp.where(odd, near, one), jnp.where(odd, far, three))
    return left, right


def lanes_of(shape):
    return lax.broadcasted_iota(jnp.int32, shape, len(shape) - 1)


def rows_of(shape):
    return lax.broadcasted_iota(jnp.int32, shape, len(shape) - 2)


def roll(value, by, axis):
    return pltpu.roll(value, by % value.shape[axis], axis)


def lane_partner(value, odd_lane):
    return jnp.where(odd_lane, roll(value, 1, 1), roll(value, -1, 1))


def row_partner(value, odd_row):
    return jnp.where(odd_row, roll(value, 1, 0), roll(value, -1, 0))


def first_kernel(v_ref, edge_ref, below_ref, corner_ref):
    sub = rows_of((8, 128))
    for comp in range(3):
        corner_ref[comp : comp + 1] = v_ref[comp, 0, 0:1]
        below_ref[comp] = v_ref[comp, 0]
        for j in range(2):
            first = v_ref[comp, 8 * j]
            for r in range(1, 8):
                first = jnp.where(sub == r, roll(v_ref[comp, 8 * j + r], r, 0), first)
            edge_ref[comp, 8 * j : 8 * j + 8] = first


def lat_tile(field, away):
    if 3 <= field < 6:
        return 20 + 4 * (field - 3) + away - 1
    return 5 * min(field, 3) + away - 1


def cut_kernel(v_ref, f_ref, mu_ref, up_ref, down_ref):
    for field in range(7):
        for away in range(1, 5 if 3 <= field < 6 else 6):
            for ref, r in ((up_ref, away - 1), (down_ref, 16 - away)):
                if field == 6:
                    value = mu_ref[r]
                else:
                    value = v_ref[field, r] if field < 3 else f_ref[field - 3, r]
                ref[lat_tile(field, away)] = value


def blend_kernel(rows_ref, cols_ref, weights_ref, v_ref, own_ref, edge_ref, below_ref, corner_ref):
    tall, flat = rows_of((16, 128)), rows_of((8, 128))
    for slot in range(3):
        row, col = rows_ref[slot], cols_ref[slot]
        w0, w1, w2, w3 = (weights_ref[k, slot] for k in range(4))
        here, next_one = flat == col, flat == col + 1
        upper = jnp.where(here, w0, jnp.where(next_one, w2, 0.0))
        lower = jnp.where(here, w1, jnp.where(next_one, w3, 0.0))
        within = row < 15
        next_row = jnp.where(within, row + 1, row)
        inner = jnp.where(within, lower, 0.0)
        for comp in range(3):
            total = upper * v_ref[comp, row] + inner * v_ref[comp, next_row]
            own_ref[3 * slot + comp] = jnp.sum(total, axis=0, keepdims=True)
        beside = jnp.where(tall == row, w2, jnp.where(tall == row + 1, w3, 0.0))
        edge_ref[slot] = jnp.where(col == 7, beside, 0.0)
        below_ref[slot] = jnp.where(within, 0.0, lower)
        both = jnp.where((row == 15) & (col == 7), w3, 0.0)
        corner_ref[slot] = jnp.full((1, 128), both, jnp.float32)


def interp_kernel(
    own_ref, edge_w, below_w, corner_w, edge_ref, below_ref, corner_ref, out_ref
):
    for slot in range(3):
        for comp in range(3):
            beside = edge_w[slot] * edge_ref[comp]
            total = beside[0:8] + beside[8:16] + below_w[slot] * below_ref[comp]
            total = jnp.sum(total, axis=0, keepdims=True) + own_ref[3 * slot + comp]
            total = total + corner_w[slot] * corner_ref[comp : comp + 1]
            for dest in range(out_ref.shape[0] // 9):
                out_ref[9 * dest + 3 * slot + comp] = total


def pick_kernel(place_ref, cells_ref, source_ref, row_ref, out_ref):
    lon, last_lat, last_lon = place_ref[1], place_ref[2], place_ref[3]
    edge = (lon == 0) | (lon == last_lon)

    def copy(dest, position):
        base = source_ref[cells_ref[dest * CELLS + position]]
        for comp in range(3):
            out_ref[dest * 3 * CELLS + position * 3 + comp] = row_ref[base + comp]

    @pl.when(edge)
    def _():
        def step(dest, carry):
            for position in range(CELLS):
                copy(dest, position)
            return carry

        lax.fori_loop(0, last_lat + 1, step, 0)

    @pl.when(~edge)
    def _():
        for position in range(16):
            copy(0, position)
            copy(last_lat, position)


def side_tile(ref, field, r, col, sub):
    value = ref[12 * field + (r + 4) // 2]
    if r % 2:
        value = roll(value, 4, 0)
    extra = {0: 0, 1: 1, 2: 2, 6: 3}.get(field)
    if extra is None or not 0 <= r < 16:
        return value
    fifth = roll(ref[84 + 2 * extra + r // 8], col - r % 8, 0)
    return jnp.where(sub == col, fifth, value)


def pack_kernel(v_ref, f_ref, mu_ref, above_ref, below_ref, right_ref, left_ref):
    sub = rows_of((8, 128))

    def row(field, r):
        if r < 0:
            return above_ref[lat_tile(field, -r)]
        if r > 15:
            return below_ref[lat_tile(field, r - 15)]
        if field == 6:
            return mu_ref[r]
        return v_ref[field, r] if field < 3 else f_ref[field - 3, r]

    for field in range(7):
        for t in range(12):
            even, odd = row(field, 2 * t - 4), roll(row(field, 2 * t - 3), 4, 0)
            right_ref[12 * field + t] = jnp.where(sub < 4, odd, even)
            left_ref[12 * field + t] = jnp.where(sub < 4, even, odd)
    for n, field in enumerate((0, 1, 2, 6)):
        for j in range(2):
            third = fourth = row(field, 8 * j)
            for r in range(8):
                value = row(field, 8 * j + r)
                third = jnp.where(sub == r, roll(value, r - 3, 0), third)
                fourth = jnp.where(sub == r, roll(value, r - 4, 0), fourth)
            right_ref[84 + 2 * n + j] = third
            left_ref[84 + 2 * n + j] = fourth


def prepare(
    place_ref, f_ref, mu_ref, left_ref, right_ref, above_ref, below_ref,
    F, C, DG, over_ref, visc_ref, MU,
):
    lat, lon = place_ref[0], place_ref[1]
    last_lat, last_lon = place_ref[2], place_ref[3]
    wide = (24, 128)
    lane, row = lanes_of(wide), rows_of(wide)
    odd_lane, odd_row = (lane & 1) == 1, (row & 1) == 1
    own = slice(PAD, PAD + 16)
    sub = rows_of((8, 128))
    MU[own, 8:16] = mu_ref[...]
    for r in range(-4, 20):
        MU[r + PAD, 0:8] = side_tile(left_ref, 6, r, 3, sub)
        MU[r + PAD, 16:24] = side_tile(right_ref, 6, r, 4, sub)
    for away in range(1, 6):
        for i, ref in ((PAD - away, above_ref), (PAD + 15 + away, below_ref)):
            value = ref[lat_tile(6, away)]
            MU[i, 8:16] = value
            if away == 5:
                MU[i, 0:8] = MU[i, 16:24] = value

    @pl.when(lat == 0)
    def _():
        MU[4] = MU[6]
        MU[5] = MU[6]

    @pl.when(lat == last_lat)
    def _():
        MU[22] = MU[21]
        MU[23] = MU[21]

    @pl.when(lon == 0)
    def _():
        for i in range(1, 27):
            MU[i, 0:8] = jnp.broadcast_to(MU[i, 8:9], (8, 128))

    @pl.when(lon == last_lon)
    def _():
        for i in range(1, 27):
            MU[i, 16:24] = jnp.broadcast_to(MU[i, 15:16], (8, 128))

    for i in range(2, 26):
        mid = MU[i]
        north = 0.5 * (mid + MU[i - 1])
        south = 0.5 * (mid + MU[i + 1])
        west = 0.5 * (mid + roll(mid, 1, 0))
        east = 0.5 * (mid + roll(mid, -1, 0))
        down = 0.5 * (mid + jnp.where(lane == 0, mid, roll(mid, 1, 1)))
        up = 0.5 * (mid + jnp.where(lane == 127, mid, roll(mid, -1, 1)))
        total = north + south + west + east + down + up
        inverse = 1.0 / total
        C[0, i] = north * inverse
        C[1, i] = south * inverse
        C[2, i] = west * inverse
        C[3, i] = east * inverse
        C[4, i] = jnp.where(lane == 0, 0.0, down * inverse)
        C[5, i] = jnp.where(lane == 127, 0.0, up * inverse)
        r = i - PAD
        if 0 <= r < 16:
            DG[r] = total[8:16]
        for comp in range(3):
            if 0 <= r < 16:
                force = f_ref[comp, r]
            else:
                ref, away = (above_ref, -r) if r < 0 else (below_ref, r - 15)
                force = ref[lat_tile(3 + comp, away)]
            F[comp, i, 0:8] = side_tile(left_ref, 3 + comp, r, 3, sub) * inverse[0:8]
            F[comp, i, 8:16] = force * inverse[8:16]
            F[comp, i, 16:24] = side_tile(right_ref, 3 + comp, r, 4, sub) * inverse[16:24]

    def coarse_visc(i):
        both = MU[i] + MU[i + 1]
        flat = 0.25 * (both + row_partner(both, odd_row))
        return flat, 0.5 * (flat + lane_partner(flat, odd_lane))

    layers = [coarse_visc(PAD + 2 * k) for k in (-1, 0)]
    for k in range(8):
        layers.append(coarse_visc(PAD + 2 * k + 2))
        before, (flat, visc), after = layers[k][1], layers[k + 1], layers[k + 2][1]
        edge_down = jnp.where(lane == 0, flat, roll(flat, 1, 1))
        edge_up = jnp.where(lane == 127, flat, roll(flat, -1, 1))
        total = 6.0 * visc + before + after + roll(visc, 2, 0) + roll(visc, -2, 0)
        total = total + jnp.where(lane < 2, edge_down, roll(visc, 2, 1))
        total = total + jnp.where(lane >= 126, edge_up, roll(visc, -2, 1))
        over_ref[k] = RELAX / (0.125 * total[8:16])
        visc_ref[k] = visc[8:16]


def smooth_kernel(
    place_ref, ghost_ref, v_ref, f_ref, mu_ref, left_ref, right_ref, above_ref, below_ref, slot_ref,
    res_ref, smooth_ref, message_ref, A, B, F, C, DG, over_ref, visc_ref, MU,
):
    lat, lon = place_ref[0], place_ref[1]
    last_lat, last_lon = place_ref[2], place_ref[3]
    wide = (24, 128)
    lane, row = lanes_of(wide), rows_of(wide)
    sub = rows_of((8, 128))
    own = slice(PAD, PAD + 16)

    for comp in range(3):
        A[comp, own, 8:16] = v_ref[comp]
        for r in range(-4, 20):
            A[comp, r + PAD, 0:8] = side_tile(left_ref, comp, r, 3, sub)
            A[comp, r + PAD, 16:24] = side_tile(right_ref, comp, r, 4, sub)
        for away in range(1, 6):
            for i, ref in ((PAD - away, above_ref), (PAD + 15 + away, below_ref)):
                value = ref[lat_tile(comp, away)]
                A[comp, i, 8:16] = value
                if away == 5:
                    A[comp, i, 0:8] = A[comp, i, 16:24] = value

    edge = (lon == 0) | (lon == last_lon)
    all_cols, all_rows = (last_lon + 1) * 8, (last_lat + 1) * 16

    def fill_row(i, start):
        for col in range(-4, 12):
            along = jnp.where(lon == 0, col, col + 4)
            packed_at = jnp.where((lat == 0) & (along < 4), along, along + 20)
            position = jnp.clip(jnp.where(edge, packed_at, col + 4), 0, CELLS - 1)
            cell = start + jnp.clip(lon * 8 + col, 0, all_cols - 1)
            base = ghost_ref[cell] + 3 * position
            for comp in range(3):
                A[comp, i, 8 + col : 9 + col] = slot_ref[base + comp]

    def fill_side(col, start):
        for r in range(-4, 20):
            base = ghost_ref[start + jnp.clip(lat * 16 + r, 0, all_rows - 1)] + 3 * (r + 4)
            for comp in range(3):
                A[comp, r + PAD, 8 + col : 9 + col] = slot_ref[base + comp]

    prepare(
        place_ref, f_ref, mu_ref, left_ref, right_ref, above_ref, below_ref,
        F, C, DG, over_ref, visc_ref, MU,
    )
    pl.when(lat == 0)(lambda: fill_row(5, 0))
    pl.when(lat == last_lat)(lambda: fill_row(22, all_cols))
    pl.when(lon == 0)(lambda: fill_side(-1, 2 * all_cols))
    pl.when(lon == last_lon)(lambda: fill_side(8, 2 * all_cols + all_rows))

    inside = ((row >= 8) | (lon > 0)) & ((row < 16) | (lon < last_lon))
    parity = jnp.where(inside, (row + lane) & 1, 2)

    def weighted(source, comp, i, here):
        total = F[comp, i] + C[0, i] * source[comp, i - 1]
        total = total + C[1, i] * source[comp, i + 1]
        total = total + C[2, i] * roll(here, 1, 0)
        total = total + C[3, i] * roll(here, -1, 0)
        total = total + C[4, i] * roll(here, 1, 1)
        return total + C[5, i] * roll(here, -1, 1)

    wanted = {}
    for colour in range(2):
        wanted[colour, "mid"] = jnp.int32(colour)
        wanted[colour, "top"] = jnp.where(lat == 0, 3, colour)
        wanted[colour, "low"] = jnp.where(lat == last_lat, 3, colour)

    def relax(colour, reach, source, target):
        for r in range(-reach, 16 + reach):
            i = r + PAD
            zone = "top" if r < 0 else "low" if r > 15 else "mid"
            mask = parity == wanted[(colour + r) % 2, zone]
            for comp in range(3):
                here = source[comp, i]
                target[comp, i] = jnp.where(mask, weighted(source, comp, i, here), here)

    relax(0, 4, A, B)
    relax(1, 3, B, A)
    relax(0, 2, A, B)
    relax(1, 1, B, A)

    tile = (8, 128)
    lane8, row8 = lanes_of(tile), rows_of(tile)
    odd_lane8, odd_row8 = (lane8 & 1) == 1, (row8 & 1) == 1

    def packed(parts):
        low = jnp.where(odd_lane8, parts[1], parts[0])
        high = jnp.where(odd_lane8, parts[3], parts[2])
        return jnp.where(odd_row8, high, low)

    for k in range(8):
        parts = []
        for comp in range(3):
            rhs = jnp.zeros(tile, jnp.float32)
            for r in (2 * k, 2 * k + 1):
                here = A[comp, r + PAD]
                smooth_ref[comp, r] = here[8:16]
                left = DG[r] * (weighted(A, comp, r + PAD, here) - here)[8:16]
                res_ref[comp, r] = left
                rhs = rhs + left
            rhs = rhs + lane_partner(rhs, odd_lane8)
            rhs = rhs + row_partner(rhs, odd_row8)
            parts.append(0.125 * rhs * over_ref[k])
        message_ref[k] = packed(parts + [visc_ref[k]])
        if k % 4 == 3:
            message_ref[8 + k // 4] = packed([over_ref[j] for j in range(k - 3, k + 1)])


def coarse_kernel(
    mid_ref, above_ref, below_ref, smooth_ref, out_ref, Q, CV, DV, E, AN, AS, AW, AE, AD, AU
):
    wide = (40, 128)
    lane, row = lanes_of(wide), rows_of(wide)
    odd_lane, odd_row = (lane & 1) == 1, (row & 1) == 1

    def spread(value, part, odd_l, odd_r):
        keep = odd_l if part % 2 else ~odd_l
        value = jnp.where(keep, value, roll(value, -1 if part % 2 else 1, 1))
        keep = odd_r if part // 2 else ~odd_r
        return jnp.where(keep, value, roll(value, -1 if part // 2 else 1, 0))

    def far(n):
        return max(0, 7 - n, n - 14)

    for n in range(22):
        away = far(n)
        if away == 0:
            t = n - 7
            Q[n] = mid_ref[t]
            cols, over = slice(0, 40), mid_ref[8 + t // 4]
        else:
            ref, t = (above_ref, n + 1) if n < 7 else (below_ref, n - 15)
            tiles = range(5) if away < 3 else range(1, 4)
            first = 5 * (away - 1) if away < 3 else 10 + 3 * (away - 3) - 1
            for j in tiles:
                Q[n, 8 * j : 8 * j + 8] = ref[first + j]
            cols = slice(8 * tiles[0], 8 * tiles[-1] + 8)
            over = [ref[25 + 5 * (t // 4) + j] for j in tiles]
            over = jnp.concatenate(over, axis=0)
        CV[n, cols] = spread(Q[n, cols], 3, odd_lane[cols], odd_row[cols])
        DV[n, cols] = 0.125 * spread(over, t % 4, odd_lane[cols], odd_row[cols])

    def span(reach):
        return slice(0, 40) if reach > 3 else slice(8, 32)

    for n in range(1, 21):
        cols = span(6 - far(n))
        edge = lane[cols]
        visc, over = CV[n, cols], DV[n, cols]
        AN[n, cols] = over * (visc + CV[n - 1, cols])
        AS[n, cols] = over * (visc + CV[n + 1, cols])
        AW[n, cols] = over * (visc + roll(visc, 2, 0))
        AE[n, cols] = over * (visc + roll(visc, -2, 0))
        AD[n, cols] = jnp.where(edge < 2, 0.0, over * (visc + roll(visc, 2, 1)))
        AU[n, cols] = jnp.where(edge >= 126, 0.0, over * (visc + roll(visc, -2, 1)))

    for turn in range(1, COARSE):
        old = Q if turn == 1 else E.at[turn % 2]
        new = E.at[(turn + 1) % 2]
        for n in range(turn, 22 - turn):
            cols = span(7 - turn - far(n))
            here = old[n, cols]
            total = Q[n, cols] + (1.0 - RELAX) * here
            total = total + AN[n, cols] * old[n - 1, cols]
            total = total + AS[n, cols] * old[n + 1, cols]
            total = total + AW[n, cols] * roll(here, 2, 0)
            total = total + AE[n, cols] * roll(here, -2, 0)
            total = total + AD[n, cols] * roll(here, 2, 1)
            new[n, cols] = total + AU[n, cols] * roll(here, -2, 1)

    final = E.at[COARSE % 2]
    tile = (8, 128)
    lane8, row8 = lanes_of(tile), rows_of(tile)
    odd_lane8, odd_row8 = (lane8 & 1) == 1, (row8 & 1) == 1
    for k in range(8):
        value = final[7 + k, 16:24]
        for comp in range(3):
            error = spread(value, comp, odd_lane8, odd_row8)
            for r in (2 * k, 2 * k + 1):
                out_ref[comp, r] = smooth_ref[comp, r] + error


def wanted_cells(lats, lons, lon):
    dest = jnp.arange(lats, dtype=jnp.int32)[:, None]
    position = jnp.arange(CELLS, dtype=jnp.int32)[None, :]
    rows, cols = lats * 16, lons * 8
    edge = (lon == 0) | (lon == lons - 1)
    side_row = dest * 16 + position - 4
    on_side = edge & (position < 24) & (side_row >= 0) & (side_row < rows)
    side = 2 * cols + jnp.where(lon == 0, 0, rows) + jnp.clip(side_row, 0, rows - 1)
    along = jnp.where((dest == 0) & (position < 4), position, position - 20)
    corner_col = jnp.where(lon == 0, along, lon * 8 + along - 4)
    col = jnp.where(edge, corner_col, lon * 8 + position - 4)
    row_cell = jnp.where(dest == 0, 0, cols) + jnp.clip(col, 0, cols - 1)
    return jnp.where(on_side, side, row_cell)


def per_device(velocity, forcing, viscosity, ghost_slots, corner_rows, corner_cols, corner_weights):
    v, f, mu = velocity[0], forcing[0], viscosity[0]
    lats, lons = lax.axis_size("lat"), lax.axis_size("lon")
    params = pltpu.CompilerParams(vmem_limit_bytes=32 * 2**20)
    f32 = jnp.float32
    place = jnp.stack(
        [lax.axis_index("lat"), lax.axis_index("lon"), jnp.int32(lats - 1), jnp.int32(lons - 1)]
    ).astype(jnp.int32)
    slots = ghost_slots[0]
    source_rows = ((slots // 3) % lons) * 9 + (slots % 3) * 3
    ghost_rows = (slots // (3 * lons)) * (3 * CELLS)
    cells = wanted_cells(lats, lons, lax.axis_index("lon")).reshape(-1)

    def kernel(body, shapes, specs):
        return pl.pallas_call(
            body,
            out_shape=[jax.ShapeDtypeStruct(shape, f32) for shape in shapes],
            in_specs=specs,
            out_specs=[VMEM] * len(shapes),
            compiler_params=params,
        )

    edge, first_row, first_cell = kernel(
        first_kernel, ((3, 16, 128), (3, 8, 128), (3, 128)), [VMEM]
    )(v)
    edge = shifted(edge, 0, -1)
    first_cell = shifted(first_cell, -1, -1)
    first_row = shifted(first_row, -1, 0)
    blended = kernel(
        blend_kernel, ((9, 1, 128), (3, 16, 128), (3, 8, 128), (3, 1, 128)), [SMEM] * 3 + [VMEM]
    )(corner_rows[0, 0], corner_cols[0, 0], corner_weights[0, 0], v)
    (values,) = kernel(interp_kernel, ((9 * lons, 1, 128),), [VMEM] * 7)(
        *blended, edge, first_row, first_cell
    )
    values = lax.ppermute(values.reshape(lons, 1, 1152), "patch", [(0, 1), (1, 0)])
    around = lax.all_to_all(values, "lon", 0, 0, tiled=True)
    to_above, to_below = kernel(cut_kernel, ((32, 8, 128),) * 2, [VMEM] * 3)(v, f, mu)
    above, below = exchange("lat", to_above, to_below)

    chosen = pl.pallas_call(
        pick_kernel,
        out_shape=jax.ShapeDtypeStruct((lats * 3 * CELLS, 1, 128), f32),
        in_specs=[SMEM, SMEM, SMEM, VMEM],
        out_specs=VMEM,
        compiler_params=params,
        name="pick",
    )(place, cells, source_rows, around.reshape(lons * 9, 1, 128))
    everything = lax.all_to_all(chosen.reshape(lats, 3 * CELLS, 128), "lat", 0, 0, tiled=True)
    everything = everything.reshape(lats * 3 * CELLS, 1, 128)
    to_right, to_left = kernel(pack_kernel, ((92, 8, 128),) * 2, [VMEM] * 5)(v, f, mu, above, below)
    left, right = exchange("lon", to_left, to_right)

    block = jax.ShapeDtypeStruct((3, 16, 8, 128), f32)
    field = (3, 28, 24, 128)
    residual, smoothed, message = pl.pallas_call(
        smooth_kernel,
        out_shape=(block, block, jax.ShapeDtypeStruct((10, 8, 128), f32)),
        in_specs=[SMEM, SMEM] + [VMEM] * 8,
        out_specs=(VMEM, VMEM, VMEM),
        scratch_shapes=[pltpu.VMEM(field, f32)] * 3
        + [
            pltpu.VMEM(shape, f32)
            for shape in ((6, 28, 24, 128), (16, 8, 128), (8, 8, 128), (8, 8, 128), (28, 24, 128))
        ],
        compiler_params=params,
        name="smooth",
    )(place, ghost_rows, v, f, mu, left, right, above, below, everything)

    left, right = two_neighbours("lon", message)
    band = jnp.concatenate([*left, message, *right], axis=1)
    tile_list = (-1, 8, 128)
    inverse = band[8:10].reshape(tile_list)
    to_above = [band[0:2].reshape(tile_list), band[2:7, 8:32].reshape(tile_list), inverse]
    to_below = [band[7:8], band[6:7]] + [band[r : r + 1, 8:32] for r in (5, 4, 3, 2, 1)]
    to_below = [part.reshape(tile_list) for part in to_below] + [inverse]
    band_above, band_below = exchange(
        "lat", jnp.concatenate(to_above, axis=0), jnp.concatenate(to_below, axis=0)
    )
    coarse = pltpu.VMEM((22, 40, 128), f32)
    new = pl.pallas_call(
        coarse_kernel,
        out_shape=block,
        in_specs=[VMEM] * 4,
        out_specs=VMEM,
        scratch_shapes=[coarse, coarse, coarse, pltpu.VMEM((2, 22, 40, 128), f32)] + [coarse] * 6,
        compiler_params=params,
        name="coarse",
    )(band, band_above, band_below, smoothed)
    return new[None], residual[None]


def solution(mesh):
    placed = (
        P("patch", None, "lat", "lon", None),
        P("patch", None, "lat", "lon", None),
        P("patch", "lat", "lon", None),
        P("patch", None),
        P("patch", "lat", "lon"),
        P("patch", "lat", "lon"),
        P("patch", "lat", None, "lon"),
    )
    return jax.shard_map(
        per_device,
        mesh=mesh,
        in_specs=placed,
        out_specs=(P("patch", None, "lat", "lon", None), P("patch", None, "lat", "lon", None)),
        check_vma=False,
    )
```

```python
import jax
import jax.numpy as jnp
from jax import lax
from jax.experimental import pallas as pl
from jax.experimental.pallas import tpu as pltpu
from jax.sharding import PartitionSpec as P


AXES = ("patch", "lat", "lon")
RELAX = 0.8
COARSE = 8
PAD = 6
CELLS = 32
VMEM = pl.BlockSpec(memory_space=pltpu.VMEM)
SMEM = pl.BlockSpec(memory_space=pltpu.SMEM)


def shifted(value, by_lat, by_lon, flip=0):
    patches, lats, lons = (lax.axis_size(axis) for axis in AXES)
    pairs = []
    for p in range(patches):
        for a in range(lats):
            for b in range(lons):
                a2, b2 = a + by_lat, b + by_lon
                if 0 <= a2 < lats and 0 <= b2 < lons:
                    pairs.append(((p * lats + a) * lons + b, ((p ^ flip) * lats + a2) * lons + b2))
    return lax.ppermute(value, AXES, pairs)


def lanes_of(shape):
    return lax.broadcasted_iota(jnp.int32, shape, len(shape) - 1)


def rows_of(shape):
    return lax.broadcasted_iota(jnp.int32, shape, len(shape) - 2)


def roll(value, by, axis):
    return pltpu.roll(value, by % value.shape[axis], axis)


def lane_partner(value, odd_lane):
    return jnp.where(odd_lane, roll(value, 1, 1), roll(value, -1, 1))


def row_partner(value, odd_row):
    return jnp.where(odd_row, roll(value, 1, 0), roll(value, -1, 0))


def first_kernel(v_ref, edge_ref, below_ref, corner_ref):
    sub = rows_of((8, 128))
    for comp in range(3):
        corner_ref[comp : comp + 1] = v_ref[comp, 0, 0:1]
        below_ref[comp] = v_ref[comp, 0]
        for j in range(2):
            first = v_ref[comp, 8 * j]
            for r in range(1, 8):
                first = jnp.where(sub == r, roll(v_ref[comp, 8 * j + r], r, 0), first)
            edge_ref[comp, 8 * j : 8 * j + 8] = first


def lat_tile(field, away):
    if 3 <= field < 6:
        return 20 + 4 * (field - 3) + away - 1
    return 5 * min(field, 3) + away - 1


def cut_kernel(v_ref, f_ref, mu_ref, up_ref, down_ref):
    for field in range(7):
        for away in range(1, 5 if 3 <= field < 6 else 6):
            for ref, r in ((up_ref, away - 1), (down_ref, 16 - away)):
                if field == 6:
                    value = mu_ref[r]
                else:
                    value = v_ref[field, r] if field < 3 else f_ref[field - 3, r]
                ref[lat_tile(field, away)] = value


def blend_kernel(rows_ref, cols_ref, weights_ref, v_ref, out_ref):
    tall, flat = rows_of((16, 128)), rows_of((8, 128))
    for slot in range(3):
        row, col = rows_ref[slot], cols_ref[slot]
        w0, w1, w2, w3 = (weights_ref[k, slot] for k in range(4))
        here, next_one = flat == col, flat == col + 1
        upper = jnp.where(here, w0, jnp.where(next_one, w2, 0.0))
        lower = jnp.where(here, w1, jnp.where(next_one, w3, 0.0))
        within = row < 15
        next_row = jnp.where(within, row + 1, row)
        inner = jnp.where(within, lower, 0.0)
        for comp in range(3):
            total = upper * v_ref[comp, row] + inner * v_ref[comp, next_row]
            at = 3 * slot + comp
            out_ref[at : at + 1] = jnp.sum(total, axis=0, keepdims=True)
        beside = jnp.where(tall == row, w2, jnp.where(tall == row + 1, w3, 0.0))
        out_ref[16 + 16 * slot : 32 + 16 * slot] = jnp.where(col == 7, beside, 0.0)
        out_ref[64 + 8 * slot : 72 + 8 * slot] = jnp.where(within, 0.0, lower)
        both = jnp.where((row == 15) & (col == 7), w3, 0.0)
        out_ref[9 + slot : 10 + slot] = jnp.full((1, 128), both, jnp.float32)
    out_ref[12:16] = jnp.zeros((4, 128), jnp.float32)


def interp_kernel(blend_ref, edge_ref, below_ref, corner_ref, out_ref):
    for slot in range(3):
        edge_w = blend_ref[16 + 16 * slot : 32 + 16 * slot]
        below_w = blend_ref[64 + 8 * slot : 72 + 8 * slot]
        corner_w = blend_ref[9 + slot : 10 + slot]
        for comp in range(3):
            at = 3 * slot + comp
            beside = edge_w * edge_ref[comp]
            total = beside[0:8] + beside[8:16] + below_w * below_ref[comp]
            total = jnp.sum(total, axis=0, keepdims=True) + blend_ref[at : at + 1]
            total = total + corner_w * corner_ref[comp : comp + 1]
            for dest in range(out_ref.shape[0] // 9):
                out_ref[9 * dest + at] = total


def pick_kernel(place_ref, cells_ref, source_ref, row_ref, out_ref):
    lon, last_lat, last_lon = place_ref[1], place_ref[2], place_ref[3]
    edge = (lon == 0) | (lon == last_lon)

    def copy(dest, position):
        base = source_ref[cells_ref[dest * CELLS + position]]
        for comp in range(3):
            out_ref[dest * 3 * CELLS + position * 3 + comp] = row_ref[base + comp]

    @pl.when(edge)
    def _():
        def step(dest, carry):
            for position in range(CELLS):
                copy(dest, position)
            return carry

        lax.fori_loop(0, last_lat + 1, step, 0)

    @pl.when(~edge)
    def _():
        for position in range(16):
            copy(0, position)
            copy(last_lat, position)


def side_tile(ref, field, r, col, sub):
    value = ref[12 * field + (r + 4) // 2]
    if r % 2:
        value = roll(value, 4, 0)
    extra = {0: 0, 1: 1, 2: 2, 6: 3}.get(field)
    if extra is None or not 0 <= r < 16:
        return value
    fifth = roll(ref[84 + 2 * extra + r // 8], col - r % 8, 0)
    return jnp.where(sub == col, fifth, value)


def pack_kernel(v_ref, f_ref, mu_ref, above_ref, below_ref, right_ref, left_ref):
    sub = rows_of((8, 128))

    def row(field, r):
        if r < 0:
            return above_ref[lat_tile(field, -r)]
        if r > 15:
            return below_ref[lat_tile(field, r - 15)]
        if field == 6:
            return mu_ref[r]
        return v_ref[field, r] if field < 3 else f_ref[field - 3, r]

    for field in range(7):
        for t in range(12):
            even, odd = row(field, 2 * t - 4), roll(row(field, 2 * t - 3), 4, 0)
            right_ref[12 * field + t] = jnp.where(sub < 4, odd, even)
            left_ref[12 * field + t] = jnp.where(sub < 4, even, odd)
    for n, field in enumerate((0, 1, 2, 6)):
        for j in range(2):
            third = fourth = row(field, 8 * j)
            for r in range(8):
                value = row(field, 8 * j + r)
                third = jnp.where(sub == r, roll(value, r - 3, 0), third)
                fourth = jnp.where(sub == r, roll(value, r - 4, 0), fourth)
            right_ref[84 + 2 * n + j] = third
            left_ref[84 + 2 * n + j] = fourth


def prepare(
    place_ref, f_ref, mu_ref, left_ref, right_ref, above_ref, below_ref,
    F, C, DG, over_ref, visc_ref, MU,
):
    lat, lon = place_ref[0], place_ref[1]
    last_lat, last_lon = place_ref[2], place_ref[3]
    wide = (24, 128)
    lane, row = lanes_of(wide), rows_of(wide)
    odd_lane, odd_row = (lane & 1) == 1, (row & 1) == 1
    own = slice(PAD, PAD + 16)
    sub = rows_of((8, 128))
    MU[own, 8:16] = mu_ref[...]
    for r in range(-4, 20):
        MU[r + PAD, 0:8] = side_tile(left_ref, 6, r, 3, sub)
        MU[r + PAD, 16:24] = side_tile(right_ref, 6, r, 4, sub)
    for away in range(1, 6):
        for i, ref in ((PAD - away, above_ref), (PAD + 15 + away, below_ref)):
            value = ref[lat_tile(6, away)]
            MU[i, 8:16] = value
            if away == 5:
                MU[i, 0:8] = MU[i, 16:24] = value

    @pl.when(lat == 0)
    def _():
        MU[4] = MU[6]
        MU[5] = MU[6]

    @pl.when(lat == last_lat)
    def _():
        MU[22] = MU[21]
        MU[23] = MU[21]

    @pl.when(lon == 0)
    def _():
        for i in range(1, 27):
            MU[i, 0:8] = jnp.broadcast_to(MU[i, 8:9], (8, 128))

    @pl.when(lon == last_lon)
    def _():
        for i in range(1, 27):
            MU[i, 16:24] = jnp.broadcast_to(MU[i, 15:16], (8, 128))

    for i in range(2, 26):
        mid = MU[i]
        north = 0.5 * (mid + MU[i - 1])
        south = 0.5 * (mid + MU[i + 1])
        west = 0.5 * (mid + roll(mid, 1, 0))
        east = 0.5 * (mid + roll(mid, -1, 0))
        down = 0.5 * (mid + jnp.where(lane == 0, mid, roll(mid, 1, 1)))
        up = 0.5 * (mid + jnp.where(lane == 127, mid, roll(mid, -1, 1)))
        total = north + south + west + east + down + up
        inverse = 1.0 / total
        C[0, i] = north * inverse
        C[1, i] = south * inverse
        C[2, i] = west * inverse
        C[3, i] = east * inverse
        C[4, i] = jnp.where(lane == 0, 0.0, down * inverse)
        C[5, i] = jnp.where(lane == 127, 0.0, up * inverse)
        r = i - PAD
        if 0 <= r < 16:
            DG[r] = total[8:16]
        for comp in range(3):
            if 0 <= r < 16:
                force = f_ref[comp, r]
            else:
                ref, away = (above_ref, -r) if r < 0 else (below_ref, r - 15)
                force = ref[lat_tile(3 + comp, away)]
            F[comp, i, 0:8] = side_tile(left_ref, 3 + comp, r, 3, sub) * inverse[0:8]
            F[comp, i, 8:16] = force * inverse[8:16]
            F[comp, i, 16:24] = side_tile(right_ref, 3 + comp, r, 4, sub) * inverse[16:24]

    def coarse_visc(i):
        both = MU[i] + MU[i + 1]
        flat = 0.25 * (both + row_partner(both, odd_row))
        return flat, 0.5 * (flat + lane_partner(flat, odd_lane))

    layers = [coarse_visc(PAD + 2 * k) for k in (-1, 0)]
    for k in range(8):
        layers.append(coarse_visc(PAD + 2 * k + 2))
        before, (flat, visc), after = layers[k][1], layers[k + 1], layers[k + 2][1]
        edge_down = jnp.where(lane == 0, flat, roll(flat, 1, 1))
        edge_up = jnp.where(lane == 127, flat, roll(flat, -1, 1))
        total = 6.0 * visc + before + after + roll(visc, 2, 0) + roll(visc, -2, 0)
        total = total + jnp.where(lane < 2, edge_down, roll(visc, 2, 1))
        total = total + jnp.where(lane >= 126, edge_up, roll(visc, -2, 1))
        over_ref[k] = RELAX / (0.125 * total[8:16])
        visc_ref[k] = visc[8:16]


def smooth_kernel(
    place_ref, ghost_ref, v_ref, f_ref, mu_ref, left_ref, right_ref, above_ref, below_ref, slot_ref,
    res_ref, smooth_ref, message_ref, A, B, F, C, DG, over_ref, visc_ref, MU,
):
    lat, lon = place_ref[0], place_ref[1]
    last_lat, last_lon = place_ref[2], place_ref[3]
    wide = (24, 128)
    lane, row = lanes_of(wide), rows_of(wide)
    sub = rows_of((8, 128))
    own = slice(PAD, PAD + 16)

    for comp in range(3):
        A[comp, own, 8:16] = v_ref[comp]
        for r in range(-4, 20):
            A[comp, r + PAD, 0:8] = side_tile(left_ref, comp, r, 3, sub)
            A[comp, r + PAD, 16:24] = side_tile(right_ref, comp, r, 4, sub)
        for away in range(1, 6):
            for i, ref in ((PAD - away, above_ref), (PAD + 15 + away, below_ref)):
                value = ref[lat_tile(comp, away)]
                A[comp, i, 8:16] = value
                if away == 5:
                    A[comp, i, 0:8] = A[comp, i, 16:24] = value

    edge = (lon == 0) | (lon == last_lon)
    all_cols, all_rows = (last_lon + 1) * 8, (last_lat + 1) * 16

    def fill_row(i, start):
        for col in range(-4, 12):
            along = jnp.where(lon == 0, col, col + 4)
            packed_at = jnp.where((lat == 0) & (along < 4), along, along + 20)
            position = jnp.clip(jnp.where(edge, packed_at, col + 4), 0, CELLS - 1)
            cell = start + jnp.clip(lon * 8 + col, 0, all_cols - 1)
            base = ghost_ref[cell] + 3 * position
            for comp in range(3):
                A[comp, i, 8 + col : 9 + col] = slot_ref[base + comp]

    def fill_side(col, start):
        for r in range(-4, 20):
            base = ghost_ref[start + jnp.clip(lat * 16 + r, 0, all_rows - 1)] + 3 * (r + 4)
            for comp in range(3):
                A[comp, r + PAD, 8 + col : 9 + col] = slot_ref[base + comp]

    prepare(
        place_ref, f_ref, mu_ref, left_ref, right_ref, above_ref, below_ref,
        F, C, DG, over_ref, visc_ref, MU,
    )
    pl.when(lat == 0)(lambda: fill_row(5, 0))
    pl.when(lat == last_lat)(lambda: fill_row(22, all_cols))
    pl.when(lon == 0)(lambda: fill_side(-1, 2 * all_cols))
    pl.when(lon == last_lon)(lambda: fill_side(8, 2 * all_cols + all_rows))

    inside = ((row >= 8) | (lon > 0)) & ((row < 16) | (lon < last_lon))
    parity = jnp.where(inside, (row + lane) & 1, 2)

    def weighted(source, comp, i, here):
        total = F[comp, i] + C[0, i] * source[comp, i - 1]
        total = total + C[1, i] * source[comp, i + 1]
        total = total + C[2, i] * roll(here, 1, 0)
        total = total + C[3, i] * roll(here, -1, 0)
        total = total + C[4, i] * roll(here, 1, 1)
        return total + C[5, i] * roll(here, -1, 1)

    wanted = {}
    for colour in range(2):
        wanted[colour, "mid"] = jnp.int32(colour)
        wanted[colour, "top"] = jnp.where(lat == 0, 3, colour)
        wanted[colour, "low"] = jnp.where(lat == last_lat, 3, colour)

    def relax(colour, reach, source, target):
        for r in range(-reach, 16 + reach):
            i = r + PAD
            zone = "top" if r < 0 else "low" if r > 15 else "mid"
            mask = parity == wanted[(colour + r) % 2, zone]
            for comp in range(3):
                here = source[comp, i]
                target[comp, i] = jnp.where(mask, weighted(source, comp, i, here), here)

    relax(0, 4, A, B)
    relax(1, 3, B, A)
    relax(0, 2, A, B)
    relax(1, 1, B, A)

    tile = (8, 128)
    lane8, row8 = lanes_of(tile), rows_of(tile)
    odd_lane8, odd_row8 = (lane8 & 1) == 1, (row8 & 1) == 1

    def packed(parts):
        low = jnp.where(odd_lane8, parts[1], parts[0])
        high = jnp.where(odd_lane8, parts[3], parts[2])
        return jnp.where(odd_row8, high, low)

    for k in range(8):
        parts = []
        for comp in range(3):
            rhs = jnp.zeros(tile, jnp.float32)
            for r in (2 * k, 2 * k + 1):
                here = A[comp, r + PAD]
                smooth_ref[comp, r] = here[8:16]
                left = DG[r] * (weighted(A, comp, r + PAD, here) - here)[8:16]
                res_ref[comp, r] = left
                rhs = rhs + left
            rhs = rhs + lane_partner(rhs, odd_lane8)
            rhs = rhs + row_partner(rhs, odd_row8)
            parts.append(0.125 * rhs * over_ref[k])
        message_ref[k] = packed(parts + [visc_ref[k]])
        if k % 4 == 3:
            message_ref[8 + k // 4] = packed([over_ref[j] for j in range(k - 3, k + 1)])


def coarse_kernel(
    mid_ref, above_ref, below_ref, smooth_ref, out_ref, Q, CV, DV, E, AN, AS, AW, AE, AD, AU
):
    wide = (40, 128)
    lane, row = lanes_of(wide), rows_of(wide)
    odd_lane, odd_row = (lane & 1) == 1, (row & 1) == 1

    def spread(value, part, odd_l, odd_r):
        keep = odd_l if part % 2 else ~odd_l
        value = jnp.where(keep, value, roll(value, -1 if part % 2 else 1, 1))
        keep = odd_r if part // 2 else ~odd_r
        return jnp.where(keep, value, roll(value, -1 if part // 2 else 1, 0))

    def far(n):
        return max(0, 7 - n, n - 14)

    for n in range(22):
        away = far(n)
        if away == 0:
            t = n - 7
            Q[n] = mid_ref[t]
            cols, over = slice(0, 40), mid_ref[8 + t // 4]
        else:
            ref, t = (above_ref, n + 1) if n < 7 else (below_ref, n - 15)
            tiles = range(5) if away < 3 else range(1, 4)
            first = 5 * (away - 1) if away < 3 else 10 + 3 * (away - 3) - 1
            for j in tiles:
                Q[n, 8 * j : 8 * j + 8] = ref[first + j]
            cols = slice(8 * tiles[0], 8 * tiles[-1] + 8)
            over = [ref[25 + 5 * (t // 4) + j] for j in tiles]
            over = jnp.concatenate(over, axis=0)
        CV[n, cols] = spread(Q[n, cols], 3, odd_lane[cols], odd_row[cols])
        DV[n, cols] = 0.125 * spread(over, t % 4, odd_lane[cols], odd_row[cols])

    def span(reach):
        return slice(0, 40) if reach > 3 else slice(8, 32)

    for n in range(1, 21):
        cols = span(6 - far(n))
        edge = lane[cols]
        visc, over = CV[n, cols], DV[n, cols]
        AN[n, cols] = over * (visc + CV[n - 1, cols])
        AS[n, cols] = over * (visc + CV[n + 1, cols])
        AW[n, cols] = over * (visc + roll(visc, 2, 0))
        AE[n, cols] = over * (visc + roll(visc, -2, 0))
        AD[n, cols] = jnp.where(edge < 2, 0.0, over * (visc + roll(visc, 2, 1)))
        AU[n, cols] = jnp.where(edge >= 126, 0.0, over * (visc + roll(visc, -2, 1)))

    for turn in range(1, COARSE):
        old = Q if turn == 1 else E.at[turn % 2]
        new = E.at[(turn + 1) % 2]
        for n in range(turn, 22 - turn):
            cols = span(7 - turn - far(n))
            here = old[n, cols]
            total = Q[n, cols] + (1.0 - RELAX) * here
            total = total + AN[n, cols] * old[n - 1, cols]
            total = total + AS[n, cols] * old[n + 1, cols]
            total = total + AW[n, cols] * roll(here, 2, 0)
            total = total + AE[n, cols] * roll(here, -2, 0)
            total = total + AD[n, cols] * roll(here, 2, 1)
            new[n, cols] = total + AU[n, cols] * roll(here, -2, 1)

    final = E.at[COARSE % 2]
    tile = (8, 128)
    lane8, row8 = lanes_of(tile), rows_of(tile)
    odd_lane8, odd_row8 = (lane8 & 1) == 1, (row8 & 1) == 1
    for k in range(8):
        value = final[7 + k, 16:24]
        for comp in range(3):
            error = spread(value, comp, odd_lane8, odd_row8)
            for r in (2 * k, 2 * k + 1):
                out_ref[comp, r] = smooth_ref[comp, r] + error


def wanted_cells(lats, lons, lon):
    dest = jnp.arange(lats, dtype=jnp.int32)[:, None]
    position = jnp.arange(CELLS, dtype=jnp.int32)[None, :]
    rows, cols = lats * 16, lons * 8
    edge = (lon == 0) | (lon == lons - 1)
    side_row = dest * 16 + position - 4
    on_side = edge & (position < 24) & (side_row >= 0) & (side_row < rows)
    side = 2 * cols + jnp.where(lon == 0, 0, rows) + jnp.clip(side_row, 0, rows - 1)
    along = jnp.where((dest == 0) & (position < 4), position, position - 20)
    corner_col = jnp.where(lon == 0, along, lon * 8 + along - 4)
    col = jnp.where(edge, corner_col, lon * 8 + position - 4)
    row_cell = jnp.where(dest == 0, 0, cols) + jnp.clip(col, 0, cols - 1)
    return jnp.where(on_side, side, row_cell)


def per_device(velocity, forcing, viscosity, ghost_slots, corner_rows, corner_cols, corner_weights):
    v, f, mu = velocity[0], forcing[0], viscosity[0]
    lats, lons = lax.axis_size("lat"), lax.axis_size("lon")
    params = pltpu.CompilerParams(vmem_limit_bytes=32 * 2**20)
    f32 = jnp.float32
    place = jnp.stack(
        [lax.axis_index("lat"), lax.axis_index("lon"), jnp.int32(lats - 1), jnp.int32(lons - 1)]
    ).astype(jnp.int32)
    slots = ghost_slots[0]
    source_rows = ((slots // 3) % lons) * 9 + (slots % 3) * 3
    ghost_rows = (slots // (3 * lons)) * (3 * CELLS)
    cells = wanted_cells(lats, lons, lax.axis_index("lon")).reshape(-1)

    def kernel(body, shapes, specs):
        return pl.pallas_call(
            body,
            out_shape=[jax.ShapeDtypeStruct(shape, f32) for shape in shapes],
            in_specs=specs,
            out_specs=[VMEM] * len(shapes),
            compiler_params=params,
        )

    edge, first_row, first_cell = kernel(
        first_kernel, ((3, 16, 128), (3, 8, 128), (3, 128)), [VMEM]
    )(v)
    first_cell = shifted(first_cell, -1, -1, 1)
    first_row = shifted(first_row, -1, 0, 1)
    edge = shifted(edge, 0, -1, 1)
    (blended,) = kernel(blend_kernel, ((88, 128),), [SMEM] * 3 + [VMEM])(
        corner_rows[0, 0], corner_cols[0, 0], corner_weights[0, 0], v
    )
    blended = shifted(blended, 0, 0, 1)
    (values,) = kernel(interp_kernel, ((9 * lons, 1, 128),), [VMEM] * 4)(
        blended, edge, first_row, first_cell
    )
    around = lax.all_to_all(values.reshape(lons, 1, 1152), "lon", 0, 0, tiled=True)
    to_above, to_below = kernel(cut_kernel, ((32, 8, 128),) * 2, [VMEM] * 3)(v, f, mu)
    below = shifted(to_above, -1, 0)
    above = shifted(to_below, 1, 0)

    chosen = pl.pallas_call(
        pick_kernel,
        out_shape=jax.ShapeDtypeStruct((lats * 3 * CELLS, 1, 128), f32),
        in_specs=[SMEM, SMEM, SMEM, VMEM],
        out_specs=VMEM,
        compiler_params=params,
        name="pick",
    )(place, cells, source_rows, around.reshape(lons * 9, 1, 128))
    everything = lax.all_to_all(chosen.reshape(lats, 3 * CELLS, 128), "lat", 0, 0, tiled=True)
    everything = everything.reshape(lats * 3 * CELLS, 1, 128)
    to_right, to_left = kernel(pack_kernel, ((92, 8, 128),) * 2, [VMEM] * 5)(v, f, mu, above, below)
    left = shifted(to_right, 0, 1)
    right = shifted(to_left, 0, -1)

    block = jax.ShapeDtypeStruct((3, 16, 8, 128), f32)
    field = (3, 28, 24, 128)
    residual, smoothed, message = pl.pallas_call(
        smooth_kernel,
        out_shape=(block, block, jax.ShapeDtypeStruct((10, 8, 128), f32)),
        in_specs=[SMEM, SMEM] + [VMEM] * 8,
        out_specs=(VMEM, VMEM, VMEM),
        scratch_shapes=[pltpu.VMEM(field, f32)] * 3
        + [
            pltpu.VMEM(shape, f32)
            for shape in ((6, 28, 24, 128), (16, 8, 128), (8, 8, 128), (8, 8, 128), (28, 24, 128))
        ],
        compiler_params=params,
        name="smooth",
    )(place, ghost_rows, v, f, mu, left, right, above, below, everything)

    tiles = [
        shifted(message, 0, 2),
        shifted(message, 0, 1),
        message,
        shifted(message, 0, -1),
        shifted(message, 0, -2),
    ]
    band = jnp.concatenate(tiles, axis=1)
    tile_list = (-1, 8, 128)
    inverse = band[8:10].reshape(tile_list)
    to_above = [band[0:2].reshape(tile_list), band[2:7, 8:32].reshape(tile_list), inverse]
    to_below = [band[7:8], band[6:7]] + [band[r : r + 1, 8:32] for r in (5, 4, 3, 2, 1)]
    to_below = [part.reshape(tile_list) for part in to_below] + [inverse]
    band_below = shifted(jnp.concatenate(to_above, axis=0), -1, 0)
    band_above = shifted(jnp.concatenate(to_below, axis=0), 1, 0)
    coarse = pltpu.VMEM((22, 40, 128), f32)
    new = pl.pallas_call(
        coarse_kernel,
        out_shape=block,
        in_specs=[VMEM] * 4,
        out_specs=VMEM,
        scratch_shapes=[coarse, coarse, coarse, pltpu.VMEM((2, 22, 40, 128), f32)] + [coarse] * 6,
        compiler_params=params,
        name="coarse",
    )(band, band_above, band_below, smoothed)
    return new[None], residual[None]


def solution(mesh):
    placed = (
        P("patch", None, "lat", "lon", None),
        P("patch", None, "lat", "lon", None),
        P("patch", "lat", "lon", None),
        P("patch", None),
        P("patch", "lat", "lon"),
        P("patch", "lat", "lon"),
        P("patch", "lat", None, "lon"),
    )
    return jax.shard_map(
        per_device,
        mesh=mesh,
        in_specs=placed,
        out_specs=(P("patch", None, "lat", "lon", None), P("patch", None, "lat", "lon", None)),
        check_vma=False,
    )
```

```python
import jax
import jax.numpy as jnp
from jax import lax
from jax.experimental import pallas as pl
from jax.experimental.pallas import tpu as pltpu
from jax.sharding import PartitionSpec as P


AXES = ("patch", "lat", "lon")
RELAX = 0.8
COARSE = 8
PAD = 6
CELLS = 32
VMEM = pl.BlockSpec(memory_space=pltpu.VMEM)
SMEM = pl.BlockSpec(memory_space=pltpu.SMEM)


def shifted(value, by_lat, by_lon, flip=0):
    patches, lats, lons = (lax.axis_size(axis) for axis in AXES)
    pairs = []
    for p in range(patches):
        for a in range(lats):
            for b in range(lons):
                a2, b2 = a + by_lat, b + by_lon
                if 0 <= a2 < lats and 0 <= b2 < lons:
                    pairs.append(((p * lats + a) * lons + b, ((p ^ flip) * lats + a2) * lons + b2))
    return lax.ppermute(value, AXES, pairs)


def lanes_of(shape):
    return lax.broadcasted_iota(jnp.int32, shape, len(shape) - 1)


def rows_of(shape):
    return lax.broadcasted_iota(jnp.int32, shape, len(shape) - 2)


def roll(value, by, axis):
    return pltpu.roll(value, by % value.shape[axis], axis)


def lane_partner(value, odd_lane):
    return jnp.where(odd_lane, roll(value, 1, 1), roll(value, -1, 1))


def row_partner(value, odd_row):
    return jnp.where(odd_row, roll(value, 1, 0), roll(value, -1, 0))


def first_kernel(
    rows_hbm, cols_hbm, weights_hbm, v_hbm, edge_ref, below_ref, corner_ref, blend_ref,
    rows_ref, cols_ref, weights_ref, v_ref, done,
):
    sub = rows_of((8, 128))
    pairs = (v_hbm, v_ref), (rows_hbm, rows_ref), (cols_hbm, cols_ref), (weights_hbm, weights_ref)
    copies = [pltpu.make_async_copy(*pair, done.at[n]) for n, pair in enumerate(pairs)]
    for copy in copies:
        copy.start()
    for copy in copies:
        copy.wait()
    blend(rows_ref, cols_ref, weights_ref, v_ref, blend_ref)
    for comp in range(3):
        corner_ref[comp : comp + 1] = v_ref[comp, 0, 0:1]
        below_ref[comp] = v_ref[comp, 0]
        for j in range(2):
            first = v_ref[comp, 8 * j]
            for r in range(1, 8):
                first = jnp.where(sub == r, roll(v_ref[comp, 8 * j + r], r, 0), first)
            edge_ref[comp, 8 * j : 8 * j + 8] = first


def lat_tile(field, away):
    if 3 <= field < 6:
        return 20 + 4 * (field - 3) + away - 1
    return 5 * min(field, 3) + away - 1


def cut_kernel(v_ref, f_ref, mu_ref, up_ref, down_ref):
    for field in range(7):
        for away in range(1, 5 if 3 <= field < 6 else 6):
            for ref, r in ((up_ref, away - 1), (down_ref, 16 - away)):
                if field == 6:
                    value = mu_ref[r]
                else:
                    value = v_ref[field, r] if field < 3 else f_ref[field - 3, r]
                ref[lat_tile(field, away)] = value


def blend(rows_ref, cols_ref, weights_ref, v_ref, out_ref):
    tall, flat = rows_of((16, 128)), rows_of((8, 128))
    for slot in range(3):
        row, col = rows_ref[0, slot], cols_ref[0, slot]
        w0, w1, w2, w3 = (weights_ref[slot, 0, k] for k in range(4))
        here, next_one = flat == col, flat == col + 1
        upper = jnp.where(here, w0, jnp.where(next_one, w2, 0.0))
        lower = jnp.where(here, w1, jnp.where(next_one, w3, 0.0))
        within = row < 15
        next_row = jnp.where(within, row + 1, row)
        inner = jnp.where(within, lower, 0.0)
        for comp in range(3):
            total = upper * v_ref[comp, row] + inner * v_ref[comp, next_row]
            at = 3 * slot + comp
            out_ref[at : at + 1] = jnp.sum(total, axis=0, keepdims=True)
        beside = jnp.where(tall == row, w2, jnp.where(tall == row + 1, w3, 0.0))
        out_ref[16 + 16 * slot : 32 + 16 * slot] = jnp.where(col == 7, beside, 0.0)
        out_ref[64 + 8 * slot : 72 + 8 * slot] = jnp.where(within, 0.0, lower)
        both = jnp.where((row == 15) & (col == 7), w3, 0.0)
        out_ref[9 + slot : 10 + slot] = jnp.full((1, 128), both, jnp.float32)
    out_ref[12:16] = jnp.zeros((4, 128), jnp.float32)


def interp_kernel(blend_ref, edge_ref, below_ref, corner_ref, out_ref):
    for slot in range(3):
        edge_w = blend_ref[16 + 16 * slot : 32 + 16 * slot]
        below_w = blend_ref[64 + 8 * slot : 72 + 8 * slot]
        corner_w = blend_ref[9 + slot : 10 + slot]
        for comp in range(3):
            at = 3 * slot + comp
            beside = edge_w * edge_ref[comp]
            total = beside[0:8] + beside[8:16] + below_w * below_ref[comp]
            total = jnp.sum(total, axis=0, keepdims=True) + blend_ref[at : at + 1]
            total = total + corner_w * corner_ref[comp : comp + 1]
            for dest in range(out_ref.shape[0] // 9):
                out_ref[9 * dest + at] = total


def pick_kernel(place_ref, cells_ref, source_ref, row_ref, out_ref):
    lon, last_lat, last_lon = place_ref[1], place_ref[2], place_ref[3]
    edge = (lon == 0) | (lon == last_lon)

    def copy(dest, position):
        base = source_ref[cells_ref[dest * CELLS + position]]
        for comp in range(3):
            out_ref[dest * 3 * CELLS + position * 3 + comp] = row_ref[base + comp]

    @pl.when(edge)
    def _():
        def step(dest, carry):
            for position in range(CELLS):
                copy(dest, position)
            return carry

        lax.fori_loop(0, last_lat + 1, step, 0)

    @pl.when(~edge)
    def _():
        for position in range(16):
            copy(0, position)
            copy(last_lat, position)


def side_tile(ref, field, r, col, sub):
    value = ref[12 * field + (r + 4) // 2]
    if r % 2:
        value = roll(value, 4, 0)
    extra = {0: 0, 1: 1, 2: 2, 6: 3}.get(field)
    if extra is None or not 0 <= r < 16:
        return value
    fifth = roll(ref[84 + 2 * extra + r // 8], col - r % 8, 0)
    return jnp.where(sub == col, fifth, value)


def pack_kernel(v_ref, f_ref, mu_ref, above_ref, below_ref, right_ref, left_ref):
    sub = rows_of((8, 128))

    def row(field, r):
        if r < 0:
            return above_ref[lat_tile(field, -r)]
        if r > 15:
            return below_ref[lat_tile(field, r - 15)]
        if field == 6:
            return mu_ref[r]
        return v_ref[field, r] if field < 3 else f_ref[field - 3, r]

    for field in range(7):
        for t in range(12):
            even, odd = row(field, 2 * t - 4), roll(row(field, 2 * t - 3), 4, 0)
            right_ref[12 * field + t] = jnp.where(sub < 4, odd, even)
            left_ref[12 * field + t] = jnp.where(sub < 4, even, odd)
    for n, field in enumerate((0, 1, 2, 6)):
        for j in range(2):
            third = fourth = row(field, 8 * j)
            for r in range(8):
                value = row(field, 8 * j + r)
                third = jnp.where(sub == r, roll(value, r - 3, 0), third)
                fourth = jnp.where(sub == r, roll(value, r - 4, 0), fourth)
            right_ref[84 + 2 * n + j] = third
            left_ref[84 + 2 * n + j] = fourth


def prepare(
    place_ref, f_ref, mu_ref, left_ref, right_ref, above_ref, below_ref,
    F, C, DG, over_ref, visc_ref, MU,
):
    lat, lon = place_ref[0], place_ref[1]
    last_lat, last_lon = place_ref[2], place_ref[3]
    wide = (24, 128)
    lane, row = lanes_of(wide), rows_of(wide)
    odd_lane, odd_row = (lane & 1) == 1, (row & 1) == 1
    own = slice(PAD, PAD + 16)
    sub = rows_of((8, 128))
    MU[own, 8:16] = mu_ref[...]
    for r in range(-4, 20):
        MU[r + PAD, 0:8] = side_tile(left_ref, 6, r, 3, sub)
        MU[r + PAD, 16:24] = side_tile(right_ref, 6, r, 4, sub)
    for away in range(1, 6):
        for i, ref in ((PAD - away, above_ref), (PAD + 15 + away, below_ref)):
            value = ref[lat_tile(6, away)]
            MU[i, 8:16] = value
            if away == 5:
                MU[i, 0:8] = MU[i, 16:24] = value

    @pl.when(lat == 0)
    def _():
        MU[4] = MU[6]
        MU[5] = MU[6]

    @pl.when(lat == last_lat)
    def _():
        MU[22] = MU[21]
        MU[23] = MU[21]

    @pl.when(lon == 0)
    def _():
        for i in range(1, 27):
            MU[i, 0:8] = jnp.broadcast_to(MU[i, 8:9], (8, 128))

    @pl.when(lon == last_lon)
    def _():
        for i in range(1, 27):
            MU[i, 16:24] = jnp.broadcast_to(MU[i, 15:16], (8, 128))

    for i in range(2, 26):
        mid = MU[i]
        north = 0.5 * (mid + MU[i - 1])
        south = 0.5 * (mid + MU[i + 1])
        west = 0.5 * (mid + roll(mid, 1, 0))
        east = 0.5 * (mid + roll(mid, -1, 0))
        down = 0.5 * (mid + jnp.where(lane == 0, mid, roll(mid, 1, 1)))
        up = 0.5 * (mid + jnp.where(lane == 127, mid, roll(mid, -1, 1)))
        total = north + south + west + east + down + up
        inverse = 1.0 / total
        C[0, i] = north * inverse
        C[1, i] = south * inverse
        C[2, i] = west * inverse
        C[3, i] = east * inverse
        C[4, i] = jnp.where(lane == 0, 0.0, down * inverse)
        C[5, i] = jnp.where(lane == 127, 0.0, up * inverse)
        r = i - PAD
        if 0 <= r < 16:
            DG[r] = total[8:16]
        for comp in range(3):
            if 0 <= r < 16:
                force = f_ref[comp, r]
            else:
                ref, away = (above_ref, -r) if r < 0 else (below_ref, r - 15)
                force = ref[lat_tile(3 + comp, away)]
            F[comp, i, 0:8] = side_tile(left_ref, 3 + comp, r, 3, sub) * inverse[0:8]
            F[comp, i, 8:16] = force * inverse[8:16]
            F[comp, i, 16:24] = side_tile(right_ref, 3 + comp, r, 4, sub) * inverse[16:24]

    def coarse_visc(i):
        both = MU[i] + MU[i + 1]
        flat = 0.25 * (both + row_partner(both, odd_row))
        return flat, 0.5 * (flat + lane_partner(flat, odd_lane))

    layers = [coarse_visc(PAD + 2 * k) for k in (-1, 0)]
    for k in range(8):
        layers.append(coarse_visc(PAD + 2 * k + 2))
        before, (flat, visc), after = layers[k][1], layers[k + 1], layers[k + 2][1]
        edge_down = jnp.where(lane == 0, flat, roll(flat, 1, 1))
        edge_up = jnp.where(lane == 127, flat, roll(flat, -1, 1))
        total = 6.0 * visc + before + after + roll(visc, 2, 0) + roll(visc, -2, 0)
        total = total + jnp.where(lane < 2, edge_down, roll(visc, 2, 1))
        total = total + jnp.where(lane >= 126, edge_up, roll(visc, -2, 1))
        over_ref[k] = RELAX / (0.125 * total[8:16])
        visc_ref[k] = visc[8:16]


def smooth_kernel(
    place_ref, ghost_ref, v_ref, f_ref, mu_ref, left_ref, right_ref, above_ref, below_ref, slot_ref,
    res_ref, smooth_ref, message_ref, A, B, F, C, DG, over_ref, visc_ref, MU,
):
    lat, lon = place_ref[0], place_ref[1]
    last_lat, last_lon = place_ref[2], place_ref[3]
    wide = (24, 128)
    lane, row = lanes_of(wide), rows_of(wide)
    sub = rows_of((8, 128))
    own = slice(PAD, PAD + 16)

    for comp in range(3):
        A[comp, own, 8:16] = v_ref[comp]
        for r in range(-4, 20):
            A[comp, r + PAD, 0:8] = side_tile(left_ref, comp, r, 3, sub)
            A[comp, r + PAD, 16:24] = side_tile(right_ref, comp, r, 4, sub)
        for away in range(1, 6):
            for i, ref in ((PAD - away, above_ref), (PAD + 15 + away, below_ref)):
                value = ref[lat_tile(comp, away)]
                A[comp, i, 8:16] = value
                if away == 5:
                    A[comp, i, 0:8] = A[comp, i, 16:24] = value

    edge = (lon == 0) | (lon == last_lon)
    all_cols, all_rows = (last_lon + 1) * 8, (last_lat + 1) * 16

    def fill_row(i, start):
        for col in range(-4, 12):
            along = jnp.where(lon == 0, col, col + 4)
            packed_at = jnp.where((lat == 0) & (along < 4), along, along + 20)
            position = jnp.clip(jnp.where(edge, packed_at, col + 4), 0, CELLS - 1)
            cell = start + jnp.clip(lon * 8 + col, 0, all_cols - 1)
            base = ghost_ref[cell] + 3 * position
            for comp in range(3):
                A[comp, i, 8 + col : 9 + col] = slot_ref[base + comp]

    def fill_side(col, start):
        for r in range(-4, 20):
            base = ghost_ref[start + jnp.clip(lat * 16 + r, 0, all_rows - 1)] + 3 * (r + 4)
            for comp in range(3):
                A[comp, r + PAD, 8 + col : 9 + col] = slot_ref[base + comp]

    prepare(
        place_ref, f_ref, mu_ref, left_ref, right_ref, above_ref, below_ref,
        F, C, DG, over_ref, visc_ref, MU,
    )
    pl.when(lat == 0)(lambda: fill_row(5, 0))
    pl.when(lat == last_lat)(lambda: fill_row(22, all_cols))
    pl.when(lon == 0)(lambda: fill_side(-1, 2 * all_cols))
    pl.when(lon == last_lon)(lambda: fill_side(8, 2 * all_cols + all_rows))

    inside = ((row >= 8) | (lon > 0)) & ((row < 16) | (lon < last_lon))
    parity = jnp.where(inside, (row + lane) & 1, 2)

    def weighted(source, comp, i, here):
        total = F[comp, i] + C[0, i] * source[comp, i - 1]
        total = total + C[1, i] * source[comp, i + 1]
        total = total + C[2, i] * roll(here, 1, 0)
        total = total + C[3, i] * roll(here, -1, 0)
        total = total + C[4, i] * roll(here, 1, 1)
        return total + C[5, i] * roll(here, -1, 1)

    wanted = {}
    for colour in range(2):
        wanted[colour, "mid"] = jnp.int32(colour)
        wanted[colour, "top"] = jnp.where(lat == 0, 3, colour)
        wanted[colour, "low"] = jnp.where(lat == last_lat, 3, colour)

    def relax(colour, reach, source, target):
        for r in range(-reach, 16 + reach):
            i = r + PAD
            zone = "top" if r < 0 else "low" if r > 15 else "mid"
            mask = parity == wanted[(colour + r) % 2, zone]
            for comp in range(3):
                here = source[comp, i]
                target[comp, i] = jnp.where(mask, weighted(source, comp, i, here), here)

    relax(0, 4, A, B)
    relax(1, 3, B, A)
    relax(0, 2, A, B)
    relax(1, 1, B, A)

    tile = (8, 128)
    lane8, row8 = lanes_of(tile), rows_of(tile)
    odd_lane8, odd_row8 = (lane8 & 1) == 1, (row8 & 1) == 1

    def packed(parts):
        low = jnp.where(odd_lane8, parts[1], parts[0])
        high = jnp.where(odd_lane8, parts[3], parts[2])
        return jnp.where(odd_row8, high, low)

    for k in range(8):
        parts = []
        for comp in range(3):
            rhs = jnp.zeros(tile, jnp.float32)
            for r in (2 * k, 2 * k + 1):
                here = A[comp, r + PAD]
                smooth_ref[comp, r] = here[8:16]
                left = DG[r] * (weighted(A, comp, r + PAD, here) - here)[8:16]
                res_ref[comp, r] = left
                rhs = rhs + left
            rhs = rhs + lane_partner(rhs, odd_lane8)
            rhs = rhs + row_partner(rhs, odd_row8)
            parts.append(0.125 * rhs * over_ref[k])
        message_ref[k] = packed(parts + [visc_ref[k]])
        if k % 4 == 3:
            message_ref[8 + k // 4] = packed([over_ref[j] for j in range(k - 3, k + 1)])


def coarse_kernel(
    mid_ref, above_ref, below_ref, smooth_ref, left_ref, out_ref, res_ref,
    done, Q, CV, DV, E, AN, AS, AW, AE, AD, AU,
):
    leave = pltpu.make_async_copy(left_ref, res_ref, done)
    leave.start()
    wide = (40, 128)
    lane, row = lanes_of(wide), rows_of(wide)
    odd_lane, odd_row = (lane & 1) == 1, (row & 1) == 1

    def spread(value, part, odd_l, odd_r):
        keep = odd_l if part % 2 else ~odd_l
        value = jnp.where(keep, value, roll(value, -1 if part % 2 else 1, 1))
        keep = odd_r if part // 2 else ~odd_r
        return jnp.where(keep, value, roll(value, -1 if part // 2 else 1, 0))

    def far(n):
        return max(0, 7 - n, n - 14)

    for n in range(22):
        away = far(n)
        if away == 0:
            t = n - 7
            Q[n] = mid_ref[t]
            cols, over = slice(0, 40), mid_ref[8 + t // 4]
        else:
            ref, t = (above_ref, n + 1) if n < 7 else (below_ref, n - 15)
            tiles = range(5) if away < 3 else range(1, 4)
            first = 5 * (away - 1) if away < 3 else 10 + 3 * (away - 3) - 1
            for j in tiles:
                Q[n, 8 * j : 8 * j + 8] = ref[first + j]
            cols = slice(8 * tiles[0], 8 * tiles[-1] + 8)
            over = [ref[25 + 5 * (t // 4) + j] for j in tiles]
            over = jnp.concatenate(over, axis=0)
        CV[n, cols] = spread(Q[n, cols], 3, odd_lane[cols], odd_row[cols])
        DV[n, cols] = 0.125 * spread(over, t % 4, odd_lane[cols], odd_row[cols])

    def span(reach):
        return slice(0, 40) if reach > 3 else slice(8, 32)

    for n in range(1, 21):
        cols = span(6 - far(n))
        edge = lane[cols]
        visc, over = CV[n, cols], DV[n, cols]
        AN[n, cols] = over * (visc + CV[n - 1, cols])
        AS[n, cols] = over * (visc + CV[n + 1, cols])
        AW[n, cols] = over * (visc + roll(visc, 2, 0))
        AE[n, cols] = over * (visc + roll(visc, -2, 0))
        AD[n, cols] = jnp.where(edge < 2, 0.0, over * (visc + roll(visc, 2, 1)))
        AU[n, cols] = jnp.where(edge >= 126, 0.0, over * (visc + roll(visc, -2, 1)))

    for turn in range(1, COARSE):
        old = Q if turn == 1 else E.at[turn % 2]
        new = E.at[(turn + 1) % 2]
        for n in range(turn, 22 - turn):
            cols = span(7 - turn - far(n))
            here = old[n, cols]
            total = Q[n, cols] + (1.0 - RELAX) * here
            total = total + AN[n, cols] * old[n - 1, cols]
            total = total + AS[n, cols] * old[n + 1, cols]
            total = total + AW[n, cols] * roll(here, 2, 0)
            total = total + AE[n, cols] * roll(here, -2, 0)
            total = total + AD[n, cols] * roll(here, 2, 1)
            new[n, cols] = total + AU[n, cols] * roll(here, -2, 1)

    final = E.at[COARSE % 2]
    tile = (8, 128)
    lane8, row8 = lanes_of(tile), rows_of(tile)
    odd_lane8, odd_row8 = (lane8 & 1) == 1, (row8 & 1) == 1
    for k in range(8):
        value = final[7 + k, 16:24]
        for comp in range(3):
            error = spread(value, comp, odd_lane8, odd_row8)
            for r in (2 * k, 2 * k + 1):
                out_ref[comp, r] = smooth_ref[comp, r] + error
    leave.wait()


def wanted_cells(lats, lons, lon):
    dest = jnp.arange(lats, dtype=jnp.int32)[:, None]
    position = jnp.arange(CELLS, dtype=jnp.int32)[None, :]
    rows, cols = lats * 16, lons * 8
    edge = (lon == 0) | (lon == lons - 1)
    side_row = dest * 16 + position - 4
    on_side = edge & (position < 24) & (side_row >= 0) & (side_row < rows)
    side = 2 * cols + jnp.where(lon == 0, 0, rows) + jnp.clip(side_row, 0, rows - 1)
    along = jnp.where((dest == 0) & (position < 4), position, position - 20)
    corner_col = jnp.where(lon == 0, along, lon * 8 + along - 4)
    col = jnp.where(edge, corner_col, lon * 8 + position - 4)
    row_cell = jnp.where(dest == 0, 0, cols) + jnp.clip(col, 0, cols - 1)
    return jnp.where(on_side, side, row_cell)


def per_device(velocity, forcing, viscosity, ghost_slots, corner_rows, corner_cols, corner_weights):
    v, f, mu = velocity[0], forcing[0], viscosity[0]
    lats, lons = lax.axis_size("lat"), lax.axis_size("lon")
    params = pltpu.CompilerParams(vmem_limit_bytes=32 * 2**20)
    f32 = jnp.float32

    def kernel(body, shapes, specs):
        return pl.pallas_call(
            body,
            out_shape=[jax.ShapeDtypeStruct(shape, f32) for shape in shapes],
            in_specs=specs,
            out_specs=[VMEM] * len(shapes),
            compiler_params=params,
        )

    weights = jnp.transpose(corner_weights, (0, 3, 1, 2))[0]
    shapes = ((3, 16, 128), (3, 8, 128), (3, 128), (88, 128))
    edge, first_row, first_cell, blended = pl.pallas_call(
        first_kernel,
        out_shape=[jax.ShapeDtypeStruct(shape, f32) for shape in shapes],
        in_specs=[pl.BlockSpec(memory_space=pltpu.HBM)] * 4,
        out_specs=[VMEM] * 4,
        scratch_shapes=[
            pltpu.SMEM((1, 3), jnp.int32),
            pltpu.SMEM((1, 3), jnp.int32),
            pltpu.SMEM((3, 1, 4), f32),
            pltpu.VMEM(v.shape, f32),
            pltpu.SemaphoreType.DMA((4,)),
        ],
        compiler_params=params,
        name="first",
    )(
        *(
            pltpu.with_memory_space_constraint(operand, pltpu.HBM)
            for operand in (corner_rows[0], corner_cols[0], weights, v)
        )
    )
    first_cell = shifted(first_cell, -1, -1, 1)
    first_row = shifted(first_row, -1, 0, 1)
    edge = shifted(edge, 0, -1, 1)
    blended = shifted(blended, 0, 0, 1)
    (values,) = kernel(interp_kernel, ((9 * lons, 1, 128),), [VMEM] * 4)(
        blended, edge, first_row, first_cell
    )
    around = lax.all_to_all(values.reshape(lons, 1, 1152), "lon", 0, 0, tiled=True)
    to_above, to_below = kernel(cut_kernel, ((32, 8, 128),) * 2, [VMEM] * 3)(v, f, mu)
    slots, lat_at, lon_at, to_above = lax.optimization_barrier(
        (ghost_slots, lax.axis_index("lat"), lax.axis_index("lon"), to_above)
    )
    slots = slots[0]
    place = jnp.stack([lat_at, lon_at, jnp.int32(lats - 1), jnp.int32(lons - 1)])
    source_rows = ((slots // 3) % lons) * 9 + (slots % 3) * 3
    ghost_rows = (slots // (3 * lons)) * (3 * CELLS)
    cells = wanted_cells(lats, lons, lon_at).reshape(-1)
    below = shifted(to_above, -1, 0)
    above = shifted(to_below, 1, 0)

    chosen = pl.pallas_call(
        pick_kernel,
        out_shape=jax.ShapeDtypeStruct((lats * 3 * CELLS, 1, 128), f32),
        in_specs=[SMEM, SMEM, SMEM, VMEM],
        out_specs=VMEM,
        compiler_params=params,
        name="pick",
    )(place, cells, source_rows, around.reshape(lons * 9, 1, 128))
    everything = lax.all_to_all(chosen.reshape(lats, 3 * CELLS, 128), "lat", 0, 0, tiled=True)
    everything = everything.reshape(lats * 3 * CELLS, 1, 128)
    to_right, to_left = kernel(pack_kernel, ((92, 8, 128),) * 2, [VMEM] * 5)(v, f, mu, above, below)
    left = shifted(to_right, 0, 1)
    right = shifted(to_left, 0, -1)

    block = jax.ShapeDtypeStruct((3, 16, 8, 128), f32)
    field = (3, 28, 24, 128)
    residual, smoothed, message = pl.pallas_call(
        smooth_kernel,
        out_shape=(block, block, jax.ShapeDtypeStruct((10, 8, 128), f32)),
        in_specs=[SMEM, SMEM] + [VMEM] * 8,
        out_specs=(VMEM, VMEM, VMEM),
        scratch_shapes=[pltpu.VMEM(field, f32)] * 3
        + [
            pltpu.VMEM(shape, f32)
            for shape in ((6, 28, 24, 128), (16, 8, 128), (8, 8, 128), (8, 8, 128), (28, 24, 128))
        ],
        compiler_params=params,
        name="smooth",
    )(place, ghost_rows, v, f, mu, left, right, above, below, everything)

    tiles = [
        shifted(message, 0, 2),
        shifted(message, 0, 1),
        message,
        shifted(message, 0, -1),
        shifted(message, 0, -2),
    ]
    band = jnp.concatenate(tiles, axis=1)
    tile_list = (-1, 8, 128)
    inverse = band[8:10].reshape(tile_list)
    to_above = [band[0:2].reshape(tile_list), band[2:7, 8:32].reshape(tile_list), inverse]
    to_below = [band[7:8], band[6:7]] + [band[r : r + 1, 8:32] for r in (5, 4, 3, 2, 1)]
    to_below = [part.reshape(tile_list) for part in to_below] + [inverse]
    band_below = shifted(jnp.concatenate(to_above, axis=0), -1, 0)
    band_above = shifted(jnp.concatenate(to_below, axis=0), 1, 0)
    coarse = pltpu.VMEM((22, 40, 128), f32)
    new, residual = pl.pallas_call(
        coarse_kernel,
        out_shape=(block, block),
        in_specs=[VMEM] * 5,
        out_specs=(VMEM, pl.BlockSpec(memory_space=pl.ANY)),
        scratch_shapes=[pltpu.SemaphoreType.DMA(()), coarse, coarse, coarse]
        + [pltpu.VMEM((2, 22, 40, 128), f32)]
        + [coarse] * 6,
        compiler_params=params,
        name="coarse",
    )(band, band_above, band_below, smoothed, residual)
    return new[None], residual[None]


def solution(mesh):
    placed = (
        P("patch", None, "lat", "lon", None),
        P("patch", None, "lat", "lon", None),
        P("patch", "lat", "lon", None),
        P("patch", None),
        P("patch", "lat", "lon"),
        P("patch", "lat", "lon"),
        P("patch", "lat", None, "lon"),
    )
    return jax.shard_map(
        per_device,
        mesh=mesh,
        in_specs=placed,
        out_specs=(P("patch", None, "lat", "lon", None), P("patch", None, "lat", "lon", None)),
        check_vma=False,
    )
```

```python
import jax
import jax.numpy as jnp
from jax import lax
from jax.experimental import pallas as pl
from jax.experimental.pallas import tpu as pltpu
from jax.sharding import PartitionSpec as P


AXES = ("patch", "lat", "lon")
RELAX = 0.8
COARSE = 8
PAD = 6
CELLS = 32
OUTER = (-3, -4, 18, 19)
VMEM = pl.BlockSpec(memory_space=pltpu.VMEM)
SMEM = pl.BlockSpec(memory_space=pltpu.SMEM)


def shifted(value, by_lat, by_lon, flip=0):
    patches, lats, lons = (lax.axis_size(axis) for axis in AXES)
    pairs = []
    for p in range(patches):
        for a in range(lats):
            for b in range(lons):
                a2, b2 = a + by_lat, b + by_lon
                if 0 <= a2 < lats and 0 <= b2 < lons:
                    pairs.append(((p * lats + a) * lons + b, ((p ^ flip) * lats + a2) * lons + b2))
    return lax.ppermute(value, AXES, pairs)


def lanes_of(shape):
    return lax.broadcasted_iota(jnp.int32, shape, len(shape) - 1)


def rows_of(shape):
    return lax.broadcasted_iota(jnp.int32, shape, len(shape) - 2)


def roll(value, by, axis):
    return pltpu.roll(value, by % value.shape[axis], axis)


def lane_partner(value, odd_lane):
    return jnp.where(odd_lane, roll(value, 1, 1), roll(value, -1, 1))


def row_partner(value, odd_row):
    return jnp.where(odd_row, roll(value, 1, 0), roll(value, -1, 0))


def first_kernel(
    rows_hbm, cols_hbm, weights_hbm, v_hbm, slot_hbm,
    edge_ref, below_ref, corner_ref, blend_ref, source_ref, ghost_ref,
    rows_ref, cols_ref, weights_ref, v_ref, slot_ref, done,
):
    sub = rows_of((8, 128))
    pairs = (v_hbm, v_ref), (rows_hbm, rows_ref), (cols_hbm, cols_ref), (weights_hbm, weights_ref)
    pairs = pairs + ((slot_hbm, slot_ref),)
    copies = [pltpu.make_async_copy(*pair, done.at[n]) for n, pair in enumerate(pairs)]
    for copy in copies:
        copy.start()
    for copy in copies:
        copy.wait()
    slots = slot_ref[...]
    third = (slots * 21846) >> 16
    source_ref[...] = (third & 31) * 9 + (slots - 3 * third) * 3
    ghost_ref[...] = (third >> 5) * (3 * CELLS)
    blend(rows_ref, cols_ref, weights_ref, v_ref, blend_ref)
    for comp in range(3):
        corner_ref[comp : comp + 1] = v_ref[comp, 0, 0:1]
        below_ref[comp] = v_ref[comp, 0]
        for j in range(2):
            first = v_ref[comp, 8 * j]
            for r in range(1, 8):
                first = jnp.where(sub == r, roll(v_ref[comp, 8 * j + r], r, 0), first)
            edge_ref[comp, 8 * j : 8 * j + 8] = first


def lat_tile(field, away):
    if 3 <= field < 6:
        return 20 + 4 * (field - 3) + away - 1
    return 5 * min(field, 3) + away - 1


def cut_kernel(
    place_ref, v_ref, f_ref, mu_ref, up_ref, down_ref, cells_ref
):
    cells_ref[...] = wanted_cells(place_ref)
    for field in range(7):
        for away in range(1, 5 if 3 <= field < 6 else 6):
            for ref, r in ((up_ref, away - 1), (down_ref, 16 - away)):
                if field == 6:
                    value = mu_ref[r]
                else:
                    value = v_ref[field, r] if field < 3 else f_ref[field - 3, r]
                ref[lat_tile(field, away)] = value


def blend(rows_ref, cols_ref, weights_ref, v_ref, out_ref):
    tall, flat = rows_of((16, 128)), rows_of((8, 128))
    for slot in range(3):
        row, col = rows_ref[0, slot], cols_ref[0, slot]
        w0, w1, w2, w3 = (weights_ref[slot, 0, k] for k in range(4))
        here, next_one = flat == col, flat == col + 1
        upper = jnp.where(here, w0, jnp.where(next_one, w2, 0.0))
        lower = jnp.where(here, w1, jnp.where(next_one, w3, 0.0))
        within = row < 15
        next_row = jnp.where(within, row + 1, row)
        inner = jnp.where(within, lower, 0.0)
        for comp in range(3):
            total = upper * v_ref[comp, row] + inner * v_ref[comp, next_row]
            at = 3 * slot + comp
            out_ref[at : at + 1] = jnp.sum(total, axis=0, keepdims=True)
        beside = jnp.where(tall == row, w2, jnp.where(tall == row + 1, w3, 0.0))
        out_ref[16 + 16 * slot : 32 + 16 * slot] = jnp.where(col == 7, beside, 0.0)
        out_ref[64 + 8 * slot : 72 + 8 * slot] = jnp.where(within, 0.0, lower)
        both = jnp.where((row == 15) & (col == 7), w3, 0.0)
        out_ref[9 + slot : 10 + slot] = jnp.full((1, 128), both, jnp.float32)
    out_ref[12:16] = jnp.zeros((4, 128), jnp.float32)


def interp_kernel(blend_ref, edge_ref, below_ref, corner_ref, out_ref):
    for slot in range(3):
        edge_w = blend_ref[16 + 16 * slot : 32 + 16 * slot]
        below_w = blend_ref[64 + 8 * slot : 72 + 8 * slot]
        corner_w = blend_ref[9 + slot : 10 + slot]
        for comp in range(3):
            at = 3 * slot + comp
            beside = edge_w * edge_ref[comp]
            total = beside[0:8] + beside[8:16] + below_w * below_ref[comp]
            total = jnp.sum(total, axis=0, keepdims=True) + blend_ref[at : at + 1]
            total = total + corner_w * corner_ref[comp : comp + 1]
            for dest in range(out_ref.shape[0] // 9):
                out_ref[9 * dest + at] = total


def pick_kernel(place_ref, cells_ref, source_ref, row_ref, out_ref):
    lon, last_lat, last_lon = place_ref[1], place_ref[2], place_ref[3]
    edge = (lon == 0) | (lon == last_lon)

    def copy(dest, position):
        base = source_ref[0, cells_ref[dest, position]]
        for comp in range(3):
            out_ref[dest * 3 * CELLS + position * 3 + comp] = row_ref[base + comp]

    @pl.when(edge)
    def _():
        def step(dest, carry):
            for position in range(CELLS):
                copy(dest, position)
            return carry

        lax.fori_loop(0, last_lat + 1, step, 0)

    @pl.when(~edge)
    def _():
        for position in range(16):
            copy(0, position)
            copy(last_lat, position)


def side_tile(ref, field, r, col, sub):
    if r in OUTER:
        by = 2 * OUTER.index(r)
        return roll(ref[70 + field], by if col == 3 else -by, 0)
    value = ref[10 * field + (r + 2) // 2]
    if r % 2:
        value = roll(value, 4, 0)
    extra = {0: 0, 1: 1, 2: 2, 6: 3}.get(field)
    if extra is None or not 0 <= r < 16:
        return value
    fifth = roll(ref[77 + 2 * extra + r // 8], col - r % 8, 0)
    return jnp.where(sub == col, fifth, value)


def pack_kernel(v_ref, f_ref, mu_ref, above_ref, below_ref, right_ref, left_ref):
    sub = rows_of((8, 128))

    def row(field, r):
        if r < 0:
            return above_ref[lat_tile(field, -r)]
        if r > 15:
            return below_ref[lat_tile(field, r - 15)]
        if field == 6:
            return mu_ref[r]
        return v_ref[field, r] if field < 3 else f_ref[field - 3, r]

    for field in range(7):
        for t in range(10):
            even, odd = row(field, 2 * t - 2), roll(row(field, 2 * t - 1), 4, 0)
            right_ref[10 * field + t] = jnp.where(sub < 4, odd, even)
            left_ref[10 * field + t] = jnp.where(sub < 4, even, odd)
        high = low = row(field, OUTER[0])
        for k in range(1, 4):
            value = row(field, OUTER[k])
            high = jnp.where((sub >> 1) == 3 - k, roll(value, -2 * k, 0), high)
            low = jnp.where((sub >> 1) == k, roll(value, 2 * k, 0), low)
        right_ref[70 + field] = high
        left_ref[70 + field] = low
    for n, field in enumerate((0, 1, 2, 6)):
        for j in range(2):
            third = fourth = row(field, 8 * j)
            for r in range(8):
                value = row(field, 8 * j + r)
                third = jnp.where(sub == r, roll(value, r - 3, 0), third)
                fourth = jnp.where(sub == r, roll(value, r - 4, 0), fourth)
            right_ref[77 + 2 * n + j] = third
            left_ref[77 + 2 * n + j] = fourth


def prepare(
    place_ref, f_ref, mu_ref, left_ref, right_ref, above_ref, below_ref,
    F, C, DG, over_ref, visc_ref, MU,
):
    lat, lon = place_ref[0], place_ref[1]
    last_lat, last_lon = place_ref[2], place_ref[3]
    wide = (24, 128)
    lane, row = lanes_of(wide), rows_of(wide)
    odd_lane, odd_row = (lane & 1) == 1, (row & 1) == 1
    own = slice(PAD, PAD + 16)
    sub = rows_of((8, 128))
    MU[own, 8:16] = mu_ref[...]
    for r in range(-4, 20):
        MU[r + PAD, 0:8] = side_tile(left_ref, 6, r, 3, sub)
        MU[r + PAD, 16:24] = side_tile(right_ref, 6, r, 4, sub)
    for away in range(1, 6):
        for i, ref in ((PAD - away, above_ref), (PAD + 15 + away, below_ref)):
            value = ref[lat_tile(6, away)]
            MU[i, 8:16] = value
            if away == 5:
                MU[i, 0:8] = MU[i, 16:24] = value

    @pl.when(lat == 0)
    def _():
        MU[4] = MU[6]
        MU[5] = MU[6]

    @pl.when(lat == last_lat)
    def _():
        MU[22] = MU[21]
        MU[23] = MU[21]

    @pl.when(lon == 0)
    def _():
        for i in range(1, 27):
            MU[i, 0:8] = jnp.broadcast_to(MU[i, 8:9], (8, 128))

    @pl.when(lon == last_lon)
    def _():
        for i in range(1, 27):
            MU[i, 16:24] = jnp.broadcast_to(MU[i, 15:16], (8, 128))

    for i in range(2, 26):
        mid = MU[i]
        north = 0.5 * (mid + MU[i - 1])
        south = 0.5 * (mid + MU[i + 1])
        west = 0.5 * (mid + roll(mid, 1, 0))
        east = 0.5 * (mid + roll(mid, -1, 0))
        down = 0.5 * (mid + jnp.where(lane == 0, mid, roll(mid, 1, 1)))
        up = 0.5 * (mid + jnp.where(lane == 127, mid, roll(mid, -1, 1)))
        total = north + south + west + east + down + up
        inverse = 1.0 / total
        C[0, i] = north * inverse
        C[1, i] = south * inverse
        C[2, i] = west * inverse
        C[3, i] = east * inverse
        C[4, i] = jnp.where(lane == 0, 0.0, down * inverse)
        C[5, i] = jnp.where(lane == 127, 0.0, up * inverse)
        r = i - PAD
        if 0 <= r < 16:
            DG[r] = total[8:16]
        for comp in range(3):
            if 0 <= r < 16:
                force = f_ref[comp, r]
            else:
                ref, away = (above_ref, -r) if r < 0 else (below_ref, r - 15)
                force = ref[lat_tile(3 + comp, away)]
            F[comp, i, 0:8] = side_tile(left_ref, 3 + comp, r, 3, sub) * inverse[0:8]
            F[comp, i, 8:16] = force * inverse[8:16]
            F[comp, i, 16:24] = side_tile(right_ref, 3 + comp, r, 4, sub) * inverse[16:24]

    def coarse_visc(i):
        both = MU[i] + MU[i + 1]
        flat = 0.25 * (both + row_partner(both, odd_row))
        return flat, 0.5 * (flat + lane_partner(flat, odd_lane))

    layers = [coarse_visc(PAD + 2 * k) for k in (-1, 0)]
    for k in range(8):
        layers.append(coarse_visc(PAD + 2 * k + 2))
        before, (flat, visc), after = layers[k][1], layers[k + 1], layers[k + 2][1]
        edge_down = jnp.where(lane == 0, flat, roll(flat, 1, 1))
        edge_up = jnp.where(lane == 127, flat, roll(flat, -1, 1))
        total = 6.0 * visc + before + after + roll(visc, 2, 0) + roll(visc, -2, 0)
        total = total + jnp.where(lane < 2, edge_down, roll(visc, 2, 1))
        total = total + jnp.where(lane >= 126, edge_up, roll(visc, -2, 1))
        over_ref[k] = RELAX / (0.125 * total[8:16])
        visc_ref[k] = visc[8:16]


def smooth_kernel(
    place_ref, ghost_ref, v_ref, f_ref, mu_ref, left_ref, right_ref, above_ref, below_ref, slot_ref,
    res_ref, smooth_ref, message_ref, A, B, F, C, DG, over_ref, visc_ref, MU,
):
    lat, lon = place_ref[0], place_ref[1]
    last_lat, last_lon = place_ref[2], place_ref[3]
    wide = (24, 128)
    lane, row = lanes_of(wide), rows_of(wide)
    sub = rows_of((8, 128))
    own = slice(PAD, PAD + 16)

    for comp in range(3):
        A[comp, own, 8:16] = v_ref[comp]
        for r in range(-4, 20):
            A[comp, r + PAD, 0:8] = side_tile(left_ref, comp, r, 3, sub)
            A[comp, r + PAD, 16:24] = side_tile(right_ref, comp, r, 4, sub)
        for away in range(1, 6):
            for i, ref in ((PAD - away, above_ref), (PAD + 15 + away, below_ref)):
                value = ref[lat_tile(comp, away)]
                A[comp, i, 8:16] = value
                if away == 5:
                    A[comp, i, 0:8] = A[comp, i, 16:24] = value

    edge = (lon == 0) | (lon == last_lon)
    all_cols, all_rows = (last_lon + 1) * 8, (last_lat + 1) * 16

    def fill_row(i, start):
        for col in range(-4, 12):
            along = jnp.where(lon == 0, col, col + 4)
            packed_at = jnp.where((lat == 0) & (along < 4), along, along + 20)
            position = jnp.clip(jnp.where(edge, packed_at, col + 4), 0, CELLS - 1)
            cell = start + jnp.clip(lon * 8 + col, 0, all_cols - 1)
            base = ghost_ref[0, cell] + 3 * position
            for comp in range(3):
                A[comp, i, 8 + col : 9 + col] = slot_ref[base + comp]

    def fill_side(col, start):
        for r in range(-4, 20):
            base = ghost_ref[0, start + jnp.clip(lat * 16 + r, 0, all_rows - 1)] + 3 * (r + 4)
            for comp in range(3):
                A[comp, r + PAD, 8 + col : 9 + col] = slot_ref[base + comp]

    prepare(
        place_ref, f_ref, mu_ref, left_ref, right_ref, above_ref, below_ref,
        F, C, DG, over_ref, visc_ref, MU,
    )
    pl.when(lat == 0)(lambda: fill_row(5, 0))
    pl.when(lat == last_lat)(lambda: fill_row(22, all_cols))
    pl.when(lon == 0)(lambda: fill_side(-1, 2 * all_cols))
    pl.when(lon == last_lon)(lambda: fill_side(8, 2 * all_cols + all_rows))

    inside = ((row >= 8) | (lon > 0)) & ((row < 16) | (lon < last_lon))
    parity = jnp.where(inside, (row + lane) & 1, 2)

    def weighted(source, comp, i, here):
        total = F[comp, i] + C[0, i] * source[comp, i - 1]
        total = total + C[1, i] * source[comp, i + 1]
        total = total + C[2, i] * roll(here, 1, 0)
        total = total + C[3, i] * roll(here, -1, 0)
        total = total + C[4, i] * roll(here, 1, 1)
        return total + C[5, i] * roll(here, -1, 1)

    wanted = {}
    for colour in range(2):
        wanted[colour, "mid"] = jnp.int32(colour)
        wanted[colour, "top"] = jnp.where(lat == 0, 3, colour)
        wanted[colour, "low"] = jnp.where(lat == last_lat, 3, colour)

    def relax(colour, reach, source, target):
        for r in range(-reach, 16 + reach):
            i = r + PAD
            zone = "top" if r < 0 else "low" if r > 15 else "mid"
            mask = parity == wanted[(colour + r) % 2, zone]
            for comp in range(3):
                here = source[comp, i]
                target[comp, i] = jnp.where(mask, weighted(source, comp, i, here), here)

    relax(0, 4, A, B)
    relax(1, 3, B, A)
    relax(0, 2, A, B)
    relax(1, 1, B, A)

    tile = (8, 128)
    lane8, row8 = lanes_of(tile), rows_of(tile)
    odd_lane8, odd_row8 = (lane8 & 1) == 1, (row8 & 1) == 1

    def packed(parts):
        low = jnp.where(odd_lane8, parts[1], parts[0])
        high = jnp.where(odd_lane8, parts[3], parts[2])
        return jnp.where(odd_row8, high, low)

    for k in range(8):
        parts = []
        for comp in range(3):
            rhs = jnp.zeros(tile, jnp.float32)
            for r in (2 * k, 2 * k + 1):
                here = A[comp, r + PAD]
                smooth_ref[comp, r] = here[8:16]
                left = DG[r] * (weighted(A, comp, r + PAD, here) - here)[8:16]
                res_ref[comp, r] = left
                rhs = rhs + left
            rhs = rhs + lane_partner(rhs, odd_lane8)
            rhs = rhs + row_partner(rhs, odd_row8)
            parts.append(0.125 * rhs * over_ref[k])
        message_ref[k] = packed(parts + [visc_ref[k]])
        if k % 4 == 3:
            message_ref[8 + k // 4] = packed([over_ref[j] for j in range(k - 3, k + 1)])


def coarse_kernel(
    mid_ref, above_ref, below_ref, smooth_ref, left_ref, out_ref, res_ref,
    done, Q, CV, DV, E, AN, AS, AW, AE, AD, AU,
):
    leave = pltpu.make_async_copy(left_ref, res_ref, done)
    leave.start()
    wide = (40, 128)
    lane, row = lanes_of(wide), rows_of(wide)
    odd_lane, odd_row = (lane & 1) == 1, (row & 1) == 1

    def spread(value, part, odd_l, odd_r):
        keep = odd_l if part % 2 else ~odd_l
        value = jnp.where(keep, value, roll(value, -1 if part % 2 else 1, 1))
        keep = odd_r if part // 2 else ~odd_r
        return jnp.where(keep, value, roll(value, -1 if part // 2 else 1, 0))

    def far(n):
        return max(0, 7 - n, n - 14)

    for n in range(22):
        away = far(n)
        if away == 0:
            t = n - 7
            Q[n] = mid_ref[t]
            cols, over = slice(0, 40), mid_ref[8 + t // 4]
        else:
            ref, t = (above_ref, n + 1) if n < 7 else (below_ref, n - 15)
            tiles = range(5) if away < 3 else range(1, 4)
            first = 5 * (away - 1) if away < 3 else 10 + 3 * (away - 3) - 1
            for j in tiles:
                Q[n, 8 * j : 8 * j + 8] = ref[first + j]
            cols = slice(8 * tiles[0], 8 * tiles[-1] + 8)
            over = [ref[25 + 5 * (t // 4) + j] for j in tiles]
            over = jnp.concatenate(over, axis=0)
        CV[n, cols] = spread(Q[n, cols], 3, odd_lane[cols], odd_row[cols])
        DV[n, cols] = 0.125 * spread(over, t % 4, odd_lane[cols], odd_row[cols])

    def span(reach):
        return slice(0, 40) if reach > 3 else slice(8, 32)

    for n in range(1, 21):
        cols = span(6 - far(n))
        edge = lane[cols]
        visc, over = CV[n, cols], DV[n, cols]
        AN[n, cols] = over * (visc + CV[n - 1, cols])
        AS[n, cols] = over * (visc + CV[n + 1, cols])
        AW[n, cols] = over * (visc + roll(visc, 2, 0))
        AE[n, cols] = over * (visc + roll(visc, -2, 0))
        AD[n, cols] = jnp.where(edge < 2, 0.0, over * (visc + roll(visc, 2, 1)))
        AU[n, cols] = jnp.where(edge >= 126, 0.0, over * (visc + roll(visc, -2, 1)))

    for turn in range(1, COARSE):
        old = Q if turn == 1 else E.at[turn % 2]
        new = E.at[(turn + 1) % 2]
        for n in range(turn, 22 - turn):
            cols = span(7 - turn - far(n))
            here = old[n, cols]
            total = Q[n, cols] + (1.0 - RELAX) * here
            total = total + AN[n, cols] * old[n - 1, cols]
            total = total + AS[n, cols] * old[n + 1, cols]
            total = total + AW[n, cols] * roll(here, 2, 0)
            total = total + AE[n, cols] * roll(here, -2, 0)
            total = total + AD[n, cols] * roll(here, 2, 1)
            new[n, cols] = total + AU[n, cols] * roll(here, -2, 1)

    final = E.at[COARSE % 2]
    tile = (8, 128)
    lane8, row8 = lanes_of(tile), rows_of(tile)
    odd_lane8, odd_row8 = (lane8 & 1) == 1, (row8 & 1) == 1
    for k in range(8):
        value = final[7 + k, 16:24]
        for comp in range(3):
            error = spread(value, comp, odd_lane8, odd_row8)
            for r in (2 * k, 2 * k + 1):
                out_ref[comp, r] = smooth_ref[comp, r] + error
    leave.wait()


def wanted_cells(place_ref):
    lon, last_lat, last_lon = place_ref[1], place_ref[2], place_ref[3]
    dest = lax.broadcasted_iota(jnp.int32, (8, CELLS), 0)
    position = lax.broadcasted_iota(jnp.int32, (8, CELLS), 1)
    rows, cols = (last_lat + 1) * 16, (last_lon + 1) * 8
    first = jnp.where(lon == 0, 1, 0)
    edge = jnp.where((lon == 0) | (lon == last_lon), 1, 0)
    side_row = dest * 16 + position - 4
    on_side = (edge > 0) & (position < 24) & (side_row >= 0) & (side_row < rows)
    side = 2 * cols + (1 - first) * rows + jnp.clip(side_row, 0, rows - 1)
    along = jnp.where((dest == 0) & (position < 4), position, position - 20)
    corner_col = along + (1 - first) * (lon * 8 - 4)
    col = edge * corner_col + (1 - edge) * (lon * 8 + position - 4)
    row_cell = jnp.where(dest == 0, 0, cols) + jnp.clip(col, 0, cols - 1)
    return jnp.where(on_side, side, row_cell)


def per_device(velocity, forcing, viscosity, ghost_slots, corner_rows, corner_cols, corner_weights):
    v, f, mu = velocity[0], forcing[0], viscosity[0]
    lats, lons = lax.axis_size("lat"), lax.axis_size("lon")
    params = pltpu.CompilerParams(vmem_limit_bytes=32 * 2**20)
    f32 = jnp.float32

    def kernel(body, shapes, specs):
        return pl.pallas_call(
            body,
            out_shape=[jax.ShapeDtypeStruct(shape, f32) for shape in shapes],
            in_specs=specs,
            out_specs=[VMEM] * len(shapes),
            compiler_params=params,
        )

    weights = jnp.transpose(corner_weights, (0, 3, 1, 2))[0]
    shapes = ((3, 16, 128), (3, 8, 128), (3, 128), (88, 128))
    edge, first_row, first_cell, blended, source_rows, ghost_rows = pl.pallas_call(
        first_kernel,
        out_shape=[jax.ShapeDtypeStruct(shape, f32) for shape in shapes]
        + [jax.ShapeDtypeStruct(ghost_slots.shape, jnp.int32)] * 2,
        in_specs=[pl.BlockSpec(memory_space=pltpu.HBM)] * 5,
        out_specs=[VMEM] * 6,
        scratch_shapes=[
            pltpu.SMEM((1, 3), jnp.int32),
            pltpu.SMEM((1, 3), jnp.int32),
            pltpu.SMEM((3, 1, 4), f32),
            pltpu.VMEM(v.shape, f32),
            pltpu.VMEM(ghost_slots.shape, jnp.int32),
            pltpu.SemaphoreType.DMA((5,)),
        ],
        compiler_params=params,
        name="first",
    )(
        *(
            pltpu.with_memory_space_constraint(operand, pltpu.HBM)
            for operand in (corner_rows[0], corner_cols[0], weights, v, ghost_slots)
        )
    )
    first_cell = shifted(first_cell, -1, -1, 1)
    first_row = shifted(first_row, -1, 0, 1)
    edge = shifted(edge, 0, -1, 1)
    blended = shifted(blended, 0, 0, 1)
    (values,) = kernel(interp_kernel, ((9 * lons, 1, 128),), [VMEM] * 4)(
        blended, edge, first_row, first_cell
    )
    around = lax.all_to_all(values.reshape(lons, 1, 1152), "lon", 0, 0, tiled=True)
    place = jnp.stack(
        [lax.axis_index("lat"), lax.axis_index("lon"), jnp.int32(lats - 1), jnp.int32(lons - 1)]
    )
    to_above, to_below, cells = pl.pallas_call(
        cut_kernel,
        out_shape=[jax.ShapeDtypeStruct((32, 8, 128), f32)] * 2
        + [jax.ShapeDtypeStruct((lats, CELLS), jnp.int32)],
        in_specs=[SMEM] + [VMEM] * 3,
        out_specs=[VMEM] * 3,
        compiler_params=params,
        name="cut",
    )(place, v, f, mu)
    below = shifted(to_above, -1, 0)
    above = shifted(to_below, 1, 0)

    chosen = pl.pallas_call(
        pick_kernel,
        out_shape=jax.ShapeDtypeStruct((lats * 3 * CELLS, 1, 128), f32),
        in_specs=[SMEM, SMEM, SMEM, VMEM],
        out_specs=VMEM,
        compiler_params=params,
        name="pick",
    )(place, cells, source_rows, around.reshape(lons * 9, 1, 128))
    everything = lax.all_to_all(chosen.reshape(lats, 3 * CELLS, 128), "lat", 0, 0, tiled=True)
    everything = everything.reshape(lats * 3 * CELLS, 1, 128)
    to_right, to_left = kernel(pack_kernel, ((85, 8, 128),) * 2, [VMEM] * 5)(v, f, mu, above, below)
    left = shifted(to_right, 0, 1)
    right = shifted(to_left, 0, -1)

    block = jax.ShapeDtypeStruct((3, 16, 8, 128), f32)
    field = (3, 28, 24, 128)
    residual, smoothed, message = pl.pallas_call(
        smooth_kernel,
        out_shape=(block, block, jax.ShapeDtypeStruct((10, 8, 128), f32)),
        in_specs=[SMEM, SMEM] + [VMEM] * 8,
        out_specs=(VMEM, VMEM, VMEM),
        scratch_shapes=[pltpu.VMEM(field, f32)] * 3
        + [
            pltpu.VMEM(shape, f32)
            for shape in ((6, 28, 24, 128), (16, 8, 128), (8, 8, 128), (8, 8, 128), (28, 24, 128))
        ],
        compiler_params=params,
        name="smooth",
    )(place, ghost_rows, v, f, mu, left, right, above, below, everything)

    tiles = [
        shifted(message, 0, 2),
        shifted(message, 0, 1),
        message,
        shifted(message, 0, -1),
        shifted(message, 0, -2),
    ]
    band = jnp.concatenate(tiles, axis=1)
    tile_list = (-1, 8, 128)
    inverse = band[8:10].reshape(tile_list)
    to_above = [band[0:2].reshape(tile_list), band[2:7, 8:32].reshape(tile_list), inverse]
    to_below = [band[7:8], band[6:7]] + [band[r : r + 1, 8:32] for r in (5, 4, 3, 2, 1)]
    to_below = [part.reshape(tile_list) for part in to_below] + [inverse]
    band_below = shifted(jnp.concatenate(to_above, axis=0), -1, 0)
    band_above = shifted(jnp.concatenate(to_below, axis=0), 1, 0)
    coarse = pltpu.VMEM((22, 40, 128), f32)
    new, residual = pl.pallas_call(
        coarse_kernel,
        out_shape=(block, block),
        in_specs=[VMEM] * 5,
        out_specs=(VMEM, pl.BlockSpec(memory_space=pl.ANY)),
        scratch_shapes=[pltpu.SemaphoreType.DMA(()), coarse, coarse, coarse]
        + [pltpu.VMEM((2, 22, 40, 128), f32)]
        + [coarse] * 6,
        compiler_params=params,
        name="coarse",
    )(band, band_above, band_below, smoothed, residual)
    return new[None], residual[None]


def solution(mesh):
    placed = (
        P("patch", None, "lat", "lon", None),
        P("patch", None, "lat", "lon", None),
        P("patch", "lat", "lon", None),
        P("patch", None),
        P("patch", "lat", "lon"),
        P("patch", "lat", "lon"),
        P("patch", "lat", None, "lon"),
    )
    return jax.shard_map(
        per_device,
        mesh=mesh,
        in_specs=placed,
        out_specs=(P("patch", None, "lat", "lon", None), P("patch", None, "lat", "lon", None)),
        check_vma=False,
    )
```

```python
import jax
import jax.numpy as jnp
from jax import lax
from jax.experimental import pallas as pl
from jax.experimental.pallas import tpu as pltpu
from jax.sharding import PartitionSpec as P


AXES = ("patch", "lat", "lon")
RELAX = 0.8
COARSE = 8
PAD = 6
CELLS = 32
OUTER = (-3, -4, 18, 19)
VMEM = pl.BlockSpec(memory_space=pltpu.VMEM)
SMEM = pl.BlockSpec(memory_space=pltpu.SMEM)


def shifted(value, by_lat, by_lon, flip=0):
    patches, lats, lons = (lax.axis_size(axis) for axis in AXES)
    pairs = []
    for p in range(patches):
        for a in range(lats):
            for b in range(lons):
                a2, b2 = a + by_lat, b + by_lon
                if 0 <= a2 < lats and 0 <= b2 < lons:
                    pairs.append(((p * lats + a) * lons + b, ((p ^ flip) * lats + a2) * lons + b2))
    return lax.ppermute(value, AXES, pairs)


def lanes_of(shape):
    return lax.broadcasted_iota(jnp.int32, shape, len(shape) - 1)


def rows_of(shape):
    return lax.broadcasted_iota(jnp.int32, shape, len(shape) - 2)


def roll(value, by, axis):
    return pltpu.roll(value, by % value.shape[axis], axis)


def lane_partner(value, odd_lane):
    return jnp.where(odd_lane, roll(value, 1, 1), roll(value, -1, 1))


def row_partner(value, odd_row):
    return jnp.where(odd_row, roll(value, 1, 0), roll(value, -1, 0))


def first_kernel(
    rows_hbm, cols_hbm, weights_hbm, v_hbm, slot_hbm,
    edge_ref, below_ref, corner_ref, blend_ref, source_ref, ghost_ref,
    rows_ref, cols_ref, weights_ref, v_ref, slot_ref, done,
):
    sub = rows_of((8, 128))
    pairs = (v_hbm, v_ref), (rows_hbm, rows_ref), (cols_hbm, cols_ref), (weights_hbm, weights_ref)
    pairs = pairs + ((slot_hbm, slot_ref),)
    copies = [pltpu.make_async_copy(*pair, done.at[n]) for n, pair in enumerate(pairs)]
    for copy in copies:
        copy.start()
    for copy in copies:
        copy.wait()
    slots = slot_ref[...]
    third = (slots * 21846) >> 16
    source_ref[...] = (third & 31) * 9 + (slots - 3 * third) * 3
    ghost_ref[...] = (third >> 5) * (3 * CELLS)
    blend(rows_ref, cols_ref, weights_ref, v_ref, blend_ref)
    for comp in range(3):
        corner_ref[comp : comp + 1] = v_ref[comp, 0, 0:1]
        below_ref[comp] = v_ref[comp, 0]
        for j in range(2):
            first = v_ref[comp, 8 * j]
            for r in range(1, 8):
                first = jnp.where(sub == r, roll(v_ref[comp, 8 * j + r], r, 0), first)
            edge_ref[comp, 8 * j : 8 * j + 8] = first


def lat_tile(field, away):
    if 3 <= field < 6:
        return 20 + 4 * (field - 3) + away - 1
    return 5 * min(field, 3) + away - 1


def cut_kernel(v_ref, f_ref, mu_ref, up_ref, down_ref, cells_ref):
    cells_ref[...] = wanted_cells()
    for field in range(7):
        for away in range(1, 5 if 3 <= field < 6 else 6):
            for ref, r in ((up_ref, away - 1), (down_ref, 16 - away)):
                if field == 6:
                    value = mu_ref[r]
                else:
                    value = v_ref[field, r] if field < 3 else f_ref[field - 3, r]
                ref[lat_tile(field, away)] = value


def blend(rows_ref, cols_ref, weights_ref, v_ref, out_ref):
    tall, flat = rows_of((16, 128)), rows_of((8, 128))
    for slot in range(3):
        row, col = rows_ref[0, slot], cols_ref[0, slot]
        w0, w1, w2, w3 = (weights_ref[slot, 0, k] for k in range(4))
        here, next_one = flat == col, flat == col + 1
        upper = jnp.where(here, w0, jnp.where(next_one, w2, 0.0))
        lower = jnp.where(here, w1, jnp.where(next_one, w3, 0.0))
        within = row < 15
        next_row = jnp.where(within, row + 1, row)
        inner = jnp.where(within, lower, 0.0)
        for comp in range(3):
            total = upper * v_ref[comp, row] + inner * v_ref[comp, next_row]
            at = 3 * slot + comp
            out_ref[at : at + 1] = jnp.sum(total, axis=0, keepdims=True)
        beside = jnp.where(tall == row, w2, jnp.where(tall == row + 1, w3, 0.0))
        out_ref[16 + 16 * slot : 32 + 16 * slot] = jnp.where(col == 7, beside, 0.0)
        out_ref[64 + 8 * slot : 72 + 8 * slot] = jnp.where(within, 0.0, lower)
        both = jnp.where((row == 15) & (col == 7), w3, 0.0)
        out_ref[9 + slot : 10 + slot] = jnp.full((1, 128), both, jnp.float32)
    out_ref[12:16] = jnp.zeros((4, 128), jnp.float32)


def interp_kernel(blend_ref, edge_ref, below_ref, corner_ref, out_ref):
    for slot in range(3):
        edge_w = blend_ref[16 + 16 * slot : 32 + 16 * slot]
        below_w = blend_ref[64 + 8 * slot : 72 + 8 * slot]
        corner_w = blend_ref[9 + slot : 10 + slot]
        for comp in range(3):
            at = 3 * slot + comp
            beside = edge_w * edge_ref[comp]
            total = beside[0:8] + beside[8:16] + below_w * below_ref[comp]
            total = jnp.sum(total, axis=0, keepdims=True) + blend_ref[at : at + 1]
            total = total + corner_w * corner_ref[comp : comp + 1]
            for dest in range(out_ref.shape[0] // 9):
                out_ref[9 * dest + at] = total


def pick_kernel(cells_ref, source_ref, row_ref, out_ref, held, done):
    _, lon, last_lat, last_lon = place()
    edge = (lon == 0) | (lon == last_lon)

    def fill(dest, count):
        for position in range(count):
            base = source_ref[0, cells_ref[dest, position]]
            for comp in range(3):
                held[dest, position * 3 + comp] = row_ref[base + comp]
        return leave(dest, count)

    def leave(dest, count):
        rows = pl.ds(0, 3 * count)
        return pltpu.make_async_copy(held.at[dest, rows], out_ref.at[dest, rows], done.at[dest])

    @pl.when(edge)
    def _():
        for dest in range(last_lat + 1):
            fill(dest, CELLS).start()
        for dest in range(last_lat + 1):
            leave(dest, CELLS).wait()

    @pl.when(~edge)
    def _():
        copies = [fill(dest, 16) for dest in (0, last_lat)]
        for copy in copies:
            copy.start()
        for copy in copies:
            copy.wait()


def side_tile(ref, field, r, col, sub):
    if r in OUTER:
        by = 2 * OUTER.index(r)
        return roll(ref[70 + field], by if col == 3 else -by, 0)
    value = ref[10 * field + (r + 2) // 2]
    if r % 2:
        value = roll(value, 4, 0)
    extra = {0: 0, 1: 1, 2: 2, 6: 3}.get(field)
    if extra is None or not 0 <= r < 16:
        return value
    fifth = roll(ref[77 + 2 * extra + r // 8], col - r % 8, 0)
    return jnp.where(sub == col, fifth, value)


def pack_kernel(v_ref, f_ref, mu_ref, above_ref, below_ref, right_ref, left_ref):
    sub = rows_of((8, 128))

    def row(field, r):
        if r < 0:
            return above_ref[lat_tile(field, -r)]
        if r > 15:
            return below_ref[lat_tile(field, r - 15)]
        if field == 6:
            return mu_ref[r]
        return v_ref[field, r] if field < 3 else f_ref[field - 3, r]

    for field in range(7):
        for t in range(10):
            even, odd = row(field, 2 * t - 2), roll(row(field, 2 * t - 1), 4, 0)
            right_ref[10 * field + t] = jnp.where(sub < 4, odd, even)
            left_ref[10 * field + t] = jnp.where(sub < 4, even, odd)
        high = low = row(field, OUTER[0])
        for k in range(1, 4):
            value = row(field, OUTER[k])
            high = jnp.where((sub >> 1) == 3 - k, roll(value, -2 * k, 0), high)
            low = jnp.where((sub >> 1) == k, roll(value, 2 * k, 0), low)
        right_ref[70 + field] = high
        left_ref[70 + field] = low
    for n, field in enumerate((0, 1, 2, 6)):
        for j in range(2):
            third = fourth = row(field, 8 * j)
            for r in range(8):
                value = row(field, 8 * j + r)
                third = jnp.where(sub == r, roll(value, r - 3, 0), third)
                fourth = jnp.where(sub == r, roll(value, r - 4, 0), fourth)
            right_ref[77 + 2 * n + j] = third
            left_ref[77 + 2 * n + j] = fourth


def prepare(
    f_ref, mu_ref, left_ref, right_ref, above_ref, below_ref,
    F, C, DG, over_ref, visc_ref, MU,
):
    lat, lon, last_lat, last_lon = place()
    wide = (24, 128)
    lane, row = lanes_of(wide), rows_of(wide)
    odd_lane, odd_row = (lane & 1) == 1, (row & 1) == 1
    own = slice(PAD, PAD + 16)
    sub = rows_of((8, 128))
    MU[own, 8:16] = mu_ref[...]
    for r in range(-4, 20):
        MU[r + PAD, 0:8] = side_tile(left_ref, 6, r, 3, sub)
        MU[r + PAD, 16:24] = side_tile(right_ref, 6, r, 4, sub)
    for away in range(1, 6):
        for i, ref in ((PAD - away, above_ref), (PAD + 15 + away, below_ref)):
            value = ref[lat_tile(6, away)]
            MU[i, 8:16] = value
            if away == 5:
                MU[i, 0:8] = MU[i, 16:24] = value

    @pl.when(lat == 0)
    def _():
        MU[4] = MU[6]
        MU[5] = MU[6]

    @pl.when(lat == last_lat)
    def _():
        MU[22] = MU[21]
        MU[23] = MU[21]

    @pl.when(lon == 0)
    def _():
        for i in range(1, 27):
            MU[i, 0:8] = jnp.broadcast_to(MU[i, 8:9], (8, 128))

    @pl.when(lon == last_lon)
    def _():
        for i in range(1, 27):
            MU[i, 16:24] = jnp.broadcast_to(MU[i, 15:16], (8, 128))

    for i in range(2, 26):
        mid = MU[i]
        north = 0.5 * (mid + MU[i - 1])
        south = 0.5 * (mid + MU[i + 1])
        west = 0.5 * (mid + roll(mid, 1, 0))
        east = 0.5 * (mid + roll(mid, -1, 0))
        down = 0.5 * (mid + jnp.where(lane == 0, mid, roll(mid, 1, 1)))
        up = 0.5 * (mid + jnp.where(lane == 127, mid, roll(mid, -1, 1)))
        total = north + south + west + east + down + up
        inverse = 1.0 / total
        C[0, i] = north * inverse
        C[1, i] = south * inverse
        C[2, i] = west * inverse
        C[3, i] = east * inverse
        C[4, i] = jnp.where(lane == 0, 0.0, down * inverse)
        C[5, i] = jnp.where(lane == 127, 0.0, up * inverse)
        r = i - PAD
        if 0 <= r < 16:
            DG[r] = total[8:16]
        for comp in range(3):
            if 0 <= r < 16:
                force = f_ref[comp, r]
            else:
                ref, away = (above_ref, -r) if r < 0 else (below_ref, r - 15)
                force = ref[lat_tile(3 + comp, away)]
            F[comp, i, 0:8] = side_tile(left_ref, 3 + comp, r, 3, sub) * inverse[0:8]
            F[comp, i, 8:16] = force * inverse[8:16]
            F[comp, i, 16:24] = side_tile(right_ref, 3 + comp, r, 4, sub) * inverse[16:24]

    def coarse_visc(i):
        both = MU[i] + MU[i + 1]
        flat = 0.25 * (both + row_partner(both, odd_row))
        return flat, 0.5 * (flat + lane_partner(flat, odd_lane))

    layers = [coarse_visc(PAD + 2 * k) for k in (-1, 0)]
    for k in range(8):
        layers.append(coarse_visc(PAD + 2 * k + 2))
        before, (flat, visc), after = layers[k][1], layers[k + 1], layers[k + 2][1]
        edge_down = jnp.where(lane == 0, flat, roll(flat, 1, 1))
        edge_up = jnp.where(lane == 127, flat, roll(flat, -1, 1))
        total = 6.0 * visc + before + after + roll(visc, 2, 0) + roll(visc, -2, 0)
        total = total + jnp.where(lane < 2, edge_down, roll(visc, 2, 1))
        total = total + jnp.where(lane >= 126, edge_up, roll(visc, -2, 1))
        over_ref[k] = RELAX / (0.125 * total[8:16])
        visc_ref[k] = visc[8:16]


def smooth_kernel(
    ghost_ref, v_ref, f_ref, mu_ref, left_ref, right_ref, above_ref, below_ref, slot_ref,
    res_ref, smooth_ref, message_ref, A, B, F, C, DG, over_ref, visc_ref, MU,
):
    lat, lon, last_lat, last_lon = place()
    wide = (24, 128)
    lane, row = lanes_of(wide), rows_of(wide)
    sub = rows_of((8, 128))
    own = slice(PAD, PAD + 16)

    for comp in range(3):
        A[comp, own, 8:16] = v_ref[comp]
        for r in range(-4, 20):
            A[comp, r + PAD, 0:8] = side_tile(left_ref, comp, r, 3, sub)
            A[comp, r + PAD, 16:24] = side_tile(right_ref, comp, r, 4, sub)
        for away in range(1, 6):
            for i, ref in ((PAD - away, above_ref), (PAD + 15 + away, below_ref)):
                value = ref[lat_tile(comp, away)]
                A[comp, i, 8:16] = value
                if away == 5:
                    A[comp, i, 0:8] = A[comp, i, 16:24] = value

    edge = (lon == 0) | (lon == last_lon)
    all_cols, all_rows = (last_lon + 1) * 8, (last_lat + 1) * 16

    def fill_row(i, start):
        for col in range(-4, 12):
            along = jnp.where(lon == 0, col, col + 4)
            packed_at = jnp.where((lat == 0) & (along < 4), along, along + 20)
            position = jnp.clip(jnp.where(edge, packed_at, col + 4), 0, CELLS - 1)
            cell = start + jnp.clip(lon * 8 + col, 0, all_cols - 1)
            base = ghost_ref[0, cell] + 3 * position
            for comp in range(3):
                A[comp, i, 8 + col : 9 + col] = slot_ref[base + comp]

    def fill_side(col, start):
        for r in range(-4, 20):
            base = ghost_ref[0, start + jnp.clip(lat * 16 + r, 0, all_rows - 1)] + 3 * (r + 4)
            for comp in range(3):
                A[comp, r + PAD, 8 + col : 9 + col] = slot_ref[base + comp]

    prepare(
        f_ref, mu_ref, left_ref, right_ref, above_ref, below_ref,
        F, C, DG, over_ref, visc_ref, MU,
    )
    pl.when(lat == 0)(lambda: fill_row(5, 0))
    pl.when(lat == last_lat)(lambda: fill_row(22, all_cols))
    pl.when(lon == 0)(lambda: fill_side(-1, 2 * all_cols))
    pl.when(lon == last_lon)(lambda: fill_side(8, 2 * all_cols + all_rows))

    inside = ((row >= 8) | (lon > 0)) & ((row < 16) | (lon < last_lon))
    parity = jnp.where(inside, (row + lane) & 1, 2)

    def weighted(source, comp, i, here):
        total = F[comp, i] + C[0, i] * source[comp, i - 1]
        total = total + C[1, i] * source[comp, i + 1]
        total = total + C[2, i] * roll(here, 1, 0)
        total = total + C[3, i] * roll(here, -1, 0)
        total = total + C[4, i] * roll(here, 1, 1)
        return total + C[5, i] * roll(here, -1, 1)

    wanted = {}
    for colour in range(2):
        wanted[colour, "mid"] = jnp.int32(colour)
        wanted[colour, "top"] = jnp.where(lat == 0, 3, colour)
        wanted[colour, "low"] = jnp.where(lat == last_lat, 3, colour)

    def relax(colour, reach, source, target):
        for r in range(-reach, 16 + reach):
            i = r + PAD
            zone = "top" if r < 0 else "low" if r > 15 else "mid"
            mask = parity == wanted[(colour + r) % 2, zone]
            for comp in range(3):
                here = source[comp, i]
                target[comp, i] = jnp.where(mask, weighted(source, comp, i, here), here)

    relax(0, 4, A, B)
    relax(1, 3, B, A)
    relax(0, 2, A, B)
    relax(1, 1, B, A)

    tile = (8, 128)
    lane8, row8 = lanes_of(tile), rows_of(tile)
    odd_lane8, odd_row8 = (lane8 & 1) == 1, (row8 & 1) == 1

    def packed(parts):
        low = jnp.where(odd_lane8, parts[1], parts[0])
        high = jnp.where(odd_lane8, parts[3], parts[2])
        return jnp.where(odd_row8, high, low)

    for k in range(8):
        parts = []
        for comp in range(3):
            rhs = jnp.zeros(tile, jnp.float32)
            for r in (2 * k, 2 * k + 1):
                here = A[comp, r + PAD]
                smooth_ref[comp, r] = here[8:16]
                left = DG[r] * (weighted(A, comp, r + PAD, here) - here)[8:16]
                res_ref[comp, r] = left
                rhs = rhs + left
            rhs = rhs + lane_partner(rhs, odd_lane8)
            rhs = rhs + row_partner(rhs, odd_row8)
            parts.append(0.125 * rhs * over_ref[k])
        message_ref[k] = packed(parts + [visc_ref[k]])
        if k % 4 == 3:
            message_ref[8 + k // 4] = packed([over_ref[j] for j in range(k - 3, k + 1)])


def coarse_kernel(
    mid_ref, above_ref, below_ref, smooth_ref, left_ref, out_ref, res_ref,
    done, Q, CV, DV, E, AN, AS, AW, AE, AD, AU,
):
    leave = pltpu.make_async_copy(left_ref, res_ref, done)
    leave.start()
    wide = (40, 128)
    lane, row = lanes_of(wide), rows_of(wide)
    odd_lane, odd_row = (lane & 1) == 1, (row & 1) == 1

    def spread(value, part, odd_l, odd_r):
        keep = odd_l if part % 2 else ~odd_l
        value = jnp.where(keep, value, roll(value, -1 if part % 2 else 1, 1))
        keep = odd_r if part // 2 else ~odd_r
        return jnp.where(keep, value, roll(value, -1 if part // 2 else 1, 0))

    def far(n):
        return max(0, 7 - n, n - 14)

    for n in range(22):
        away = far(n)
        if away == 0:
            t = n - 7
            Q[n] = mid_ref[t]
            cols, over = slice(0, 40), mid_ref[8 + t // 4]
        else:
            ref, t = (above_ref, n + 1) if n < 7 else (below_ref, n - 15)
            tiles = range(5) if away < 3 else range(1, 4)
            first = 5 * (away - 1) if away < 3 else 10 + 3 * (away - 3) - 1
            for j in tiles:
                Q[n, 8 * j : 8 * j + 8] = ref[first + j]
            cols = slice(8 * tiles[0], 8 * tiles[-1] + 8)
            over = [ref[25 + 5 * (t // 4) + j] for j in tiles]
            over = jnp.concatenate(over, axis=0)
        CV[n, cols] = spread(Q[n, cols], 3, odd_lane[cols], odd_row[cols])
        DV[n, cols] = 0.125 * spread(over, t % 4, odd_lane[cols], odd_row[cols])

    def span(reach):
        return slice(0, 40) if reach > 3 else slice(8, 32)

    for n in range(1, 21):
        cols = span(6 - far(n))
        edge = lane[cols]
        visc, over = CV[n, cols], DV[n, cols]
        AN[n, cols] = over * (visc + CV[n - 1, cols])
        AS[n, cols] = over * (visc + CV[n + 1, cols])
        AW[n, cols] = over * (visc + roll(visc, 2, 0))
        AE[n, cols] = over * (visc + roll(visc, -2, 0))
        AD[n, cols] = jnp.where(edge < 2, 0.0, over * (visc + roll(visc, 2, 1)))
        AU[n, cols] = jnp.where(edge >= 126, 0.0, over * (visc + roll(visc, -2, 1)))

    for turn in range(1, COARSE):
        old = Q if turn == 1 else E.at[turn % 2]
        new = E.at[(turn + 1) % 2]
        for n in range(turn, 22 - turn):
            cols = span(7 - turn - far(n))
            here = old[n, cols]
            total = Q[n, cols] + (1.0 - RELAX) * here
            total = total + AN[n, cols] * old[n - 1, cols]
            total = total + AS[n, cols] * old[n + 1, cols]
            total = total + AW[n, cols] * roll(here, 2, 0)
            total = total + AE[n, cols] * roll(here, -2, 0)
            total = total + AD[n, cols] * roll(here, 2, 1)
            new[n, cols] = total + AU[n, cols] * roll(here, -2, 1)

    final = E.at[COARSE % 2]
    tile = (8, 128)
    lane8, row8 = lanes_of(tile), rows_of(tile)
    odd_lane8, odd_row8 = (lane8 & 1) == 1, (row8 & 1) == 1
    for k in range(8):
        value = final[7 + k, 16:24]
        for comp in range(3):
            error = spread(value, comp, odd_lane8, odd_row8)
            for r in (2 * k, 2 * k + 1):
                out_ref[comp, r] = smooth_ref[comp, r] + error
    leave.wait()


def place():
    last_lat, last_lon = lax.axis_size("lat") - 1, lax.axis_size("lon") - 1
    return lax.axis_index("lat"), lax.axis_index("lon"), last_lat, last_lon


def wanted_cells():
    _, lon, last_lat, last_lon = place()
    dest = lax.broadcasted_iota(jnp.int32, (8, CELLS), 0)
    position = lax.broadcasted_iota(jnp.int32, (8, CELLS), 1)
    rows, cols = (last_lat + 1) * 16, (last_lon + 1) * 8
    first = jnp.where(lon == 0, 1, 0)
    edge = jnp.where((lon == 0) | (lon == last_lon), 1, 0)
    side_row = dest * 16 + position - 4
    on_side = (edge > 0) & (position < 24) & (side_row >= 0) & (side_row < rows)
    side = 2 * cols + (1 - first) * rows + jnp.clip(side_row, 0, rows - 1)
    along = jnp.where((dest == 0) & (position < 4), position, position - 20)
    corner_col = along + (1 - first) * (lon * 8 - 4)
    col = edge * corner_col + (1 - edge) * (lon * 8 + position - 4)
    row_cell = jnp.where(dest == 0, 0, cols) + jnp.clip(col, 0, cols - 1)
    return jnp.where(on_side, side, row_cell)


def per_device(velocity, forcing, viscosity, ghost_slots, corner_rows, corner_cols, corner_weights):
    v, f, mu = velocity[0], forcing[0], viscosity[0]
    lats, lons = lax.axis_size("lat"), lax.axis_size("lon")
    params = pltpu.CompilerParams(vmem_limit_bytes=32 * 2**20)
    f32 = jnp.float32

    def kernel(body, shapes, specs):
        return pl.pallas_call(
            body,
            out_shape=[jax.ShapeDtypeStruct(shape, f32) for shape in shapes],
            in_specs=specs,
            out_specs=[VMEM] * len(shapes),
            compiler_params=params,
        )

    weights = jnp.transpose(corner_weights, (0, 3, 1, 2))[0]
    shapes = ((3, 16, 128), (3, 8, 128), (3, 128), (88, 128))
    edge, first_row, first_cell, blended, source_rows, ghost_rows = pl.pallas_call(
        first_kernel,
        out_shape=[jax.ShapeDtypeStruct(shape, f32) for shape in shapes]
        + [jax.ShapeDtypeStruct(ghost_slots.shape, jnp.int32)] * 2,
        in_specs=[pl.BlockSpec(memory_space=pltpu.HBM)] * 5,
        out_specs=[VMEM] * 6,
        scratch_shapes=[
            pltpu.SMEM((1, 3), jnp.int32),
            pltpu.SMEM((1, 3), jnp.int32),
            pltpu.SMEM((3, 1, 4), f32),
            pltpu.VMEM(v.shape, f32),
            pltpu.VMEM(ghost_slots.shape, jnp.int32),
            pltpu.SemaphoreType.DMA((5,)),
        ],
        compiler_params=params,
        name="first",
    )(
        *(
            pltpu.with_memory_space_constraint(operand, pltpu.HBM)
            for operand in (corner_rows[0], corner_cols[0], weights, v, ghost_slots)
        )
    )
    first_cell = shifted(first_cell, -1, -1, 1)
    first_row = shifted(first_row, -1, 0, 1)
    edge = shifted(edge, 0, -1, 1)
    blended = shifted(blended, 0, 0, 1)
    (values,) = kernel(interp_kernel, ((9 * lons, 1, 128),), [VMEM] * 4)(
        blended, edge, first_row, first_cell
    )
    around = lax.all_to_all(values.reshape(lons, 1, 1152), "lon", 0, 0, tiled=True)
    to_above, to_below, cells = pl.pallas_call(
        cut_kernel,
        out_shape=[jax.ShapeDtypeStruct((32, 8, 128), f32)] * 2
        + [jax.ShapeDtypeStruct((lats, CELLS), jnp.int32)],
        in_specs=[VMEM] * 3,
        out_specs=[VMEM] * 3,
        compiler_params=params,
        name="cut",
    )(v, f, mu)
    below = shifted(to_above, -1, 0)
    above = shifted(to_below, 1, 0)

    chosen = pl.pallas_call(
        pick_kernel,
        out_shape=jax.ShapeDtypeStruct((lats, 3 * CELLS, 1, 128), f32),
        in_specs=[SMEM, SMEM, VMEM],
        out_specs=pl.BlockSpec(memory_space=pltpu.HBM),
        scratch_shapes=[
            pltpu.VMEM((lats, 3 * CELLS, 1, 128), f32),
            pltpu.SemaphoreType.DMA((lats,)),
        ],
        compiler_params=params,
        name="pick",
    )(cells, source_rows, around.reshape(lons * 9, 1, 128))
    everything = lax.all_to_all(chosen.reshape(lats, 3 * CELLS, 128), "lat", 0, 0, tiled=True)
    everything = everything.reshape(lats * 3 * CELLS, 1, 128)
    to_right, to_left = kernel(pack_kernel, ((85, 8, 128),) * 2, [VMEM] * 5)(
        v, f, mu, above, below
    )
    left = shifted(to_right, 0, 1)
    right = shifted(to_left, 0, -1)

    block = jax.ShapeDtypeStruct((3, 16, 8, 128), f32)
    field = (3, 28, 24, 128)
    residual, smoothed, message = pl.pallas_call(
        smooth_kernel,
        out_shape=(block, block, jax.ShapeDtypeStruct((10, 8, 128), f32)),
        in_specs=[SMEM] + [VMEM] * 8,
        out_specs=(VMEM, VMEM, VMEM),
        scratch_shapes=[pltpu.VMEM(field, f32)] * 3
        + [
            pltpu.VMEM(shape, f32)
            for shape in (
                (6, 28, 24, 128), (16, 8, 128), (8, 8, 128), (8, 8, 128), (28, 24, 128)
            )
        ],
        compiler_params=params,
        name="smooth",
    )(ghost_rows, v, f, mu, left, right, above, below, everything)

    tiles = [
        shifted(message, 0, 2),
        shifted(message, 0, 1),
        message,
        shifted(message, 0, -1),
        shifted(message, 0, -2),
    ]
    band = jnp.concatenate(tiles, axis=1)
    tile_list = (-1, 8, 128)
    inverse = band[8:10].reshape(tile_list)
    to_above = [band[0:2].reshape(tile_list), band[2:7, 8:32].reshape(tile_list), inverse]
    to_below = [band[7:8], band[6:7]] + [band[r : r + 1, 8:32] for r in (5, 4, 3, 2, 1)]
    to_below = [part.reshape(tile_list) for part in to_below] + [inverse]
    band_below = shifted(jnp.concatenate(to_above, axis=0), -1, 0)
    band_above = shifted(jnp.concatenate(to_below, axis=0), 1, 0)
    coarse = pltpu.VMEM((22, 40, 128), f32)
    new, residual = pl.pallas_call(
        coarse_kernel,
        out_shape=(block, block),
        in_specs=[VMEM] * 5,
        out_specs=(VMEM, pl.BlockSpec(memory_space=pl.ANY)),
        scratch_shapes=[pltpu.SemaphoreType.DMA(()), coarse, coarse, coarse]
        + [pltpu.VMEM((2, 22, 40, 128), f32)]
        + [coarse] * 6,
        compiler_params=params,
        name="coarse",
    )(band, band_above, band_below, smoothed, residual)
    return new[None], residual[None]


def solution(mesh):
    placed = (
        P("patch", None, "lat", "lon", None),
        P("patch", None, "lat", "lon", None),
        P("patch", "lat", "lon", None),
        P("patch", None),
        P("patch", "lat", "lon"),
        P("patch", "lat", "lon"),
        P("patch", "lat", None, "lon"),
    )
    return jax.shard_map(
        per_device,
        mesh=mesh,
        in_specs=placed,
        out_specs=(P("patch", None, "lat", "lon", None), P("patch", None, "lat", "lon", None)),
        check_vma=False,
    )
```

```python
import jax
import jax.numpy as jnp
from jax import lax
from jax.experimental import pallas as pl
from jax.experimental.pallas import tpu as pltpu
from jax.sharding import PartitionSpec as P


AXES = ("patch", "lat", "lon")
RELAX = 0.8
COARSE = 8
PAD = 6
CELLS = 32
OUTER = (-3, -4, 18, 19)
VMEM = pl.BlockSpec(memory_space=pltpu.VMEM)
SMEM = pl.BlockSpec(memory_space=pltpu.SMEM)


def shifted(value, by_lat, by_lon, flip=0):
    patches, lats, lons = (lax.axis_size(axis) for axis in AXES)
    pairs = []
    for p in range(patches):
        for a in range(lats):
            for b in range(lons):
                a2, b2 = a + by_lat, b + by_lon
                if 0 <= a2 < lats and 0 <= b2 < lons:
                    pairs.append(((p * lats + a) * lons + b, ((p ^ flip) * lats + a2) * lons + b2))
    return lax.ppermute(value, AXES, pairs)


def lanes_of(shape):
    return lax.broadcasted_iota(jnp.int32, shape, len(shape) - 1)


def rows_of(shape):
    return lax.broadcasted_iota(jnp.int32, shape, len(shape) - 2)


def roll(value, by, axis):
    return pltpu.roll(value, by % value.shape[axis], axis)


def lane_partner(value, odd_lane):
    return jnp.where(odd_lane, roll(value, 1, 1), roll(value, -1, 1))


def row_partner(value, odd_row):
    return jnp.where(odd_row, roll(value, 1, 0), roll(value, -1, 0))


def first_kernel(
    rows_hbm, cols_hbm, weights_hbm, v_hbm, slot_hbm,
    edge_ref, below_ref, corner_ref, blend_ref, source_ref, ghost_ref,
    rows_ref, cols_ref, weights_ref, v_ref, slot_ref, done,
):
    sub = rows_of((8, 128))
    pairs = (v_hbm, v_ref), (rows_hbm, rows_ref), (cols_hbm, cols_ref), (weights_hbm, weights_ref)
    pairs = pairs + ((slot_hbm, slot_ref),)
    copies = [pltpu.make_async_copy(*pair, done.at[n]) for n, pair in enumerate(pairs)]
    for copy in copies:
        copy.start()
    for copy in copies:
        copy.wait()
    slots = slot_ref[...]
    third = (slots * 21846) >> 16
    source_ref[...] = (third & 31) * 9 + (slots - 3 * third) * 3
    ghost_ref[...] = (third >> 5) * (3 * CELLS)
    blend(rows_ref, cols_ref, weights_ref, v_ref, blend_ref)
    for comp in range(3):
        corner_ref[comp : comp + 1] = v_ref[comp, 0, 0:1]
        below_ref[comp] = v_ref[comp, 0]
        for j in range(2):
            first = v_ref[comp, 8 * j]
            for r in range(1, 8):
                first = jnp.where(sub == r, roll(v_ref[comp, 8 * j + r], r, 0), first)
            edge_ref[comp, 8 * j : 8 * j + 8] = first


def lat_tile(field, away):
    if 3 <= field < 6:
        return 20 + 4 * (field - 3) + away - 1
    return 5 * min(field, 3) + away - 1


def cut_kernel(v_ref, f_ref, mu_ref, up_ref, down_ref, cells_ref):
    cells_ref[...] = wanted_cells()
    for field in range(7):
        for away in range(1, 5 if 3 <= field < 6 else 6):
            for ref, r in ((up_ref, away - 1), (down_ref, 16 - away)):
                if field == 6:
                    value = mu_ref[r]
                else:
                    value = v_ref[field, r] if field < 3 else f_ref[field - 3, r]
                ref[lat_tile(field, away)] = value


def blend(rows_ref, cols_ref, weights_ref, v_ref, out_ref):
    tall, flat = rows_of((16, 128)), rows_of((8, 128))
    for slot in range(3):
        row, col = rows_ref[0, slot], cols_ref[0, slot]
        w0, w1, w2, w3 = (weights_ref[slot, 0, k] for k in range(4))
        here, next_one = flat == col, flat == col + 1
        upper = jnp.where(here, w0, jnp.where(next_one, w2, 0.0))
        lower = jnp.where(here, w1, jnp.where(next_one, w3, 0.0))
        within = row < 15
        next_row = jnp.where(within, row + 1, row)
        inner = jnp.where(within, lower, 0.0)
        for comp in range(3):
            total = upper * v_ref[comp, row] + inner * v_ref[comp, next_row]
            at = 3 * slot + comp
            out_ref[at : at + 1] = jnp.sum(total, axis=0, keepdims=True)
        beside = jnp.where(tall == row, w2, jnp.where(tall == row + 1, w3, 0.0))
        out_ref[16 + 16 * slot : 32 + 16 * slot] = jnp.where(col == 7, beside, 0.0)
        out_ref[64 + 8 * slot : 72 + 8 * slot] = jnp.where(within, 0.0, lower)
        both = jnp.where((row == 15) & (col == 7), w3, 0.0)
        out_ref[9 + slot : 10 + slot] = jnp.full((1, 128), both, jnp.float32)
    out_ref[12:16] = jnp.zeros((4, 128), jnp.float32)


def interp_kernel(blend_ref, edge_ref, below_ref, corner_ref, out_ref):
    for slot in range(3):
        edge_w = blend_ref[16 + 16 * slot : 32 + 16 * slot]
        below_w = blend_ref[64 + 8 * slot : 72 + 8 * slot]
        corner_w = blend_ref[9 + slot : 10 + slot]
        for comp in range(3):
            at = 3 * slot + comp
            beside = edge_w * edge_ref[comp]
            total = beside[0:8] + beside[8:16] + below_w * below_ref[comp]
            total = jnp.sum(total, axis=0, keepdims=True) + blend_ref[at : at + 1]
            total = total + corner_w * corner_ref[comp : comp + 1]
            for dest in range(out_ref.shape[0] // 9):
                out_ref[9 * dest + at] = total


def pick_kernel(cells_ref, source_ref, row_ref, out_ref, held, done):
    _, lon, last_lat, last_lon = place()
    edge = (lon == 0) | (lon == last_lon)

    def fill(dest, count):
        for position in range(count):
            base = source_ref[0, cells_ref[dest, position]]
            for comp in range(3):
                held[dest, position * 3 + comp] = row_ref[base + comp]
        return leave(dest, count)

    def leave(dest, count):
        rows = pl.ds(0, 3 * count)
        return pltpu.make_async_copy(held.at[dest, rows], out_ref.at[dest, rows], done.at[dest])

    @pl.when(edge)
    def _():
        for dest in range(last_lat + 1):
            fill(dest, CELLS).start()
        for dest in range(last_lat + 1):
            leave(dest, CELLS).wait()

    @pl.when(~edge)
    def _():
        copies = [fill(dest, 16) for dest in (0, last_lat)]
        for copy in copies:
            copy.start()
        for copy in copies:
            copy.wait()


def side_tile(ref, field, r, col, sub):
    if r in OUTER:
        by = 2 * OUTER.index(r)
        return roll(ref[70 + field], by if col == 3 else -by, 0)
    value = ref[10 * field + (r + 2) // 2]
    if r % 2:
        value = roll(value, 4, 0)
    extra = {0: 0, 1: 1, 2: 2, 6: 3}.get(field)
    if extra is None or not 0 <= r < 16:
        return value
    fifth = roll(ref[77 + 2 * extra + r // 8], col - r % 8, 0)
    return jnp.where(sub == col, fifth, value)


def pack_kernel(v_ref, f_ref, mu_ref, above_ref, below_ref, right_ref, left_ref):
    sub = rows_of((8, 128))

    def row(field, r):
        if r < 0:
            return above_ref[lat_tile(field, -r)]
        if r > 15:
            return below_ref[lat_tile(field, r - 15)]
        if field == 6:
            return mu_ref[r]
        return v_ref[field, r] if field < 3 else f_ref[field - 3, r]

    for field in range(7):
        for t in range(10):
            even, odd = row(field, 2 * t - 2), roll(row(field, 2 * t - 1), 4, 0)
            right_ref[10 * field + t] = jnp.where(sub < 4, odd, even)
            left_ref[10 * field + t] = jnp.where(sub < 4, even, odd)
        high = low = row(field, OUTER[0])
        for k in range(1, 4):
            value = row(field, OUTER[k])
            high = jnp.where((sub >> 1) == 3 - k, roll(value, -2 * k, 0), high)
            low = jnp.where((sub >> 1) == k, roll(value, 2 * k, 0), low)
        right_ref[70 + field] = high
        left_ref[70 + field] = low
    for n, field in enumerate((0, 1, 2, 6)):
        for j in range(2):
            third = fourth = row(field, 8 * j)
            for r in range(8):
                value = row(field, 8 * j + r)
                third = jnp.where(sub == r, roll(value, r - 3, 0), third)
                fourth = jnp.where(sub == r, roll(value, r - 4, 0), fourth)
            right_ref[77 + 2 * n + j] = third
            left_ref[77 + 2 * n + j] = fourth


def prepare(
    f_ref, mu_ref, left_ref, right_ref, above_ref, below_ref,
    F, C, DG, over_ref, visc_ref, MU,
):
    lat, lon, last_lat, last_lon = place()
    wide = (24, 128)
    lane, row = lanes_of(wide), rows_of(wide)
    odd_lane, odd_row = (lane & 1) == 1, (row & 1) == 1
    own = slice(PAD, PAD + 16)
    sub = rows_of((8, 128))
    MU[own, 8:16] = mu_ref[...]
    for r in range(-4, 20):
        MU[r + PAD, 0:8] = side_tile(left_ref, 6, r, 3, sub)
        MU[r + PAD, 16:24] = side_tile(right_ref, 6, r, 4, sub)
    for away in range(1, 6):
        for i, ref in ((PAD - away, above_ref), (PAD + 15 + away, below_ref)):
            value = ref[lat_tile(6, away)]
            MU[i, 8:16] = value
            if away == 5:
                MU[i, 0:8] = MU[i, 16:24] = value

    @pl.when(lat == 0)
    def _():
        MU[4] = MU[6]
        MU[5] = MU[6]

    @pl.when(lat == last_lat)
    def _():
        MU[22] = MU[21]
        MU[23] = MU[21]

    @pl.when(lon == 0)
    def _():
        for i in range(1, 27):
            MU[i, 0:8] = jnp.broadcast_to(MU[i, 8:9], (8, 128))

    @pl.when(lon == last_lon)
    def _():
        for i in range(1, 27):
            MU[i, 16:24] = jnp.broadcast_to(MU[i, 15:16], (8, 128))

    for i in range(2, 26):
        mid = MU[i]
        north = 0.5 * (mid + MU[i - 1])
        south = 0.5 * (mid + MU[i + 1])
        west = 0.5 * (mid + roll(mid, 1, 0))
        east = 0.5 * (mid + roll(mid, -1, 0))
        down = 0.5 * (mid + jnp.where(lane == 0, mid, roll(mid, 1, 1)))
        up = 0.5 * (mid + jnp.where(lane == 127, mid, roll(mid, -1, 1)))
        total = north + south + west + east + down + up
        inverse = 1.0 / total
        C[0, i] = north * inverse
        C[1, i] = south * inverse
        C[2, i] = west * inverse
        C[3, i] = east * inverse
        C[4, i] = jnp.where(lane == 0, 0.0, down * inverse)
        C[5, i] = jnp.where(lane == 127, 0.0, up * inverse)
        r = i - PAD
        if 0 <= r < 16:
            DG[r] = total[8:16]
        for comp in range(3):
            if 0 <= r < 16:
                force = f_ref[comp, r]
            else:
                ref, away = (above_ref, -r) if r < 0 else (below_ref, r - 15)
                force = ref[lat_tile(3 + comp, away)]
            F[comp, i, 0:8] = side_tile(left_ref, 3 + comp, r, 3, sub) * inverse[0:8]
            F[comp, i, 8:16] = force * inverse[8:16]
            F[comp, i, 16:24] = side_tile(right_ref, 3 + comp, r, 4, sub) * inverse[16:24]

    def coarse_visc(i):
        both = MU[i] + MU[i + 1]
        flat = 0.25 * (both + row_partner(both, odd_row))
        return flat, 0.5 * (flat + lane_partner(flat, odd_lane))

    layers = [coarse_visc(PAD + 2 * k) for k in (-1, 0)]
    for k in range(8):
        layers.append(coarse_visc(PAD + 2 * k + 2))
        before, (flat, visc), after = layers[k][1], layers[k + 1], layers[k + 2][1]
        edge_down = jnp.where(lane == 0, flat, roll(flat, 1, 1))
        edge_up = jnp.where(lane == 127, flat, roll(flat, -1, 1))
        total = 6.0 * visc + before + after + roll(visc, 2, 0) + roll(visc, -2, 0)
        total = total + jnp.where(lane < 2, edge_down, roll(visc, 2, 1))
        total = total + jnp.where(lane >= 126, edge_up, roll(visc, -2, 1))
        over_ref[k] = RELAX / (0.125 * total[8:16])
        visc_ref[k] = visc[8:16]


def smooth_kernel(
    ghost_ref, v_ref, f_ref, mu_ref, left_ref, right_ref, above_ref, below_ref, slot_ref,
    res_ref, smooth_ref, message_ref, A, B, F, C, DG, over_ref, visc_ref, MU,
):
    lat, lon, last_lat, last_lon = place()
    wide = (24, 128)
    lane, row = lanes_of(wide), rows_of(wide)
    sub = rows_of((8, 128))
    own = slice(PAD, PAD + 16)

    for comp in range(3):
        A[comp, own, 8:16] = v_ref[comp]
        for r in range(-4, 20):
            A[comp, r + PAD, 0:8] = side_tile(left_ref, comp, r, 3, sub)
            A[comp, r + PAD, 16:24] = side_tile(right_ref, comp, r, 4, sub)
        for away in range(1, 6):
            for i, ref in ((PAD - away, above_ref), (PAD + 15 + away, below_ref)):
                value = ref[lat_tile(comp, away)]
                A[comp, i, 8:16] = value
                if away == 5:
                    A[comp, i, 0:8] = A[comp, i, 16:24] = value

    edge = (lon == 0) | (lon == last_lon)
    all_cols, all_rows = (last_lon + 1) * 8, (last_lat + 1) * 16

    def fill_row(i, start):
        for col in range(-4, 12):
            along = jnp.where(lon == 0, col, col + 4)
            packed_at = jnp.where((lat == 0) & (along < 4), along, along + 20)
            position = jnp.clip(jnp.where(edge, packed_at, col + 4), 0, CELLS - 1)
            cell = start + jnp.clip(lon * 8 + col, 0, all_cols - 1)
            base = ghost_ref[0, cell] + 3 * position
            for comp in range(3):
                A[comp, i, 8 + col : 9 + col] = slot_ref[base + comp]

    def fill_side(col, start):
        for r in range(-4, 20):
            base = ghost_ref[0, start + jnp.clip(lat * 16 + r, 0, all_rows - 1)] + 3 * (r + 4)
            for comp in range(3):
                A[comp, r + PAD, 8 + col : 9 + col] = slot_ref[base + comp]

    prepare(
        f_ref, mu_ref, left_ref, right_ref, above_ref, below_ref,
        F, C, DG, over_ref, visc_ref, MU,
    )
    pl.when(lat == 0)(lambda: fill_row(5, 0))
    pl.when(lat == last_lat)(lambda: fill_row(22, all_cols))
    pl.when(lon == 0)(lambda: fill_side(-1, 2 * all_cols))
    pl.when(lon == last_lon)(lambda: fill_side(8, 2 * all_cols + all_rows))

    inside = ((row >= 8) | (lon > 0)) & ((row < 16) | (lon < last_lon))
    parity = jnp.where(inside, (row + lane) & 1, 2)

    def weighted(source, comp, i, here):
        total = F[comp, i] + C[0, i] * source[comp, i - 1]
        total = total + C[1, i] * source[comp, i + 1]
        total = total + C[2, i] * roll(here, 1, 0)
        total = total + C[3, i] * roll(here, -1, 0)
        total = total + C[4, i] * roll(here, 1, 1)
        return total + C[5, i] * roll(here, -1, 1)

    wanted = {}
    for colour in range(2):
        wanted[colour, "mid"] = jnp.int32(colour)
        wanted[colour, "top"] = jnp.where(lat == 0, 3, colour)
        wanted[colour, "low"] = jnp.where(lat == last_lat, 3, colour)

    def relax(colour, reach, source, target):
        for r in range(-reach, 16 + reach):
            i = r + PAD
            zone = "top" if r < 0 else "low" if r > 15 else "mid"
            mask = parity == wanted[(colour + r) % 2, zone]
            for comp in range(3):
                here = source[comp, i]
                target[comp, i] = jnp.where(mask, weighted(source, comp, i, here), here)

    relax(0, 4, A, B)
    relax(1, 3, B, A)
    relax(0, 2, A, B)
    relax(1, 1, B, A)

    tile = (8, 128)
    lane8, row8 = lanes_of(tile), rows_of(tile)
    odd_lane8, odd_row8 = (lane8 & 1) == 1, (row8 & 1) == 1

    def packed(parts):
        low = jnp.where(odd_lane8, parts[1], parts[0])
        high = jnp.where(odd_lane8, parts[3], parts[2])
        return jnp.where(odd_row8, high, low)

    for k in range(8):
        parts = []
        for comp in range(3):
            rhs = jnp.zeros(tile, jnp.float32)
            for r in (2 * k, 2 * k + 1):
                here = A[comp, r + PAD]
                smooth_ref[comp, r] = here[8:16]
                left = DG[r] * (weighted(A, comp, r + PAD, here) - here)[8:16]
                res_ref[comp, r] = left
                rhs = rhs + left
            rhs = rhs + lane_partner(rhs, odd_lane8)
            rhs = rhs + row_partner(rhs, odd_row8)
            parts.append(0.125 * rhs * over_ref[k])
        message_ref[k] = packed(parts + [visc_ref[k]])
        if k % 4 == 3:
            message_ref[8 + k // 4] = packed([over_ref[j] for j in range(k - 3, k + 1)])


def coarse_kernel(
    mid_ref, above_ref, below_ref, smooth_ref, left_ref, out_ref, res_ref,
    done, Q, CV, DV, E, AN, AS, AW, AE, AD, AU,
):
    leave = pltpu.make_async_copy(left_ref, res_ref, done)
    leave.start()
    wide = (40, 128)
    lane, row = lanes_of(wide), rows_of(wide)
    odd_lane, odd_row = (lane & 1) == 1, (row & 1) == 1

    def spread(value, part, odd_l, odd_r):
        keep = odd_l if part % 2 else ~odd_l
        value = jnp.where(keep, value, roll(value, -1 if part % 2 else 1, 1))
        keep = odd_r if part // 2 else ~odd_r
        return jnp.where(keep, value, roll(value, -1 if part // 2 else 1, 0))

    def far(n):
        return max(0, 7 - n, n - 14)

    for n in range(22):
        away = far(n)
        if away == 0:
            t = n - 7
            Q[n] = mid_ref[t]
            cols, over = slice(0, 40), mid_ref[8 + t // 4]
        else:
            ref, t = (above_ref, n + 1) if n < 7 else (below_ref, n - 15)
            tiles = range(5) if away < 3 else range(1, 4)
            first = 5 * (away - 1) if away < 3 else 10 + 3 * (away - 3) - 1
            for j in tiles:
                Q[n, 8 * j : 8 * j + 8] = ref[first + j]
            cols = slice(8 * tiles[0], 8 * tiles[-1] + 8)
            over = [ref[25 + 5 * (t // 4) + j] for j in tiles]
            over = jnp.concatenate(over, axis=0)
        CV[n, cols] = spread(Q[n, cols], 3, odd_lane[cols], odd_row[cols])
        DV[n, cols] = 0.125 * spread(over, t % 4, odd_lane[cols], odd_row[cols])

    def span(reach):
        return slice(0, 40) if reach > 3 else slice(8, 32)

    for n in range(1, 21):
        cols = span(6 - far(n))
        edge = lane[cols]
        visc, over = CV[n, cols], DV[n, cols]
        AN[n, cols] = over * (visc + CV[n - 1, cols])
        AS[n, cols] = over * (visc + CV[n + 1, cols])
        AW[n, cols] = over * (visc + roll(visc, 2, 0))
        AE[n, cols] = over * (visc + roll(visc, -2, 0))
        AD[n, cols] = jnp.where(edge < 2, 0.0, over * (visc + roll(visc, 2, 1)))
        AU[n, cols] = jnp.where(edge >= 126, 0.0, over * (visc + roll(visc, -2, 1)))

    for turn in range(1, COARSE):
        old = Q if turn == 1 else E.at[turn % 2]
        new = E.at[(turn + 1) % 2]
        for n in range(turn, 22 - turn):
            cols = span(7 - turn - far(n))
            here = old[n, cols]
            total = Q[n, cols] + (1.0 - RELAX) * here
            total = total + AN[n, cols] * old[n - 1, cols]
            total = total + AS[n, cols] * old[n + 1, cols]
            total = total + AW[n, cols] * roll(here, 2, 0)
            total = total + AE[n, cols] * roll(here, -2, 0)
            total = total + AD[n, cols] * roll(here, 2, 1)
            new[n, cols] = total + AU[n, cols] * roll(here, -2, 1)

    final = E.at[COARSE % 2]
    tile = (8, 128)
    lane8, row8 = lanes_of(tile), rows_of(tile)
    odd_lane8, odd_row8 = (lane8 & 1) == 1, (row8 & 1) == 1
    for k in range(8):
        value = final[7 + k, 16:24]
        for comp in range(3):
            error = spread(value, comp, odd_lane8, odd_row8)
            for r in (2 * k, 2 * k + 1):
                out_ref[comp, r] = smooth_ref[comp, r] + error
    leave.wait()


def place():
    last_lat, last_lon = lax.axis_size("lat") - 1, lax.axis_size("lon") - 1
    return lax.axis_index("lat"), lax.axis_index("lon"), last_lat, last_lon


def wanted_cells():
    _, lon, last_lat, last_lon = place()
    dest = lax.broadcasted_iota(jnp.int32, (8, CELLS), 0)
    position = lax.broadcasted_iota(jnp.int32, (8, CELLS), 1)
    rows, cols = (last_lat + 1) * 16, (last_lon + 1) * 8
    first = jnp.where(lon == 0, 1, 0)
    edge = jnp.where((lon == 0) | (lon == last_lon), 1, 0)
    side_row = dest * 16 + position - 4
    on_side = (edge > 0) & (position < 24) & (side_row >= 0) & (side_row < rows)
    side = 2 * cols + (1 - first) * rows + jnp.clip(side_row, 0, rows - 1)
    along = jnp.where((dest == 0) & (position < 4), position, position - 20)
    corner_col = along + (1 - first) * (lon * 8 - 4)
    col = edge * corner_col + (1 - edge) * (lon * 8 + position - 4)
    row_cell = jnp.where(dest == 0, 0, cols) + jnp.clip(col, 0, cols - 1)
    return jnp.where(on_side, side, row_cell)


def per_device(velocity, forcing, viscosity, ghost_slots, corner_rows, corner_cols, corner_weights):
    v, f, mu = velocity[0], forcing[0], viscosity[0]
    lats, lons = lax.axis_size("lat"), lax.axis_size("lon")
    params = pltpu.CompilerParams(vmem_limit_bytes=32 * 2**20)
    f32 = jnp.float32

    def kernel(body, shapes, specs):
        return pl.pallas_call(
            body,
            out_shape=[jax.ShapeDtypeStruct(shape, f32) for shape in shapes],
            in_specs=specs,
            out_specs=[VMEM] * len(shapes),
            compiler_params=params,
        )

    weights = jnp.transpose(corner_weights, (0, 3, 1, 2))[0]
    shapes = ((3, 16, 128), (3, 8, 128), (3, 128), (88, 128))
    edge, first_row, first_cell, blended, source_rows, ghost_rows = pl.pallas_call(
        first_kernel,
        out_shape=[jax.ShapeDtypeStruct(shape, f32) for shape in shapes]
        + [jax.ShapeDtypeStruct(ghost_slots.shape, jnp.int32)] * 2,
        in_specs=[pl.BlockSpec(memory_space=pltpu.HBM)] * 5,
        out_specs=[VMEM] * 6,
        scratch_shapes=[
            pltpu.SMEM((1, 3), jnp.int32),
            pltpu.SMEM((1, 3), jnp.int32),
            pltpu.SMEM((3, 1, 4), f32),
            pltpu.VMEM(v.shape, f32),
            pltpu.VMEM(ghost_slots.shape, jnp.int32),
            pltpu.SemaphoreType.DMA((5,)),
        ],
        compiler_params=params,
        name="first",
    )(
        *(
            pltpu.with_memory_space_constraint(operand, pltpu.HBM)
            for operand in (corner_rows[0], corner_cols[0], weights, v, ghost_slots)
        )
    )
    first_cell = shifted(first_cell, -1, -1, 1)
    first_row = shifted(first_row, -1, 0, 1)
    edge = shifted(edge, 0, -1, 1)
    blended = shifted(blended, 0, 0, 1)
    (values,) = kernel(interp_kernel, ((9 * lons, 1, 128),), [VMEM] * 4)(
        blended, edge, first_row, first_cell
    )
    around = lax.all_to_all(values.reshape(lons, 1, 1152), "lon", 0, 0, tiled=True)
    to_above, to_below, cells = pl.pallas_call(
        cut_kernel,
        out_shape=[jax.ShapeDtypeStruct((32, 8, 128), f32)] * 2
        + [jax.ShapeDtypeStruct((lats, CELLS), jnp.int32)],
        in_specs=[VMEM] * 3,
        out_specs=[VMEM] * 3,
        compiler_params=params,
        name="cut",
    )(v, f, mu)
    below = shifted(to_above, -1, 0)
    above = shifted(to_below, 1, 0)

    chosen = pl.pallas_call(
        pick_kernel,
        out_shape=jax.ShapeDtypeStruct((lats, 3 * CELLS, 1, 128), f32),
        in_specs=[SMEM, SMEM, VMEM],
        out_specs=pl.BlockSpec(memory_space=pltpu.HBM),
        scratch_shapes=[
            pltpu.VMEM((lats, 3 * CELLS, 1, 128), f32),
            pltpu.SemaphoreType.DMA((lats,)),
        ],
        compiler_params=params,
        name="pick",
    )(cells, source_rows, around.reshape(lons * 9, 1, 128))
    everything = lax.all_to_all(chosen.reshape(lats, 3 * CELLS, 128), "lat", 0, 0, tiled=True)
    everything = everything.reshape(lats * 3 * CELLS, 1, 128)
    to_right, to_left = kernel(pack_kernel, ((85, 8, 128),) * 2, [VMEM] * 5)(v, f, mu, above, below)
    left = shifted(to_right, 0, 1)
    right = shifted(to_left, 0, -1)

    block = jax.ShapeDtypeStruct((3, 16, 8, 128), f32)
    field = (3, 28, 24, 128)
    residual, smoothed, message = pl.pallas_call(
        smooth_kernel,
        out_shape=(block, block, jax.ShapeDtypeStruct((10, 8, 128), f32)),
        in_specs=[SMEM] + [VMEM] * 8,
        out_specs=(VMEM, VMEM, VMEM),
        scratch_shapes=[pltpu.VMEM(field, f32)] * 3
        + [
            pltpu.VMEM(shape, f32)
            for shape in ((6, 28, 24, 128), (16, 8, 128), (8, 8, 128), (8, 8, 128), (28, 24, 128))
        ],
        compiler_params=params,
        name="smooth",
    )(ghost_rows, v, f, mu, left, right, above, below, everything)

    near = shifted(message, 0, 1), shifted(message, 0, -1)
    distant = shifted(message, 0, 2), shifted(message, 0, -2)
    tiles = [distant[0], near[0], message, near[1], distant[1]]
    band = jnp.concatenate(tiles, axis=1)
    tile_list = (-1, 8, 128)
    inverse = band[8:10].reshape(tile_list)
    to_above = [band[0:2].reshape(tile_list), band[2:7, 8:32].reshape(tile_list), inverse]
    to_below = [band[7:8], band[6:7]] + [band[r : r + 1, 8:32] for r in (5, 4, 3, 2, 1)]
    to_below = [part.reshape(tile_list) for part in to_below] + [inverse]
    band_below = shifted(jnp.concatenate(to_above, axis=0), -1, 0)
    band_above = shifted(jnp.concatenate(to_below, axis=0), 1, 0)
    coarse = pltpu.VMEM((22, 40, 128), f32)
    new, residual = pl.pallas_call(
        coarse_kernel,
        out_shape=(block, block),
        in_specs=[VMEM] * 5,
        out_specs=(VMEM, pl.BlockSpec(memory_space=pl.ANY)),
        scratch_shapes=[pltpu.SemaphoreType.DMA(()), coarse, coarse, coarse]
        + [pltpu.VMEM((2, 22, 40, 128), f32)]
        + [coarse] * 6,
        compiler_params=params,
        name="coarse",
    )(band, band_above, band_below, smoothed, residual)
    return new[None], residual[None]


def solution(mesh):
    placed = (
        P("patch", None, "lat", "lon", None),
        P("patch", None, "lat", "lon", None),
        P("patch", "lat", "lon", None),
        P("patch", None),
        P("patch", "lat", "lon"),
        P("patch", "lat", "lon"),
        P("patch", "lat", None, "lon"),
    )
    return jax.shard_map(
        per_device,
        mesh=mesh,
        in_specs=placed,
        out_specs=(P("patch", None, "lat", "lon", None), P("patch", None, "lat", "lon", None)),
        check_vma=False,
    )
```
